32 devices in a mesh: fsdp: 2 (over core), ctx: 4 (over y, x), tp: 4 (over z).
Axes of the slice: x: 2, y: 2, z: 4, core: 2. Of those that a mesh axis runs over, the one named last changes fastest.
Arguments:
- hidden: bfloat16 [4096, 768], P(('fsdp', 'ctx')), may hold values from -6 to 6
- seq_lengths: int32 [2, 4], P('fsdp'), may hold values from 1 to 2045, as said below
- norm_gain: float32 [768], replicated, may hold values from 0.1 to 1.9
- weight_x: bfloat16 [768, 1536], P(('fsdp', 'ctx'), 'tp'), may hold values from -0.21875 to 0.21875
- weight_z: bfloat16 [768, 1536], P(('fsdp', 'ctx'), 'tp'), may hold values from -0.21875 to 0.21875
- weight_bc: bfloat16 [768, 128], P(('fsdp', 'ctx')), may hold values from -0.0546875 to 0.0546875
- weight_dt: bfloat16 [768, 2, 24], P(('fsdp', 'ctx'), None, 'tp'), may hold values from -0.21875 to 0.21875
- conv_x: float32 [4, 1536], P(None, 'tp'), may hold values from -3 to 3
- conv_bc: float32 [4, 128], replicated, may hold values from -3 to 3
- dt_bias: float32 [2, 24], P(None, 'tp'), may hold values from -3 to -1
- log_rate: float32 [2, 24], P(None, 'tp'), may hold values from -5 to -1.5
- skip_scale: float32 [24], P('tp'), may hold values from 0.5 to 1.5
- gate_gain: float32 [1536], P('tp'), may hold values from 0.1 to 1.9
- weight_out: bfloat16 [1536, 768], P('tp', ('fsdp', 'ctx')), may hold values from -0.3125 to 0.3125
- cotangent: bfloat16 [4096, 768], P(('fsdp', 'ctx')), may hold values from -6 to 6
Outputs:
- out: bfloat16 [4096, 768], P(('fsdp', 'ctx'))
- grad_hidden: float32 [4096, 768], P(('fsdp', 'ctx'))
- grad_norm_gain: float32 [768], replicated
- grad_weight_x: float32 [768, 1536], P(('fsdp', 'ctx'), 'tp')
- grad_weight_z: float32 [768, 1536], P(('fsdp', 'ctx'), 'tp')
- grad_weight_bc: float32 [768, 128], P(('fsdp', 'ctx'))
- grad_weight_dt: float32 [768, 2, 24], P(('fsdp', 'ctx'), None, 'tp')
- grad_conv_x: float32 [4, 1536], P(None, 'tp')
- grad_conv_bc: float32 [4, 128], replicated
- grad_dt_bias: float32 [2, 24], P(None, 'tp')
- grad_log_rate: float32 [2, 24], P(None, 'tp')
- grad_skip_scale: float32 [24], P('tp')
- grad_gate_gain: float32 [1536], P('tp')
- grad_weight_out: float32 [1536, 768], P('tp', ('fsdp', 'ctx'))
The draws below stay inside these ranges and needn't reach their ends.
Inputs may be any that keep to these rules, and one draw needn't show every extreme that they name: `seq_lengths`: each row holds the lengths of the 4 sequences that fill one group's 2048 tokens; in every row one sequence, at a place drawn from the seed, is longer than 1536.
All inputs are finite; a program needn't handle non-finite values.
Results may differ from the reference program's by a relative error of at most 0.018.
Values may be sent and summed in bfloat16 or wider, within the bound.
A program may use at most 64 MiB of HBM per device.

```python
from functools import partial
import jax
import jax.numpy as jnp
from jax import lax

D = 768
HEADS = 24
STATE = 64
CONV = 4
SPAN = 128
SEQS = 4
TOK_DEV = 512
INNER = 1536
CTX_TOK = 2048
TOKENS = 4096
N_FSDP = 2


def draw_seq_lengths(key, part):
    key_long, key_place, key_weights = jax.random.split(key, 3)
    groups = N_FSDP
    longest_top = CTX_TOK - SEQS + 1
    longest = jax.random.randint(key_long, (groups,), CTX_TOK - TOK_DEV + 1, longest_top + 1)
    longest = longest.at[0].set(longest_top)
    long_place = jax.random.randint(key_place, (groups,), 0, SEQS)
    shares = jax.random.randint(key_weights, (groups, SEQS), 1, 100)
    slot_index = jnp.arange(SEQS, dtype=jnp.int32)[None, :]
    is_long = slot_index == long_place[:, None]
    shares = jnp.where(is_long, 0, shares)
    spare_tokens = CTX_TOK - longest - (SEQS - 1)
    share_sum = jnp.sum(shares, axis=1, keepdims=True)
    extra_share = spare_tokens[:, None] * shares // share_sum
    short_lengths = jnp.where(is_long, 0, 1 + extra_share)
    leftover = CTX_TOK - longest - jnp.sum(short_lengths, axis=1)
    first_short = jnp.where(long_place == 0, 1, 0)
    short_lengths = short_lengths + jnp.where(slot_index == first_short[:, None], leftover[:, None], 0)
    return jnp.where(is_long, longest[:, None], short_lengths).astype(jnp.int32)


def level_of(own_key, extent, cuts, smallest, largest):
    loudness = 1.0
    for position, shards_of in cuts:
        draws = jax.random.uniform(jax.random.fold_in(jax.random.fold_in(own_key, 6), position), (shards_of,), jnp.float32, smallest / len(cuts), largest / len(cuts))
        loudness = loudness * jnp.repeat(jnp.exp(draws), extent[position] // shards_of).reshape((-1,) + (1,) * (len(extent) - 1 - position))
    return loudness


def noise(own_key, shape, scale, limit, cuts=(), kind=jnp.bfloat16):
    gain = level_of(own_key, shape, cuts, -0.22, 0.18) if cuts else 1.0
    values = jax.random.normal(own_key, shape, jnp.float32) * scale * gain
    return jnp.minimum(jnp.maximum(values, -limit), limit).astype(kind)


def setup_inputs(seed: int = 0) -> dict:
    seeds = jax.random.split(jax.random.key(seed), 16)
    hidden = noise(seeds[0], (TOKENS, D), 1.0, 6.0, ((0, 8),))
    seq_lengths = draw_seq_lengths(jax.random.fold_in(seeds[15], 71), 0)
    norm_gain = jnp.clip(1.0 + 0.18 * jax.random.normal(seeds[2], (D,), jnp.float32), 0.1, 1.9)
    weight_x = noise(seeds[3], (D, INNER), D ** -0.5, 0.21875, ((0, 8), (1, 4)))
    weight_z = noise(seeds[4], (D, INNER), D ** -0.5, 0.21875, ((0, 8), (1, 4)))
    weight_bc = noise(seeds[5], (D, 2 * STATE), (16 * D) ** -0.5, 0.0546875, ((0, 8),))
    weight_dt = noise(seeds[6], (D, 2, HEADS), D ** -0.5, 0.21875, ((0, 8), (2, 4)))
    conv_x = noise(seeds[7], (CONV, INNER), CONV ** -0.5, 3.0, ((1, 4),), jnp.float32)
    conv_bc = noise(seeds[8], (CONV, 2 * STATE), CONV ** -0.5, 3.0, (), jnp.float32)
    dt_bias = jnp.clip(-3.0 + 2.0 * jax.random.uniform(seeds[9], (2, HEADS), jnp.float32) ** level_of(seeds[9], (2, HEADS), ((1, 4),), -0.2, 0.2), -3.0, -1.0)
    log_rate = jnp.clip(-5.0 + 3.5 * jax.random.uniform(seeds[10], (2, HEADS), jnp.float32) ** level_of(seeds[10], (2, HEADS), ((1, 4),), -0.2, 0.2), -5.0, -1.5)
    skip_scale = jnp.clip(0.5 + 1.0 * jax.random.uniform(seeds[11], (HEADS,), jnp.float32) ** level_of(seeds[11], (HEADS,), ((0, 4),), -0.2, 0.2), 0.5, 1.5)
    gate_gain = jnp.clip(1.0 + 0.18 * jax.random.normal(seeds[12], (INNER,), jnp.float32), 0.1, 1.9)
    weight_out = noise(seeds[13], (INNER, D), (INNER // 4) ** -0.5, 0.3125, ((0, 4), (1, 8)))
    cotangent = noise(seeds[14], (TOKENS, D), 1.0, 6.0, ((0, 8),))
    return {"hidden": hidden, "seq_lengths": seq_lengths, "norm_gain": norm_gain, "weight_x": weight_x, "weight_z": weight_z, "weight_bc": weight_bc, "weight_dt": weight_dt, "conv_x": conv_x, "conv_bc": conv_bc, "dt_bias": dt_bias, "log_rate": log_rate, "skip_scale": skip_scale, "gate_gain": gate_gain, "weight_out": weight_out, "cotangent": cotangent}


epsilon = 1e-05
highest = lax.Precision.HIGHEST

@jax.custom_vjp
def low(v):
    return lax.optimization_barrier(v.astype(jnp.bfloat16)).astype(jnp.float32)

@jax.custom_vjp
def low_back(v):
    return v

def low_keep(v):
    return (low(v), None)

def low_pass(kept, grad):
    return (grad,)

def back_keep(v):
    return (v, None)

def back_low(kept, grad):
    return (low(grad),)
low.defvjp(low_keep, low_pass)
low_back.defvjp(back_keep, back_low)

def both_round(value):
    return low(low_back(value))

def matmul(left, right):
    return jnp.dot(left, right, precision=highest, preferred_element_type=jnp.float32)

def segment_ids(lengths_row, positions):
    seq_ends = jnp.cumsum(lengths_row).astype(jnp.int32)
    passed = lax.optimization_barrier(jnp.sum((positions[:, None] >= seq_ends[None, :]).astype(jnp.int32), axis=1)).astype(jnp.int32)
    return (passed - (positions < 0).astype(jnp.int32)).astype(jnp.int32)

def rms_norm(values, gain_row):
    return values * lax.rsqrt(lax.optimization_barrier(jnp.mean(values * values, axis=1, keepdims=True)) + epsilon) * gain_row[None, :]

def causal_conv(padded, kernel, seg_padded):
    kernel_len = kernel.shape[0]
    length = padded.shape[0] - kernel_len + 1
    seg_here = seg_padded[kernel_len - 1:]
    summed = jnp.zeros((length, padded.shape[1]), jnp.float32)
    for offset in range(kernel_len):
        matching = (seg_padded[offset:offset + length] == seg_here).astype(jnp.float32)
        summed = summed + padded[offset:offset + length] * kernel[offset][None, :] * matching[:, None]
    return jax.nn.silu(summed)

def span_pass(carry, pieces):
    state_in, seg_prior = carry
    x_block, b_block, c_block, dt_block, decay_block, seg_block = pieces
    length = x_block.shape[0]
    cum_decay = jnp.cumsum(decay_block, axis=0)
    places = jnp.arange(length)
    below_mask = (places[:, None] > places[None, :]) & (seg_block[:, None] == seg_block[None, :])
    below_heads = below_mask[:, :, None]
    spread = cum_decay[:, None, :] - cum_decay[None, :, :]
    mixing = jnp.where(below_heads, jnp.exp(jnp.where(below_heads, spread, 0.0)), 0.0)
    scores = jnp.dot(c_block, b_block.T, precision=highest, preferred_element_type=jnp.float32)
    weighted = x_block * dt_block[:, :, None]
    inner_part = jnp.einsum('ij,ijh,jhp->ihp', scores, mixing, weighted, precision=highest)
    reach_in = (seg_block == seg_prior).astype(jnp.float32)[:, None] * jnp.exp(cum_decay)
    carried = jnp.einsum('in,hpn,ih->ihp', c_block, state_in, reach_in, precision=highest)
    to_last = (seg_block == seg_block[length - 1]).astype(jnp.float32)[:, None] * jnp.exp(cum_decay[length - 1][None, :] - cum_decay)
    state_out = reach_in[length - 1][:, None, None] * state_in + jnp.einsum('jh,jhp,jn->hpn', to_last, weighted, b_block, precision=highest)
    return ((state_out, seg_block[length - 1].astype(jnp.int32)), inner_part + carried)

def direction_pass(state_in, seg_prior, x_heads, b_rows, c_rows, step_size, log_decay, seg_rows):

    def blocks(tensor):
        return tensor.reshape((tensor.shape[0] // SPAN, SPAN) + tensor.shape[1:])
    pieces = (blocks(x_heads), blocks(b_rows), blocks(c_rows), blocks(step_size), blocks(log_decay), blocks(seg_rows))
    (state_out, seg_last), outputs = lax.scan(jax.checkpoint(span_pass), (state_in, seg_prior.astype(jnp.int32)), pieces)
    return (state_out, outputs.reshape(x_heads.shape))

def two_way(x_round, bc_round, dt_raw, dt_bias, log_rate, skip_scale, seg_rows, seg_before, seg_after):
    rows_count = x_round.shape[0]
    head_count = skip_scale.shape[0]
    x_heads = x_round.reshape(rows_count, head_count, -1)
    step_size = jax.nn.softplus(dt_raw + dt_bias[None])
    log_decay = -jnp.exp(log_rate)[None] * step_size
    b_rows, c_rows = jnp.split(bc_round, 2, axis=1)
    zero_state = jnp.zeros((head_count, x_heads.shape[2], b_rows.shape[1]), jnp.float32)
    state_fwd, y_fwd = direction_pass(zero_state, seg_before, x_heads, b_rows, c_rows, step_size[:, 0], log_decay[:, 0], seg_rows)
    state_rev, y_rev = direction_pass(zero_state, seg_after, x_heads[::-1], b_rows[::-1], c_rows[::-1], step_size[::-1, 1], log_decay[::-1, 1], seg_rows[::-1])
    decay_fwd = (seg_rows[rows_count - 1] == seg_before).astype(jnp.float32) * jnp.exp(lax.optimization_barrier(jnp.sum(log_decay[:, 0], axis=0)))
    decay_rev = (seg_rows[0] == seg_after).astype(jnp.float32) * jnp.exp(lax.optimization_barrier(jnp.sum(log_decay[:, 1], axis=0)))
    mixed = y_fwd + y_rev[::-1] + skip_scale[None, :, None] * x_heads
    return (mixed.reshape(rows_count, -1), decay_fwd, state_fwd, decay_rev, state_rev)

def group_mix(inputs, conv_x, conv_bc, dt_bias, log_rate, skip_scale):
    x_proj, bc_proj, dt_raw, seg_rows = inputs
    pad_rows = conv_x.shape[0] - 1
    seg_padded = jnp.concatenate([jnp.full((pad_rows,), -1, jnp.int32), seg_rows.astype(jnp.int32)])
    x_padded = jnp.concatenate([jnp.zeros((pad_rows, x_proj.shape[1]), jnp.float32), x_proj], axis=0)
    bc_padded = jnp.concatenate([jnp.zeros((pad_rows, bc_proj.shape[1]), jnp.float32), bc_proj], axis=0)
    x_round = both_round(causal_conv(x_padded, conv_x, seg_padded))
    bc_round = both_round(causal_conv(bc_padded, conv_bc, seg_padded))
    outside = jnp.int32(-1)
    return two_way(x_round, bc_round, dt_raw, dt_bias, log_rate, skip_scale, seg_rows.astype(jnp.int32), outside, outside)[0]

def forward(hidden, norm_gain, weight_x, weight_z, weight_bc, weight_dt, conv_x, conv_bc, dt_bias, log_rate, skip_scale, gate_gain, weight_out, seg_all):
    rounded = low(rms_norm(hidden, norm_gain))
    x_proj = low_back(matmul(rounded, weight_x))
    z_proj = low_back(matmul(rounded, weight_z))
    bc_proj = low_back(matmul(rounded, weight_bc))
    dt_raw = low_back(jnp.einsum('td,dkh->tkh', rounded, weight_dt, precision=highest))
    groups = seg_all.shape[0]

    def regroup(tensor):
        return tensor.reshape((groups, -1) + tensor.shape[1:])
    mixer_fn = jax.checkpoint(partial(group_mix, conv_x=conv_x, conv_bc=conv_bc, dt_bias=dt_bias, log_rate=log_rate, skip_scale=skip_scale))
    mixed = lax.map(mixer_fn, (regroup(x_proj), regroup(bc_proj), regroup(dt_raw), seg_all))
    mixed = mixed.reshape(hidden.shape[0], -1)
    gated = mixed * jax.nn.silu(z_proj)
    normed_gate = gated * lax.rsqrt(lax.optimization_barrier(jnp.mean(gated * gated, axis=1, keepdims=True)) + epsilon) * gate_gain[None, :]
    return hidden + matmul(both_round(normed_gate), weight_out)

def reference(hidden, seq_lengths, norm_gain, weight_x, weight_z, weight_bc, weight_dt, conv_x, conv_bc, dt_bias, log_rate, skip_scale, gate_gain, weight_out, cotangent):
    positions = jnp.arange(CTX_TOK, dtype=jnp.int32)
    seg_all = jax.vmap(lambda lengths_row: segment_ids(lengths_row, positions))(seq_lengths).astype(jnp.int32)
    floats = tuple((tensor.astype(jnp.float32) for tensor in (hidden, norm_gain, weight_x, weight_z, weight_bc, weight_dt, conv_x, conv_bc, dt_bias, log_rate, skip_scale, gate_gain, weight_out)))

    def apply_layer(hidden_in, gain_in, wx_in, wz_in, wbc_in, wdt_in, convx_in, convbc_in, bias_in, rate_in, skip_in, gategain_in, wout_in):
        return forward(hidden_in, gain_in, wx_in, wz_in, wbc_in, wdt_in, convx_in, convbc_in, bias_in, rate_in, skip_in, gategain_in, wout_in, seg_all)
    result, pull_back = jax.vjp(apply_layer, *floats)
    gradients = pull_back(cotangent.astype(jnp.float32))
    return (result.astype(jnp.bfloat16), gradients[0], gradients[1], gradients[2], gradients[3], gradients[4], gradients[5], gradients[6], gradients[7], gradients[8], gradients[9], gradients[10], gradients[11], gradients[12])
```

```python
from functools import partial

import jax
import jax.numpy as jnp
from jax import lax
from jax.experimental import pallas as pl
from jax.experimental.pallas import tpu as pltpu
from jax.sharding import PartitionSpec as P

MESH = pl.DeviceIdType.MESH
F32 = jnp.float32
BF16 = jnp.bfloat16
EPS = 1e-05
TB = 128


def mm(left, right):
    return lax.dot_general(left, right, (((1,), (0,)), ((), ())), preferred_element_type=F32)


def mm_nt(left, right):
    return lax.dot_general(left, right, (((1,), (1,)), ((), ())), preferred_element_type=F32)


def mm_tn(left, right):
    return lax.dot_general(left, right, (((0,), (0,)), ((), ())), preferred_element_type=F32)


def split3(value):
    high = value.astype(BF16)
    rest = value - high.astype(F32)
    middle = rest.astype(BF16)
    low = (rest - middle.astype(F32)).astype(BF16)
    return high, middle, low


def exact_left(ones, value, dot=mm):
    a, b, c = split3(value)
    return dot(ones, a) + dot(ones, b) + dot(ones, c)


def exact_right(value, ones, dot=mm):
    a, b, c = split3(value)
    return dot(a, ones) + dot(b, ones) + dot(c, ones)


def iota(shape, dim):
    return lax.broadcasted_iota(jnp.int32, shape, dim)


def mixer_kernel(dims, *refs):
    (lens, hid, gain, wsh, kc, hrow, prow, cot, out, gh, gwx, gwz, gwbc, gwdt, gwo, small, hbuf, nl,
     wbuf, xp, dtr, u, low, z, ggate, ld, cc, cct, dte, rea, tol, w16, q16, gm, gmt, pexp, yfr, s16,
     sbuf, dec, decbuf, into16, gated, mixed, dmix, dy, st, stbuf, gall, glow, ob, obuf, oag, hb,
     hpbuf, hag, rdy, d16, dbuf, back16, dg, dw, dcc, ddt, du, gw16, fbuf, hsend, cbuf, bcs, bcbuf,
     sm, smbuf, ssem, rsem) = refs
    nf, nc, nt, hl = dims
    tok, width = hid.shape
    rows_w = wsh.shape[0]
    inner = prow.shape[1]
    pdim = inner // hl
    conv_w = inner + 128
    p1 = inner + 256
    nb = tok // TB
    taps = 4
    f, c, t = lax.axis_index("fsdp"), lax.axis_index("ctx"), lax.axis_index("tp")
    base = c * tok
    counter = [0]

    def remote(src, dst, dev):
        i = counter[0]
        counter[0] += 1
        copy = pltpu.make_async_remote_copy(
            src_ref=src, dst_ref=dst, send_sem=ssem.at[i], recv_sem=rsem.at[i],
            device_id=dev, device_id_type=MESH,
        )
        copy.start()
        return copy

    def fs(k):
        return (lax.rem(f + k, nf), c, t)

    def cx(k):
        return (f, lax.rem(c + k, nc), t)

    def tx(k):
        return (f, c, lax.rem(t + k, nt))

    pending = []

    barrier = pltpu.get_barrier_semaphore()
    peers = [fs(k) for k in range(1, nf)] + [cx(k) for k in range(1, nc)] + [tx(k) for k in range(1, nt)]
    for dev in peers:
        pl.semaphore_signal(barrier, inc=1, device_id=dev, device_id_type=MESH)
    pl.semaphore_wait(barrier, len(peers))

    me = f * nc + c
    col_parts = (pl.ds(0, p1), pl.ds(p1, 2 * inner))
    rim = remote(hid.at[pl.ds(tok - 16, 16)], hbuf, cx(1))
    ctx_copies = []
    fwd_copies = []
    for cols in col_parts:
        ctx_copies.append(
            [remote(wsh.at[:, cols], wbuf.at[me, :, cols], cx(k)) for k in range(1, nc)]
        )
        fwd_copies.append(
            [remote(wsh.at[:, cols], wbuf.at[me, :, cols], fs(k)) for k in range(1, nf)]
        )
    wbuf[me] = wsh[...]

    gain_row = gain[...]

    def norm_low(rows):
        h = rows.astype(F32)
        r = lax.rsqrt(jnp.mean(h * h, axis=1, keepdims=True) + EPS)
        return (h * r * gain_row).astype(BF16)

    @pl.loop(0, nb)
    def _(i):
        at = pl.multiple_of(i * TB, TB)
        nl[pl.ds(16 + at, TB), :] = norm_low(hid[pl.ds(at, TB), :])

    ends = []
    total = lens[0, 0]
    ends.append(total)
    for k in range(1, lens.shape[1]):
        total = total + lens[0, k]
        ends.append(total)

    def seg_of(pos):
        seg = jnp.where(pos < 0, -1, 0)
        for e in ends:
            seg = seg + jnp.where(pos >= e, 1, 0)
        return seg

    one_pos = jnp.full((1, 1), 0, jnp.int32)
    seg_before = seg_of(one_pos + (base - 1))
    seg_first = seg_of(one_pos + base)
    seg_last = seg_of(one_pos + (base + tok - 1))
    seg_after = seg_of(one_pos + (base + tok))
    seg_row = seg_of(iota((1, tok), 1) + base)
    place_row = iota((1, tok), 1)

    def seg_col(start, count, shift=0):
        return seg_of(iota((count, 1), 0) + (base + start + shift))

    def receive_weights(part):
        cols = col_parts[part]
        later = []
        for k in range(1, nc):
            ctx_copies[part][k - 1].wait_recv()
            src = f * nc + lax.rem(c + nc - k, nc)
            for j in range(1, nf):
                later.append(remote(wbuf.at[src, :, cols], wbuf.at[src, :, cols], fs(j)))
        for copy in fwd_copies[part] + later:
            copy.wait_recv()
        pending.extend(ctx_copies[part] + fwd_copies[part] + later)

    def weights(lo, hi):
        if rows_w % 16 == 0:
            return wbuf[:, :, lo:hi].reshape(width, hi - lo)
        return wbuf[:, :, lo:hi].astype(F32).reshape(width, hi - lo).astype(BF16)

    rim.wait_recv()
    pending.append(rim)
    nl[0:16, :] = norm_low(hbuf[...])
    receive_weights(0)

    w1 = weights(0, p1)
    head = mm(nl[0:16, :], w1)
    xp[0:16, :] = head[:, :conv_w]
    for i in range(tok // 256):
        got = mm(nl[16 + i * 256 : 16 + (i + 1) * 256, :], w1)
        xp[16 + i * 256 : 16 + (i + 1) * 256, :] = got[:, :conv_w]
        dtr[i * 256 : (i + 1) * 256, :] = got[:, conv_w:] + hrow[0:1, :]

    for i in range(nb):
        lo = i * TB
        here = seg_col(lo, TB)
        acc = xp[16 + lo : 16 + lo + TB, :] * kc[taps - 1 : taps, :]
        for d in range(1, taps):
            match = (seg_col(lo, TB, -d) == here).astype(F32)
            acc = acc + xp[16 + lo - d : 16 + lo - d + TB, :] * kc[taps - 1 - d : taps - d, :] * match
        u[lo : lo + TB, :] = acc
        low[lo : lo + TB, :] = (acc * jax.nn.sigmoid(acc)).astype(BF16)

    lane = iota((1, 128), 1)
    is_fwd = lane < hl
    rate_row = -jnp.exp(hrow[1:2, :])
    raw = dtr[...]
    step = jnp.maximum(raw, 0.0) + jnp.log1p(jnp.exp(-jnp.abs(raw)))
    decay = step * rate_row
    ld[...] = decay
    tri = (iota((tok, tok), 0) >= iota((tok, tok), 1)).astype(F32).astype(BF16)
    sums = exact_left(tri, decay)
    tot = sums[tok - 1 : tok, :]
    cum = jnp.where(is_fwd, sums, tot - sums + decay)
    cc[...] = cum
    cct[...] = cum.T
    dec_mask = jnp.where(
        is_fwd,
        (seg_last == seg_before).astype(F32),
        (seg_first == seg_after).astype(F32),
    )
    dec_row = jnp.exp(tot) * dec_mask
    dec[...] = jnp.broadcast_to(dec_row, (8, 128))
    dec_copies = [remote(dec, decbuf.at[k - 1], cx(k)) for k in range(1, nc)]

    spread = (
        iota((128, 2 * inner), 0) == lax.div(iota((128, 2 * inner), 1), pdim)
    ).astype(F32).astype(BF16)
    seg_all = seg_col(0, tok)
    reach = jnp.exp(cum) * jnp.where(
        is_fwd, (seg_all == seg_before).astype(F32), (seg_all == seg_after).astype(F32)
    )
    to_end = jnp.exp(tot - cum) * jnp.where(
        is_fwd, (seg_all == seg_last).astype(F32), (seg_all == seg_first).astype(F32)
    )
    rea[...] = exact_right(reach, spread)
    tol[...] = exact_right(to_end, spread)
    dte[...] = exact_right(step, spread)

    @pl.loop(0, nb)
    def _(i):
        rows = pl.ds(pl.multiple_of(i * TB, TB), TB)
        x = low[rows, :inner].astype(F32)
        w = (jnp.concatenate([x, x], axis=1) * dte[rows, :]).astype(BF16)
        w16[rows, :] = w
        q16[rows, :] = (w.astype(F32) * tol[rows, :]).astype(BF16)

    state_n = 64
    b16 = low[:, inner : inner + state_n]
    c16 = low[:, inner + state_n :]
    s16[...] = mm_tn(b16, q16[...]).astype(BF16)

    def half_of(forward):
        return pl.ds(pl.multiple_of(jnp.where(forward, 0, inner), 128), inner)

    state_copies = []
    for k in range(1, nc):
        forward = lax.rem(c + k, nc) > c
        state_copies.append(remote(s16.at[:, half_of(forward)], sbuf.at[k - 1], cx(k)))

    local = iota((TB, TB), 0)
    below = local > iota((TB, TB), 1)
    above = local < iota((TB, TB), 1)
    pair_left = iota((1, 128), 1) < pdim

    def mix_mask(i):
        same = seg_col(i * TB, TB) == seg_row
        return same & (iota((TB, 1), 0) + i * TB != place_row)

    for i in range(nb):
        lo, hi = i * TB, (i + 1) * TB
        mask = mix_mask(i)
        g = jnp.where(mask, mm_nt(c16[lo:hi], b16), 0.0)
        gm[lo:hi, :] = g
        gmt[lo:hi, :] = jnp.where(mask, mm_nt(b16[lo:hi], c16), 0.0)

    for i in range(nb):
        lo, hi = i * TB, (i + 1) * TB
        g_diag = gm[lo:hi, lo:hi]
        g_low = jnp.where(below, g_diag, 0.0)
        g_up = jnp.where(above, g_diag, 0.0)
        for pair in range(hl // 2):
            cols = slice(pair * 128, (pair + 1) * 128)
            cols_r = slice(inner + pair * 128, inner + (pair + 1) * 128)
            ys = []
            for h in (2 * pair, 2 * pair + 1):
                fc = cc[lo:hi, h : h + 1]
                rc = cc[lo:hi, hl + h : hl + h + 1]
                fr = cct[h : h + 1, :]
                rr = cct[hl + h : hl + h + 1, :]
                p = jnp.exp(jnp.minimum(fc - fr[:, lo:hi], rc - rr[:, lo:hi]))
                pexp[h, lo:hi, lo:hi] = p.astype(BF16)
                lows = [(g_low * p).astype(BF16)]
                ups = [(g_up * p).astype(BF16)]
                if i > 0:
                    p = jnp.exp(fc - fr[:, :lo])
                    pexp[h, lo:hi, :lo] = p.astype(BF16)
                    lows.insert(0, (gm[lo:hi, :lo] * p).astype(BF16))
                if i < nb - 1:
                    p = jnp.exp(rc - rr[:, hi:])
                    pexp[h, lo:hi, hi:] = p.astype(BF16)
                    ups.append((gm[lo:hi, hi:] * p).astype(BF16))
                lows = jnp.concatenate(lows, axis=1) if len(lows) > 1 else lows[0]
                ups = jnp.concatenate(ups, axis=1) if len(ups) > 1 else ups[0]
                ys.append((mm(lows, w16[:hi, cols]), mm(ups, w16[lo:, cols_r])))
            yfr[lo:hi, cols] = jnp.where(pair_left, ys[0][0], ys[1][0])
            yfr[lo:hi, cols_r] = jnp.where(pair_left, ys[0][1], ys[1][1])

    receive_weights(1)
    wz = weights(p1, p1 + inner)
    wo = weights(p1 + inner, p1 + 2 * inner)
    for i in range(tok // 256):
        rows = slice(i * 256, (i + 1) * 256)
        z[rows, :] = mm(nl[16 + i * 256 : 16 + (i + 1) * 256, :], wz)
        ggate[rows, :] = mm(cot[rows, :], wo).astype(BF16)

    dec_spread = []
    for k in range(1, nc):
        dec_copies[k - 1].wait_recv()
        dec_spread.append(exact_right(decbuf[k - 1], spread)[0:1, :])
    pending.extend(dec_copies)
    for copy in state_copies:
        copy.wait_recv()
    pending.extend(state_copies)
    acc_f = jnp.zeros((state_n, inner), F32)
    acc_r = jnp.zeros((state_n, inner), F32)
    for k in range(nc - 1, 0, -1):
        new = dec_spread[k - 1][:, :inner] * acc_f + sbuf[k - 1].astype(F32)
        acc_f = jnp.where(k <= c, new, acc_f)
    for k in range(1, nc):
        new = dec_spread[k - 1][:, inner:] * acc_r + sbuf[k - 1].astype(F32)
        acc_r = jnp.where(k > c, new, acc_r)
    into16[:, :inner] = acc_f.astype(BF16)
    into16[:, inner:] = acc_r.astype(BF16)

    skip_row = prow[0:1, :]
    gain_gate = prow[1:2, :]
    row_s = (iota((8, inner), 0) == 0).astype(F32).astype(BF16)
    row_t = (iota((8, inner), 0) == 1).astype(F32).astype(BF16)

    for i in range(nb):
        rows = slice(i * TB, (i + 1) * TB)
        carried = mm(low[rows, inner + state_n :], into16[...]) * rea[rows, :]
        y = yfr[rows, :] + carried
        yfr[rows, :] = y
        mix = y[:, :inner] + y[:, inner:] + skip_row * low[rows, :inner].astype(F32)
        mixed[rows, :] = mix
        zz = z[rows, :]
        gt = mix * zz * jax.nn.sigmoid(zz)
        gated[rows, :] = gt
        s = exact_left(row_s, gt * gt, mm_nt)
        s = s + exact_left(row_t, ggate[rows, :].astype(F32) * gain_gate * gt, mm_nt)
        st[:, rows] = s
    st_copies = [remote(st, stbuf.at[k - 1], tx(k)) for k in range(1, nt)]
    rows_sum = st[...]
    for k in range(1, nt):
        st_copies[k - 1].wait_recv()
        rows_sum = rows_sum + stbuf[k - 1]
    pending.extend(st_copies)
    total_inner = inner * nt
    r_row = lax.rsqrt(rows_sum[0:1, :] * (1.0 / total_inner) + EPS)
    q_row = r_row * r_row * r_row * rows_sum[1:2, :] * (-1.0 / total_inner)
    row8 = iota((8, tok), 0)
    rq = jnp.where(row8 == 0, r_row, jnp.where(row8 == 1, q_row, 0.0))
    pick = (iota((8, 256), 0) == lax.div(iota((8, 256), 1), 128)).astype(F32).astype(BF16)
    rq_cols = exact_right(rq, pick, mm_tn)

    acc_gain = jnp.zeros((1, inner), F32)
    acc_skip = jnp.zeros((1, inner), F32)
    for i in range(nb):
        rows = slice(i * TB, (i + 1) * TB)
        r = rq_cols[rows, 0:1]
        q = rq_cols[rows, 128:129]
        gt = gated[rows, :]
        gg = ggate[rows, :].astype(F32)
        ghat = gt * r
        glow[rows, :] = (ghat * gain_gate).astype(BF16)
        acc_gain = acc_gain + jnp.sum(gg * ghat, axis=0, keepdims=True)
        ggated = gg * gain_gate * r + gt * q
        zz = z[rows, :]
        sg = jax.nn.sigmoid(zz)
        dm = ggated * zz * sg
        mix = mixed[rows, :]
        gall[rows, p1:] = (ggated * mix * (sg * (1.0 + zz * (1.0 - sg)))).astype(BF16)
        dmix[rows, :] = dm
        acc_skip = acc_skip + jnp.sum(dm * low[rows, :inner].astype(F32), axis=0, keepdims=True)
        d = dm.astype(BF16)
        dy[rows, :] = d
        rdy[rows, :] = (jnp.concatenate([d, d], axis=1).astype(F32) * rea[rows, :]).astype(BF16)
    d16[...] = mm_tn(low[:, inner + state_n :], rdy[...]).astype(BF16)
    back_copies = []
    for k in range(1, nc):
        forward = lax.rem(c + k, nc) < c
        back_copies.append(remote(d16.at[:, half_of(forward)], dbuf.at[k - 1], cx(k)))

    for i in range(tok // 256):
        rows = slice(i * 256, (i + 1) * 256)
        ob[rows, :] = mm_nt(glow[rows, :], wo).astype(BF16)
    chunk = tok // nt

    def spread_chunks(src, dst):
        copies = []
        for k in range(1, nt):
            at = pl.multiple_of(lax.rem(t + k, nt) * chunk, chunk)
            copies.append(remote(src.at[pl.ds(at, chunk)], dst.at[k - 1], tx(k)))
        return copies

    def gather_chunks(src, dst, total, copies):
        own = pl.ds(pl.multiple_of(t * chunk, chunk), chunk)
        acc = src[own, :].astype(F32)
        for k in range(1, nt):
            copies[k - 1].wait_recv()
            acc = acc + dst[k - 1].astype(F32)
        pending.extend(copies)
        total[own, :] = acc.astype(BF16)
        return [remote(total.at[own], total.at[own], tx(k)) for k in range(1, nt)]

    out_copies = spread_chunks(ob, obuf)

    col_sets = ((0, p1), (p1, p1 + 2 * inner))

    def send_grads(part):
        lo, hi = col_sets[part]
        copies = []
        for k in range(1, nf):
            to = pl.ds(lax.rem(f + k, nf) * nc, nc)
            copies.append(
                remote(gw16.at[to, :, pl.ds(lo, hi - lo)], fbuf.at[k - 1, :, :, pl.ds(lo, hi - lo)], fs(k))
            )
        return copies

    def pass_grads(part, copies):
        lo, hi = col_sets[part]
        for copy in copies:
            copy.wait_recv()
        pending.extend(copies)
        onward = []
        for k in range(nc):
            to = lax.rem(c + k, nc)
            acc = gw16[f * nc + to, :, lo:hi].astype(F32)
            for j in range(1, nf):
                acc = acc + fbuf[j - 1, to, :, lo:hi].astype(F32)
            hsend[k, :, lo:hi] = acc.astype(BF16)
            if k > 0:
                onward.append(
                    remote(hsend.at[k, :, pl.ds(lo, hi - lo)], cbuf.at[k - 1, :, pl.ds(lo, hi - lo)], cx(k))
                )
        return onward

    def finish_grads(part, onward):
        lo, hi = col_sets[part]
        for copy in onward:
            copy.wait_recv()
        pending.extend(onward)
        acc = hsend[0, :, lo:hi].astype(F32)
        for k in range(1, nc):
            acc = acc + cbuf[k - 1, :, lo:hi].astype(F32)
        return acc

    block = 384
    per = block // rows_w

    def store_grads(b, lo, hi, value):
        for s in range(per):
            gw16[b * per + s, :, lo:hi] = value[s * rows_w : (s + 1) * rows_w].astype(BF16)

    for b in range(width // block):
        cols = slice(b * block, (b + 1) * block)
        store_grads(b, p1, p1 + inner, mm_tn(nl[16:, cols], gall[:, p1:]))
        store_grads(b, p1 + inner, p1 + 2 * inner, mm_tn(cot[:, cols], glow[...]))
    grads1 = send_grads(1)

    for i in range(nb):
        lo, hi = i * TB, (i + 1) * TB
        g_diag = gmt[lo:hi, lo:hi]
        g_low = jnp.where(below, g_diag, 0.0)
        g_up = jnp.where(above, g_diag, 0.0)
        for pair in range(hl // 2):
            cols = slice(pair * 128, (pair + 1) * 128)
            cols_r = slice(inner + pair * 128, inner + (pair + 1) * 128)
            ds = []
            for h in (2 * pair, 2 * pair + 1):
                fc = cc[lo:hi, h : h + 1]
                rc = cc[lo:hi, hl + h : hl + h + 1]
                fr = cct[h : h + 1, :]
                rr = cct[hl + h : hl + h + 1, :]
                p = jnp.exp(jnp.minimum(fr[:, lo:hi] - fc, rr[:, lo:hi] - rc))
                ups = [(g_up * p).astype(BF16)]
                lows = [(g_low * p).astype(BF16)]
                if i < nb - 1:
                    p = jnp.exp(fr[:, hi:] - fc)
                    ups.append((gmt[lo:hi, hi:] * p).astype(BF16))
                if i > 0:
                    p = jnp.exp(rr[:, :lo] - rc)
                    lows.insert(0, (gmt[lo:hi, :lo] * p).astype(BF16))
                lows = jnp.concatenate(lows, axis=1) if len(lows) > 1 else lows[0]
                ups = jnp.concatenate(ups, axis=1) if len(ups) > 1 else ups[0]
                ds.append((mm(ups, dy[lo:, cols]), mm(lows, dy[:hi, cols])))
            dw[lo:hi, cols] = jnp.where(pair_left, ds[0][0], ds[1][0])
            dw[lo:hi, cols_r] = jnp.where(pair_left, ds[0][1], ds[1][1])

    for i in range(nb):
        lo, hi = i * TB, (i + 1) * TB
        acc_low = jnp.zeros((TB, lo), F32) if i > 0 else None
        acc_up = jnp.zeros((TB, tok - hi), F32) if i < nb - 1 else None
        acc_diag = jnp.zeros((TB, TB), F32)
        for h in range(hl):
            pair = h // 2
            cols = slice(pair * 128, (pair + 1) * 128)
            cols_r = slice(inner + pair * 128, inner + (pair + 1) * 128)
            mine = pair_left if h % 2 == 0 else jnp.logical_not(pair_left)
            d = jnp.where(mine, dy[lo:hi, cols].astype(F32), 0.0).astype(BF16)
            wf = mm_nt(d, w16[:hi, cols])
            wr = mm_nt(d, w16[lo:, cols_r])
            acc_diag = acc_diag + jnp.where(below, wf[:, lo:], wr[:, :TB]) * pexp[h, lo:hi, lo:hi].astype(F32)
            if i > 0:
                acc_low = acc_low + wf[:, :lo] * pexp[h, lo:hi, :lo].astype(F32)
            if i < nb - 1:
                acc_up = acc_up + wr[:, TB:] * pexp[h, lo:hi, hi:].astype(F32)
        parts = ([acc_low] if i > 0 else []) + [acc_diag] + ([acc_up] if i < nb - 1 else [])
        dg[lo:hi, :] = jnp.where(mix_mask(i), jnp.concatenate(parts, axis=1), 0.0).astype(BF16)

    out_ag = gather_chunks(ob, obuf, oag, out_copies)
    onward1 = pass_grads(1, grads1)

    for copy in back_copies:
        copy.wait_recv()
    pending.extend(back_copies)
    acc_f = jnp.zeros((state_n, inner), F32)
    acc_r = jnp.zeros((state_n, inner), F32)
    for k in range(1, nc):
        new = dec_spread[k - 1][:, :inner] * acc_f + dbuf[k - 1].astype(F32)
        acc_f = jnp.where(k > c, new, acc_f)
    for k in range(nc - 1, 0, -1):
        new = dec_spread[k - 1][:, inner:] * acc_r + dbuf[k - 1].astype(F32)
        acc_r = jnp.where(k <= c, new, acc_r)
    back16[:, :inner] = acc_f.astype(BF16)
    back16[:, inner:] = acc_r.astype(BF16)
    dec_own = exact_right(dec[...], spread)[0:1, :]
    last_row = dec_own * jnp.sum(
        back16[...].astype(F32) * into16[...].astype(F32), axis=0, keepdims=True
    )

    for i in range(nb):
        rows = slice(i * TB, (i + 1) * TB)
        bgt = mm(low[rows, inner : inner + state_n], back16[...])
        w = w16[rows, :].astype(F32)
        qb = q16[rows, :].astype(F32) * bgt
        last_row = last_row + jnp.sum(qb, axis=0, keepdims=True)
        dwl = dw[rows, :]
        dwt = dwl + tol[rows, :] * bgt
        x = low[rows, :inner].astype(F32)
        dted = dte[rows, :] * dwt
        gx = dted[:, :inner] + dted[:, inner:] + skip_row * dmix[rows, :]
        du[rows, :inner] = gx.astype(BF16).astype(F32)
        d = dy[rows, :].astype(F32)
        ac = jnp.concatenate([d, d], axis=1) * yfr[rows, :] - w * dwl - qb
        xd = jnp.concatenate([x, x], axis=1) * dwt
        dcc[rows, :] = exact_right(ac, spread, mm_nt)
        ddt[rows, :] = exact_right(xd, spread, mm_nt)
    last_heads = exact_right(jnp.broadcast_to(last_row, (8, 2 * inner)), spread, mm_nt)[0:1, :]
    place = iota((tok, 1), 0)
    at_end = ((place == tok - 1) & is_fwd) | ((place == 0) & jnp.logical_not(is_fwd))
    dc_all = dcc[...] + jnp.where(at_end, last_heads, 0.0)
    dsums = exact_left(tri, dc_all)
    dld = jnp.where(is_fwd, dsums[tok - 1 : tok, :] - dsums + dc_all, dsums)
    gdt = (ddt[...] + dld * rate_row) * jax.nn.sigmoid(dtr[...])
    gall[:, conv_w:p1] = gdt.astype(BF16)
    misc = slice(conv_w, conv_w + 128)
    sm[...] = jnp.zeros(sm.shape, F32)
    sm[0, 5:6, :inner] = acc_gain
    sm[0, 3:4, misc] = exact_right(
        jnp.broadcast_to(acc_skip, (8, inner)), spread[:, :inner], mm_nt
    )[0:1, :]
    sm[0, 1:2, misc] = jnp.sum(gdt, axis=0, keepdims=True)
    sm[0, 2:3, misc] = jnp.sum(dld * ld[...], axis=0, keepdims=True)

    db = mm_tn(dg[...], c16) + mm_nt(q16[...], back16[...])
    dc = mm(dg[...], b16) + mm_nt(rdy[...], into16[...])
    du[0:tok, inner:] = jnp.concatenate([db, dc], axis=1)
    edge = None
    for i in range(nb):
        rows = slice(i * TB, (i + 1) * TB)
        uu = u[rows, :]
        sg = jax.nn.sigmoid(uu)
        du[rows, :] = du[rows, :] * (sg * (1.0 + uu * (1.0 - sg)))
        if edge is None:
            edge = remote(du.at[pl.ds(0, 8)], du.at[pl.ds(tok, 8)], cx(nc - 1))
    edge.wait_recv()
    pending.append(edge)
    conv_acc = [jnp.zeros((1, conv_w), F32) for _ in range(taps)]
    for i in range(nb):
        lo, hi = i * TB, (i + 1) * TB
        here = seg_col(lo, TB)
        x_rows = xp[16 + lo : 16 + hi, :]
        acc = jnp.zeros((TB, conv_w), F32)
        for d in range(taps):
            m = du[lo + d : hi + d, :]
            if d > 0:
                m = m * (seg_col(lo, TB, d) == here).astype(F32)
            acc = acc + m * kc[taps - 1 - d : taps - d, :]
            conv_acc[taps - 1 - d] = conv_acc[taps - 1 - d] + jnp.sum(m * x_rows, axis=0, keepdims=True)
        gall[lo:hi, :conv_w] = acc.astype(BF16)
    for k in range(taps):
        sm[0, 1 + k : 2 + k, :conv_w] = conv_acc[k]

    w_all = weights(0, p1 + inner)
    acc_norm = jnp.zeros((1, width), F32)
    for i in range(tok // 256):
        rows = slice(i * 256, (i + 1) * 256)
        part = mm_nt(gall[rows, :], w_all)
        hb[rows, :] = part.astype(BF16)
        h = hid[rows, :].astype(F32)
        rr = lax.rsqrt(jnp.mean(h * h, axis=1, keepdims=True) + EPS)
        acc_norm = acc_norm + jnp.sum(part * (h * rr), axis=0, keepdims=True)
    sm[0, 0:1, :] = acc_norm
    head_copies = spread_chunks(hb, hpbuf)

    for b in range(width // block):
        cols = slice(b * block, (b + 1) * block)
        store_grads(b, 0, p1, mm_tn(nl[16:, cols], gall[:, :p1]))
    grads0 = send_grads(0)

    slot = 0
    for level, sends in enumerate(
        ([cx(k) for k in range(1, nc)], [fs(k) for k in range(1, nf)], [tx(k) for k in range(1, nt)])
    ):
        copies = [remote(sm.at[level], smbuf.at[slot + k], dev) for k, dev in enumerate(sends)]
        acc = sm[level]
        for k, copy in enumerate(copies):
            copy.wait_recv()
            acc = acc + smbuf[slot + k]
        pending.extend(copies)
        slot += len(sends)
        if level < 2:
            sm[level + 1] = acc
    both = ((iota((8, width), 0) == 0)
            | ((iota((8, width), 1) >= inner) & (iota((8, width), 1) < conv_w)
               & (iota((8, width), 0) >= 1) & (iota((8, width), 0) <= taps)))
    small[...] = jnp.where(both, acc, sm[2])

    onward0 = pass_grads(0, grads0)
    head_ag = gather_chunks(hb, hpbuf, hag, head_copies)

    got = finish_grads(1, onward1)
    gwz[...] = got[:, :inner]
    gwo[...] = got[:, inner:]
    got = finish_grads(0, onward0)
    gwx[...] = got[:, :inner]
    gwdt[...] = got[:, conv_w:]
    bcs[...] = got[:, inner:conv_w].astype(BF16)
    bc_copies = [remote(bcs, bcbuf.at[k - 1], tx(k)) for k in range(1, nt)]
    acc = got[:, inner:conv_w]
    for k in range(1, nt):
        bc_copies[k - 1].wait_recv()
        acc = acc + bcbuf[k - 1].astype(F32)
    pending.extend(bc_copies)
    gwbc[...] = acc

    for copy in out_ag + head_ag:
        copy.wait_recv()
    pending.extend(out_ag + head_ag)

    @pl.loop(0, nb)
    def _(i):
        rows = pl.ds(pl.multiple_of(i * TB, TB), TB)
        h = hid[rows, :].astype(F32)
        out[rows, :] = (h + oag[rows, :].astype(F32)).astype(BF16)
        rr = lax.rsqrt(jnp.mean(h * h, axis=1, keepdims=True) + EPS)
        q = hag[rows, :].astype(F32) * gain_row
        inner_mean = jnp.mean(q * h, axis=1, keepdims=True)
        gh[rows, :] = cot[rows, :].astype(F32) + rr * (q - h * (rr * rr * inner_mean))

    for copy in pending:
        copy.wait_send()


def per_device(dims, hidden, seq_lengths, norm_gain, weight_x, weight_z, weight_bc, weight_dt,
               conv_x, conv_bc, dt_bias, log_rate, skip_scale, gate_gain, weight_out, cotangent):
    nf, nc, nt = dims
    tok, width = hidden.shape
    rows_w, inner = weight_x.shape
    hl = skip_scale.shape[0]
    shards = nf * nc
    p1 = inner + 256
    cw = p1 + 2 * inner
    conv_w = inner + 128
    state_n = weight_bc.shape[1] // 2
    wdt = jnp.pad(weight_dt.reshape(rows_w, 2 * hl), ((0, 0), (0, 128 - 2 * hl)))
    wsh = jnp.concatenate([weight_x, weight_bc, wdt, weight_z, weight_out.T], axis=1)
    kc = jnp.concatenate([conv_x, conv_bc], axis=1)
    hrow = jnp.pad(
        jnp.stack([dt_bias.reshape(-1), log_rate.reshape(-1)]), ((0, 6), (0, 128 - 2 * hl))
    )
    prow = jnp.stack([jnp.repeat(skip_scale, inner // hl), gate_gain])
    chunk = tok // nt
    n_small = nf + nc + nt - 3
    scratch = {
        "hbuf": ((16, width), BF16),
        "nl": ((tok + 16, width), BF16),
        "wbuf": ((shards, rows_w, cw), BF16),
        "xp": ((tok + 16, conv_w), F32),
        "dtr": ((tok, 128), F32),
        "u": ((tok, conv_w), F32),
        "low": ((tok, conv_w), BF16),
        "z": ((tok, inner), F32),
        "ggate": ((tok, inner), BF16),
        "ld": ((tok, 128), F32),
        "cc": ((tok, 128), F32),
        "cct": ((128, tok), F32),
        "dte": ((tok, 2 * inner), F32),
        "rea": ((tok, 2 * inner), F32),
        "tol": ((tok, 2 * inner), F32),
        "w16": ((tok, 2 * inner), BF16),
        "q16": ((tok, 2 * inner), BF16),
        "gm": ((tok, tok), F32),
        "gmt": ((tok, tok), F32),
        "pexp": ((hl, tok, tok), BF16),
        "yfr": ((tok, 2 * inner), F32),
        "s16": ((state_n, 2 * inner), BF16),
        "sbuf": ((nc - 1, state_n, inner), BF16),
        "dec": ((8, 128), F32),
        "decbuf": ((nc - 1, 8, 128), F32),
        "into16": ((state_n, 2 * inner), BF16),
        "gated": ((tok, inner), F32),
        "mixed": ((tok, inner), F32),
        "dmix": ((tok, inner), F32),
        "dy": ((tok, inner), BF16),
        "st": ((8, tok), F32),
        "stbuf": ((nt - 1, 8, tok), F32),
        "gall": ((tok, p1 + inner), BF16),
        "glow": ((tok, inner), BF16),
        "ob": ((tok, width), BF16),
        "obuf": ((nt - 1, chunk, width), BF16),
        "oag": ((tok, width), BF16),
        "hb": ((tok, width), BF16),
        "hpbuf": ((nt - 1, chunk, width), BF16),
        "hag": ((tok, width), BF16),
        "rdy": ((tok, 2 * inner), BF16),
        "d16": ((state_n, 2 * inner), BF16),
        "dbuf": ((nc - 1, state_n, inner), BF16),
        "back16": ((state_n, 2 * inner), BF16),
        "dg": ((tok, tok), BF16),
        "dw": ((tok, 2 * inner), F32),
        "dcc": ((tok, 128), F32),
        "ddt": ((tok, 128), F32),
        "du": ((tok + 8, conv_w), F32),
        "gw16": ((shards, rows_w, cw), BF16),
        "fbuf": ((nf - 1, nc, rows_w, cw), BF16),
        "hsend": ((nc, rows_w, cw), BF16),
        "cbuf": ((nc - 1, rows_w, cw), BF16),
        "bcs": ((rows_w, 128), BF16),
        "bcbuf": ((nt - 1, rows_w, 128), BF16),
        "sm": ((3, 8, width), F32),
        "smbuf": ((n_small, 8, width), F32),
    }
    n_sems = 1 + 2 * (nc + nf - 2 + (nc - 1) * (nf - 1)) + 3 * (nc - 1) + 5 * (nt - 1) + 1
    n_sems += 2 * (nf - 1 + nc - 1) + n_small + nt - 1
    vmem = pl.BlockSpec(memory_space=pltpu.VMEM)
    f32 = lambda *shape: jax.ShapeDtypeStruct(shape, F32)
    out, gh, gwx, gwz, gwbc, gwdt, gwo, small = pl.pallas_call(
        partial(mixer_kernel, (nf, nc, nt, hl)),
        out_shape=(
            jax.ShapeDtypeStruct((tok, width), BF16), f32(tok, width),
            f32(rows_w, inner), f32(rows_w, inner), f32(rows_w, 128), f32(rows_w, 128),
            f32(rows_w, inner), f32(8, width),
        ),
        in_specs=[pl.BlockSpec(memory_space=pltpu.SMEM)] + [vmem] * 7,
        out_specs=[vmem] * 8,
        scratch_shapes=[pltpu.VMEM(s, d) for s, d in scratch.values()]
        + [pltpu.SemaphoreType.DMA((n_sems,)), pltpu.SemaphoreType.DMA((n_sems,))],
        compiler_params=pltpu.CompilerParams(
            collective_id=0, has_side_effects=True, vmem_limit_bytes=60 << 20
        ),
    )(seq_lengths, hidden, norm_gain[None, :], wsh, kc, hrow, prow, cotangent)
    misc = small[:, conv_w : conv_w + 2 * hl]
    return (
        out, gh, small[0], gwx, gwz, gwbc, gwdt[:, : 2 * hl].reshape(rows_w, 2, hl),
        small[1:5, :inner], small[1:5, inner:conv_w],
        misc[1].reshape(2, hl), misc[2].reshape(2, hl), misc[3, :hl],
        small[5, :inner], gwo.T,
    )


def solution(mesh):
    dims = tuple(mesh.shape[a] for a in ("fsdp", "ctx", "tp"))
    both = ("fsdp", "ctx")
    return jax.shard_map(
        partial(per_device, dims),
        mesh=mesh,
        in_specs=(
            P(both, None), P("fsdp", None), P(), P(both, "tp"), P(both, "tp"), P(both, None),
            P(both, None, "tp"), P(None, "tp"), P(), P(None, "tp"), P(None, "tp"), P("tp"),
            P("tp"), P("tp", both), P(both, None),
        ),
        out_specs=(
            P(both, None), P(both, None), P(), P(both, "tp"), P(both, "tp"), P(both, None),
            P(both, None, "tp"), P(None, "tp"), P(), P(None, "tp"), P(None, "tp"), P("tp"),
            P("tp"), P("tp", both),
        ),
        check_vma=False,
    )
```

```python
from functools import partial

import jax
import jax.numpy as jnp
from jax import lax
from jax.experimental import pallas as pl
from jax.experimental.pallas import tpu as pltpu
from jax.sharding import PartitionSpec as P

MESH = pl.DeviceIdType.MESH
F32 = jnp.float32
BF16 = jnp.bfloat16
EPS = 1e-05
TB = 128
PR = 64
LAG = 3
PUMP = (
    (0, 1, 1, 1), (1, 1, 1, 1), (1, 1, 1, 1), (0, 1, 0, 1), (0, 1, 0, 1), (0, 1, 0, 1), (2, 4, 6, 6, 6)
)


def mm(left, right):
    return lax.dot_general(left, right, (((1,), (0,)), ((), ())), preferred_element_type=F32)


def mm_nt(left, right):
    return lax.dot_general(left, right, (((1,), (1,)), ((), ())), preferred_element_type=F32)


def mm_tn(left, right):
    return lax.dot_general(left, right, (((0,), (0,)), ((), ())), preferred_element_type=F32)


def split3(value):
    high = value.astype(BF16)
    rest = value - high.astype(F32)
    middle = rest.astype(BF16)
    low = (rest - middle.astype(F32)).astype(BF16)
    return high, middle, low


def exact_left(ones, value, dot=mm):
    a, b, c = split3(value)
    return dot(ones, a) + dot(ones, b) + dot(ones, c)


def exact_right(value, ones, dot=mm):
    a, b, c = split3(value)
    return dot(a, ones) + dot(b, ones) + dot(c, ones)


def iota(shape, dim):
    return lax.broadcasted_iota(jnp.int32, shape, dim)


def mixer_kernel(dims, *refs):
    (lens, hid, gain, wx, wz, wbc, wdt, wot, conv_x, conv_bc, dtb, rate, skip, ggain, cot, oag, hag,
     gwx, gwz, gwbc, gwdt, gwo, small, hbuf, nl, wbuf, xp, dtr, u, low, z, ggate, ld, cc, cct, dte,
     rea, tol, w16, q16, gm, gmt, pexp, yfr, s16, sbuf, dec, decbuf, into16, gated, mixed, dmix, dy,
     st, stbuf, gall, glow, ob, oin, oex, hb, hin, hex_, rdy, d16, dbuf, back16, dg, dw, dcc, ddt,
     du, gw16, fbuf, hsend, cbuf, bcs, bcbuf, sm, smbuf, ssem, rsem) = refs
    nf, nc, nt, hl = dims
    tok, width = hid.shape
    rows_w, inner = wx.shape
    pdim = inner // hl
    state_n = wbc.shape[1] // 2
    xo = 2 * state_n
    conv_w = xo + inner
    off = (0, xo + 128, xo + 128 + inner, xo + 128 + 2 * inner, xo + 128 + 3 * inner)
    gall_w = off[3]
    nb = tok // TB
    taps = conv_x.shape[0]
    f, c, t = lax.axis_index("fsdp"), lax.axis_index("ctx"), lax.axis_index("tp")
    base = c * tok
    counter = [0]
    pending = []

    def take(count):
        counter[0] += count
        return counter[0] - count

    def describe(i, src, dst, dev):
        return pltpu.make_async_remote_copy(
            src_ref=src, dst_ref=dst, send_sem=ssem.at[i], recv_sem=rsem.at[i],
            device_id=dev, device_id_type=MESH,
        )

    def remote(src, dst, dev):
        copy = describe(take(1), src, dst, dev)
        copy.start()
        pending.append(copy)
        return copy

    def fs(k):
        return (lax.rem(f + k, nf), c, t)

    def cx(k):
        return (f, lax.rem(c + k, nc), t)

    def tx(k):
        return (f, c, lax.rem(t + k, nt))

    barrier = pltpu.get_barrier_semaphore()
    peers = [fs(k) for k in range(1, nf)] + [cx(k) for k in range(1, nc)] + [tx(k) for k in range(1, nt)]
    for dev in peers:
        pl.semaphore_signal(barrier, inc=1, device_id=dev, device_id_type=MESH)

    me = f * nc + c
    wbuf[me, :, 0:xo] = wbc[...]
    flat = jnp.concatenate(
        [wdt[h].astype(F32) for h in range(hl)] + [jnp.zeros((16 - 2 * hl, rows_w), F32)], axis=0
    ).astype(BF16)
    lane_of = lax.rem(iota((16, 128), 0), 2) * hl + lax.div(iota((16, 128), 0), 2)
    turn = (iota((16, 128), 1) == lane_of).astype(F32).astype(BF16)
    wbuf[me, :, xo : off[1]] = mm_tn(flat, turn).astype(BF16)
    wbuf[me, :, off[1] : off[2]] = wx[...]
    wbuf[me, :, off[2] : off[3]] = wz[...]
    wbuf[me, :, off[3] : off[4]] = wot[...]

    lane = iota((1, 128), 1)
    is_fwd = lane < hl
    bias_row = jnp.zeros((1, 128), F32)
    log_row = jnp.zeros((1, 128), F32)
    for d in range(2):
        for h in range(hl):
            bias_row = jnp.where(lane == d * hl + h, dtb[d, h], bias_row)
            log_row = jnp.where(lane == d * hl + h, rate[d, h], log_row)
    rate_row = -jnp.exp(log_row)
    head_of = lax.div(iota((1, inner), 1), pdim)
    skip_row = jnp.zeros((1, inner), F32)
    for h in range(hl):
        skip_row = jnp.where(head_of == h, skip[h], skip_row)
    gain_row = gain[...].reshape(1, width)
    gain_gate = ggain[...].reshape(1, inner)

    def norm_low(rows):
        h = rows.astype(F32)
        r = lax.rsqrt(jnp.mean(h * h, axis=1, keepdims=True) + EPS)
        return (h * r * gain_row).astype(BF16)

    @pl.loop(0, nb)
    def _(i):
        at = pl.multiple_of(i * TB, TB)
        nl[pl.ds(16 + at, TB), :] = norm_low(hid[pl.ds(at, TB), :])

    pl.semaphore_wait(barrier, len(peers))

    col_parts = [pl.ds(off[p], off[p + 1] - off[p]) for p in range(4)]
    rim = remote(hid.at[pl.ds(tok - 16, 16)], hbuf, cx(1))
    ctx_copies = []
    fwd_copies = []
    for cols in col_parts:
        own = wbuf.at[me, :, cols]
        ctx_copies.append([remote(own, own, cx(k)) for k in range(1, nc)])
        fwd_copies.append([remote(own, own, fs(k)) for k in range(1, nf)])

    def pass_weights(part):
        for k in range(1, nc):
            ctx_copies[part][k - 1].wait_recv()
            src = wbuf.at[f * nc + lax.rem(c + nc - k, nc), :, col_parts[part]]
            for j in range(1, nf):
                fwd_copies[part].append(remote(src, src, fs(j)))

    def get_weights(part):
        for copy in fwd_copies[part]:
            copy.wait_recv()

    def weights(lo, hi):
        if rows_w % 16 == 0:
            return wbuf[:, :, lo:hi].reshape(width, hi - lo)
        return wbuf[:, :, lo:hi].astype(F32).reshape(width, hi - lo).astype(BF16)

    ends = []
    total = lens[0, 0]
    ends.append(total)
    for k in range(1, lens.shape[1]):
        total = total + lens[0, k]
        ends.append(total)

    def seg_of(pos):
        seg = jnp.where(pos < 0, -1, 0)
        for e in ends:
            seg = seg + jnp.where(pos >= e, 1, 0)
        return seg

    one_pos = jnp.full((1, 1), 0, jnp.int32)
    seg_before = seg_of(one_pos + (base - 1))
    seg_first = seg_of(one_pos + base)
    seg_last = seg_of(one_pos + (base + tok - 1))
    seg_after = seg_of(one_pos + (base + tok))
    seg_row = seg_of(iota((1, tok), 1) + base)
    place_row = iota((1, tok), 1)

    def seg_col(start, count, shift=0):
        return seg_of(iota((count, 1), 0) + (base + start + shift))

    spread = (
        iota((128, 2 * inner), 0) == lax.div(iota((128, 2 * inner), 1), pdim)
    ).astype(F32).astype(BF16)
    tri = (iota((tok, tok), 0) >= iota((tok, tok), 1)).astype(F32).astype(BF16)
    seg_all = seg_col(0, tok)

    rim.wait_recv()
    nl[0:16, :] = norm_low(hbuf[...])
    pass_weights(0)
    get_weights(0)

    w_part = weights(off[0], off[1])
    xp[0:16, :xo] = mm(nl[0:16, :], w_part)[:, :xo]
    for i in range(tok // 256):
        got = mm(nl[16 + i * 256 : 16 + (i + 1) * 256, :], w_part)
        xp[16 + i * 256 : 16 + (i + 1) * 256, :xo] = got[:, :xo]
        dtr[i * 256 : (i + 1) * 256, :] = got[:, xo:] + bias_row

    def conv_forward(cols, taps_ref):
        for i in range(nb):
            lo = i * TB
            here = seg_col(lo, TB)
            acc = xp[16 + lo : 16 + lo + TB, cols] * taps_ref[taps - 1 : taps, :]
            for d in range(1, taps):
                match = (seg_col(lo, TB, -d) == here).astype(F32)
                acc = acc + xp[16 + lo - d : 16 + lo - d + TB, cols] * taps_ref[taps - 1 - d : taps - d, :] * match
            u[lo : lo + TB, cols] = acc
            low[lo : lo + TB, cols] = (acc * jax.nn.sigmoid(acc)).astype(BF16)

    bc_cols, x_cols = slice(0, xo), slice(xo, conv_w)
    conv_forward(bc_cols, conv_bc)
    raw = dtr[...]
    step = jnp.maximum(raw, 0.0) + jnp.log1p(jnp.exp(-jnp.abs(raw)))
    decay = step * rate_row
    ld[...] = decay
    sums = exact_left(tri, decay)
    tot = sums[tok - 1 : tok, :]
    cum = jnp.where(is_fwd, sums, tot - sums + decay)
    cc[...] = cum
    cct[...] = cum.T
    dec_mask = jnp.where(
        is_fwd,
        (seg_last == seg_before).astype(F32),
        (seg_first == seg_after).astype(F32),
    )
    dec[...] = jnp.broadcast_to(jnp.exp(tot) * dec_mask, (8, 128))
    dec_copies = [remote(dec, decbuf.at[k - 1], cx(k)) for k in range(1, nc)]
    reach = jnp.exp(cum) * jnp.where(
        is_fwd, (seg_all == seg_before).astype(F32), (seg_all == seg_after).astype(F32)
    )
    to_end = jnp.exp(tot - cum) * jnp.where(
        is_fwd, (seg_all == seg_last).astype(F32), (seg_all == seg_first).astype(F32)
    )
    dte[...] = exact_right(step, spread)
    tol[...] = exact_right(to_end, spread)
    pass_weights(1)
    rea[...] = exact_right(reach, spread)

    b16 = low[:, 0:state_n]
    c16 = low[:, state_n:xo]

    def mix_mask(i):
        same = seg_col(i * TB, TB) == seg_row
        return same & (iota((TB, 1), 0) + i * TB != place_row)

    for i in range(nb):
        lo, hi = i * TB, (i + 1) * TB
        mask = mix_mask(i)
        gm[lo:hi, :] = jnp.where(mask, mm_nt(c16[lo:hi], b16), 0.0)
        gmt[lo:hi, :] = jnp.where(mask, mm_nt(b16[lo:hi], c16), 0.0)

    get_weights(1)
    w_part = weights(off[1], off[2])
    xp[0:16, xo:] = mm(nl[0:16, :], w_part)
    for i in range(tok // 256):
        xp[16 + i * 256 : 16 + (i + 1) * 256, xo:] = mm(nl[16 + i * 256 : 16 + (i + 1) * 256, :], w_part)
    conv_forward(x_cols, conv_x)

    @pl.loop(0, nb)
    def _(i):
        rows = pl.ds(pl.multiple_of(i * TB, TB), TB)
        x = low[rows, xo:].astype(F32)
        w = (jnp.concatenate([x, x], axis=1) * dte[rows, :]).astype(BF16)
        w16[rows, :] = w
        q16[rows, :] = (w.astype(F32) * tol[rows, :]).astype(BF16)

    s16[...] = mm_tn(b16, q16[...]).astype(BF16)

    def half_of(forward):
        return pl.ds(pl.multiple_of(jnp.where(forward, 0, inner), 128), inner)

    state_copies = []
    for k in range(1, nc):
        forward = lax.rem(c + k, nc) > c
        state_copies.append(remote(s16.at[:, half_of(forward)], sbuf.at[k - 1], cx(k)))

    local = iota((TB, TB), 0)
    below = local > iota((TB, TB), 1)
    above = local < iota((TB, TB), 1)
    pair_left = iota((1, 128), 1) < pdim

    def pair_cols(pair):
        return (
            slice(pair * 128, (pair + 1) * 128),
            slice(inner + pair * 128, inner + (pair + 1) * 128),
        )

    def beside(parts):
        return jnp.concatenate(parts, axis=1) if len(parts) > 1 else parts[0]

    for i in range(nb):
        lo, hi = i * TB, (i + 1) * TB
        if i == 2:
            pass_weights(2)
        g_diag = gm[lo:hi, lo:hi]
        g_low = jnp.where(below, g_diag, 0.0)
        g_up = jnp.where(above, g_diag, 0.0)
        for pair in range(hl // 2):
            cols, cols_r = pair_cols(pair)
            ys = []
            for h in (2 * pair, 2 * pair + 1):
                fc = cc[lo:hi, h : h + 1]
                rc = cc[lo:hi, hl + h : hl + h + 1]
                fr = cct[h : h + 1, :]
                rr = cct[hl + h : hl + h + 1, :]
                p = jnp.exp(jnp.minimum(fc - fr[:, lo:hi], rc - rr[:, lo:hi]))
                pexp[h, lo:hi, lo:hi] = p.astype(BF16)
                lows = [(g_low * p).astype(BF16)]
                ups = [(g_up * p).astype(BF16)]
                if i > 0:
                    p = jnp.exp(fc - fr[:, :lo])
                    pexp[h, lo:hi, :lo] = p.astype(BF16)
                    lows.insert(0, (gm[lo:hi, :lo] * p).astype(BF16))
                if i < nb - 1:
                    p = jnp.exp(rc - rr[:, hi:])
                    pexp[h, lo:hi, hi:] = p.astype(BF16)
                    ups.append((gm[lo:hi, hi:] * p).astype(BF16))
                ys.append((mm(beside(lows), w16[:hi, cols]), mm(beside(ups), w16[lo:, cols_r])))
            yfr[lo:hi, cols] = jnp.where(pair_left, ys[0][0], ys[1][0])
            yfr[lo:hi, cols_r] = jnp.where(pair_left, ys[0][1], ys[1][1])

    get_weights(2)
    w_part = weights(off[2], off[3])
    for i in range(tok // 256):
        z[i * 256 : (i + 1) * 256, :] = mm(nl[16 + i * 256 : 16 + (i + 1) * 256, :], w_part)
    pass_weights(3)
    get_weights(3)
    wo = weights(off[3], off[4])
    for i in range(tok // 256):
        rows = slice(i * 256, (i + 1) * 256)
        ggate[rows, :] = mm(cot[rows, :], wo).astype(BF16)

    dec_spread = []
    for k in range(1, nc):
        dec_copies[k - 1].wait_recv()
        dec_spread.append(exact_right(decbuf[k - 1], spread)[0:1, :])
    for copy in state_copies:
        copy.wait_recv()
    acc_f = jnp.zeros((state_n, inner), F32)
    acc_r = jnp.zeros((state_n, inner), F32)
    for k in range(nc - 1, 0, -1):
        new = dec_spread[k - 1][:, :inner] * acc_f + sbuf[k - 1].astype(F32)
        acc_f = jnp.where(k <= c, new, acc_f)
    for k in range(1, nc):
        new = dec_spread[k - 1][:, inner:] * acc_r + sbuf[k - 1].astype(F32)
        acc_r = jnp.where(k > c, new, acc_r)
    into16[:, :inner] = acc_f.astype(BF16)
    into16[:, inner:] = acc_r.astype(BF16)

    row_s = (iota((8, inner), 0) == 0).astype(F32).astype(BF16)
    row_t = (iota((8, inner), 0) == 1).astype(F32).astype(BF16)
    for i in range(nb):
        rows = slice(i * TB, (i + 1) * TB)
        carried = mm(low[rows, state_n:xo], into16[...]) * rea[rows, :]
        y = yfr[rows, :] + carried
        yfr[rows, :] = y
        mix = y[:, :inner] + y[:, inner:] + skip_row * low[rows, xo:].astype(F32)
        mixed[rows, :] = mix
        zz = z[rows, :]
        gt = mix * zz * jax.nn.sigmoid(zz)
        gated[rows, :] = gt
        s = exact_left(row_s, gt * gt, mm_nt)
        s = s + exact_left(row_t, ggate[rows, :].astype(F32) * gain_gate * gt, mm_nt)
        st[:, rows] = s
    st_copies = [remote(st, stbuf.at[k - 1], tx(k)) for k in range(1, nt)]
    rows_sum = st[...]
    for k in range(1, nt):
        st_copies[k - 1].wait_recv()
    for k in range(nt):
        part = jnp.where(t == k, st[...], 0.0)
        for j in range(1, nt):
            part = jnp.where(lax.rem(t + nt - j, nt) == k, stbuf[j - 1], part)
        rows_sum = part if k == 0 else rows_sum + part
    total_inner = inner * nt
    r_row = lax.rsqrt(rows_sum[0:1, :] * (1.0 / total_inner) + EPS)
    q_row = r_row * r_row * r_row * rows_sum[1:2, :] * (-1.0 / total_inner)
    row8 = iota((8, tok), 0)
    rq = jnp.where(row8 == 0, r_row, jnp.where(row8 == 1, q_row, 0.0))
    pick = (iota((8, 256), 0) == lax.div(iota((8, 256), 1), 128)).astype(F32).astype(BF16)
    rq_cols = exact_right(rq, pick, mm_tn)

    is_mid = (t > 0) & (t < nt - 1)
    is_end = (t == 0) | (t == nt - 1)
    inside = (f, c, 1 + lax.div(t, nt - 1))
    across = (f, c, nt - 1 - t)
    outside = (f, c, (t - 1) * (nt - 1))
    pieces = tok // PR

    def piece(ref, p):
        return ref.at[pl.ds(p * PR, PR)]

    class Line:
        def __init__(self, own, inbox, exchange, sums):
            self.own, self.inbox, self.exchange, self.sums = own, inbox, exchange, sums
            self.ids = take(3 * pieces)

        def up(self, p):
            return describe(self.ids + p, piece(self.own, p), self.inbox.at[p], inside)

        def over(self, p):
            return describe(self.ids + pieces + p, piece(self.own, p), self.exchange.at[p], across)

        def down(self, p):
            return describe(self.ids + 2 * pieces + p, piece(self.sums, p), piece(self.sums, p), outside)

        def first(self, p):
            self.up(p).wait_recv()
            rows = slice(p * PR, (p + 1) * PR)
            both = self.own[rows, :].astype(F32) + self.inbox[p].astype(F32)
            self.own[rows, :] = both.astype(BF16)
            self.over(p).start()

        def second(self, p):
            self.over(p).wait_recv()
            rows = slice(p * PR, (p + 1) * PR)
            both = self.own[rows, :].astype(F32) + self.exchange[p].astype(F32)
            self.sums[rows, :] = both.astype(BF16)
            self.down(p).start()

        def begin(self, p_list):
            @pl.when(is_end)
            def _():
                for p in p_list:
                    self.up(p).start()

        def close(self):
            @pl.when(is_end)
            def _():
                for p in range(pieces):
                    self.down(p).wait_recv()
                for p in range(pieces):
                    self.up(p).wait_send()

            @pl.when(is_mid)
            def _():
                for p in range(pieces):
                    self.over(p).wait_send()
                    self.down(p).wait_send()

        def actions(self):
            todo = []
            for p in range(pieces + LAG):
                if p < pieces:
                    todo.append(partial(self.first, p))
                if p >= LAG:
                    todo.append(partial(self.second, p - LAG))
            return todo

    line_o = Line(ob, oin, oex, oag)
    line_h = Line(hb, hin, hex_, hag)
    todo = line_o.actions()

    def pump(count):
        now = [todo.pop(0) for _ in range(min(count, len(todo)))]
        if now:
            @pl.when(is_mid)
            def _():
                for action in now:
                    action()

    acc_gain = jnp.zeros((1, inner), F32)
    acc_skip = jnp.zeros((1, inner), F32)
    for i in range(nb):
        rows = slice(i * TB, (i + 1) * TB)
        r = rq_cols[rows, 0:1]
        q = rq_cols[rows, 128:129]
        gt = gated[rows, :]
        gg = ggate[rows, :].astype(F32)
        ghat = gt * r
        gl = (ghat * gain_gate).astype(BF16)
        glow[rows, :] = gl
        ob[rows, :] = mm_nt(gl, wo).astype(BF16)
        line_o.begin(range(i * TB // PR, (i + 1) * TB // PR))
        acc_gain = acc_gain + jnp.sum(gg * ghat, axis=0, keepdims=True)
        ggated = gg * gain_gate * r + gt * q
        zz = z[rows, :]
        sg = jax.nn.sigmoid(zz)
        dm = ggated * zz * sg
        mix = mixed[rows, :]
        gall[rows, off[2] :] = (ggated * mix * (sg * (1.0 + zz * (1.0 - sg)))).astype(BF16)
        dmix[rows, :] = dm
        acc_skip = acc_skip + jnp.sum(dm * low[rows, xo:].astype(F32), axis=0, keepdims=True)
        d = dm.astype(BF16)
        dy[rows, :] = d
        rdy[rows, :] = (jnp.concatenate([d, d], axis=1).astype(F32) * rea[rows, :]).astype(BF16)

    d16[...] = mm_tn(low[:, state_n:xo], rdy[...]).astype(BF16)
    back_copies = []
    for k in range(1, nc):
        forward = lax.rem(c + k, nc) < c
        back_copies.append(remote(d16.at[:, half_of(forward)], dbuf.at[k - 1], cx(k)))

    col_sets = ((0, off[2]), (off[2], off[4]))

    def send_grads(part):
        lo, hi = col_sets[part]
        copies = []
        for k in range(1, nf):
            to = pl.ds(lax.rem(f + k, nf) * nc, nc)
            copies.append(
                remote(gw16.at[to, :, pl.ds(lo, hi - lo)], fbuf.at[k - 1, :, :, pl.ds(lo, hi - lo)], fs(k))
            )
        return copies

    def pass_grads(part, copies):
        lo, hi = col_sets[part]
        for copy in copies:
            copy.wait_recv()
        onward = []
        for k in list(range(1, nc)) + [0]:
            to = lax.rem(c + k, nc)
            acc = gw16[f * nc + to, :, lo:hi].astype(F32)
            for j in range(1, nf):
                acc = acc + fbuf[j - 1, to, :, lo:hi].astype(F32)
            hsend[k, :, lo:hi] = acc.astype(BF16)
            if k > 0:
                onward.append(
                    remote(hsend.at[k, :, pl.ds(lo, hi - lo)], cbuf.at[k - 1, :, pl.ds(lo, hi - lo)], cx(k))
                )
        return onward

    def finish_grads(part, onward):
        lo, hi = col_sets[part]
        for copy in onward:
            copy.wait_recv()
        acc = hsend[0, :, lo:hi].astype(F32)
        for k in range(1, nc):
            acc = acc + cbuf[k - 1, :, lo:hi].astype(F32)
        return acc

    block = 384
    per = block // rows_w

    def store_grads(b, lo, hi, value):
        for s in range(per):
            gw16[b * per + s, :, lo:hi] = value[s * rows_w : (s + 1) * rows_w].astype(BF16)

    for b in range(width // block):
        cols = slice(b * block, (b + 1) * block)
        store_grads(b, off[2], off[3], mm_tn(nl[16:, cols], gall[:, off[2] :]))
        store_grads(b, off[3], off[4], mm_tn(cot[:, cols], glow[...]))
    grads1 = send_grads(1)

    for i in range(nb):
        lo, hi = i * TB, (i + 1) * TB
        g_diag = gmt[lo:hi, lo:hi]
        g_low = jnp.where(below, g_diag, 0.0)
        g_up = jnp.where(above, g_diag, 0.0)
        for pair in range(hl // 2):
            cols, cols_r = pair_cols(pair)
            ds = []
            for h in (2 * pair, 2 * pair + 1):
                fc = cc[lo:hi, h : h + 1]
                rc = cc[lo:hi, hl + h : hl + h + 1]
                fr = cct[h : h + 1, :]
                rr = cct[hl + h : hl + h + 1, :]
                p = jnp.exp(jnp.minimum(fr[:, lo:hi] - fc, rr[:, lo:hi] - rc))
                ups = [(g_up * p).astype(BF16)]
                lows = [(g_low * p).astype(BF16)]
                if i < nb - 1:
                    p = jnp.exp(fr[:, hi:] - fc)
                    ups.append((gmt[lo:hi, hi:] * p).astype(BF16))
                if i > 0:
                    p = jnp.exp(rr[:, :lo] - rc)
                    lows.insert(0, (gmt[lo:hi, :lo] * p).astype(BF16))
                ds.append((mm(beside(ups), dy[lo:, cols]), mm(beside(lows), dy[:hi, cols])))
            dw[lo:hi, cols] = jnp.where(pair_left, ds[0][0], ds[1][0])
            dw[lo:hi, cols_r] = jnp.where(pair_left, ds[0][1], ds[1][1])
        pump(PUMP[0][i])

    for i in range(nb):
        lo, hi = i * TB, (i + 1) * TB
        acc_low = jnp.zeros((TB, lo), F32) if i > 0 else None
        acc_up = jnp.zeros((TB, tok - hi), F32) if i < nb - 1 else None
        acc_diag = jnp.zeros((TB, TB), F32)
        for h in range(hl):
            cols, cols_r = pair_cols(h // 2)
            mine = pair_left if h % 2 == 0 else jnp.logical_not(pair_left)
            d = jnp.where(mine, dy[lo:hi, cols].astype(F32), 0.0).astype(BF16)
            wf = mm_nt(d, w16[:hi, cols])
            wr = mm_nt(d, w16[lo:, cols_r])
            acc_diag = acc_diag + jnp.where(below, wf[:, lo:], wr[:, :TB]) * pexp[h, lo:hi, lo:hi].astype(F32)
            if i > 0:
                acc_low = acc_low + wf[:, :lo] * pexp[h, lo:hi, :lo].astype(F32)
            if i < nb - 1:
                acc_up = acc_up + wr[:, TB:] * pexp[h, lo:hi, hi:].astype(F32)
        parts = ([acc_low] if i > 0 else []) + [acc_diag] + ([acc_up] if i < nb - 1 else [])
        dg[lo:hi, :] = jnp.where(mix_mask(i), beside(parts), 0.0).astype(BF16)
        pump(PUMP[1][i])

    onward1 = pass_grads(1, grads1)

    for copy in back_copies:
        copy.wait_recv()
    acc_f = jnp.zeros((state_n, inner), F32)
    acc_r = jnp.zeros((state_n, inner), F32)
    for k in range(1, nc):
        new = dec_spread[k - 1][:, :inner] * acc_f + dbuf[k - 1].astype(F32)
        acc_f = jnp.where(k > c, new, acc_f)
    for k in range(nc - 1, 0, -1):
        new = dec_spread[k - 1][:, inner:] * acc_r + dbuf[k - 1].astype(F32)
        acc_r = jnp.where(k <= c, new, acc_r)
    back16[:, :inner] = acc_f.astype(BF16)
    back16[:, inner:] = acc_r.astype(BF16)
    dec_own = exact_right(dec[...], spread)[0:1, :]
    last_row = dec_own * jnp.sum(
        back16[...].astype(F32) * into16[...].astype(F32), axis=0, keepdims=True
    )

    for i in range(nb):
        rows = slice(i * TB, (i + 1) * TB)
        bgt = mm(low[rows, 0:state_n], back16[...])
        w = w16[rows, :].astype(F32)
        qb = q16[rows, :].astype(F32) * bgt
        last_row = last_row + jnp.sum(qb, axis=0, keepdims=True)
        dwl = dw[rows, :]
        dwt = dwl + tol[rows, :] * bgt
        x = low[rows, xo:].astype(F32)
        dted = dte[rows, :] * dwt
        gx = dted[:, :inner] + dted[:, inner:] + skip_row * dmix[rows, :]
        du[rows, xo:] = gx.astype(BF16).astype(F32)
        d = dy[rows, :].astype(F32)
        ac = jnp.concatenate([d, d], axis=1) * yfr[rows, :] - w * dwl - qb
        xd = jnp.concatenate([x, x], axis=1) * dwt
        dcc[rows, :] = exact_right(ac, spread, mm_nt)
        ddt[rows, :] = exact_right(xd, spread, mm_nt)
        pump(PUMP[2][i])
    last_heads = exact_right(jnp.broadcast_to(last_row, (8, 2 * inner)), spread, mm_nt)[0:1, :]
    place = iota((tok, 1), 0)
    at_end = ((place == tok - 1) & is_fwd) | ((place == 0) & jnp.logical_not(is_fwd))
    dc_all = dcc[...] + jnp.where(at_end, last_heads, 0.0)
    dsums = exact_left(tri, dc_all)
    dld = jnp.where(is_fwd, dsums[tok - 1 : tok, :] - dsums + dc_all, dsums)
    gdt = (ddt[...] + dld * rate_row) * jax.nn.sigmoid(dtr[...])
    gall[:, xo : off[1]] = gdt.astype(BF16)
    misc = slice(conv_w, conv_w + 128)
    sm[...] = jnp.zeros(sm.shape, F32)
    sm[0, 5:6, :inner] = acc_gain
    sm[0, 3:4, misc] = exact_right(
        jnp.broadcast_to(acc_skip, (8, inner)), spread[:, :inner], mm_nt
    )[0:1, :]
    sm[0, 1:2, misc] = jnp.sum(gdt, axis=0, keepdims=True)
    sm[0, 2:3, misc] = jnp.sum(dld * ld[...], axis=0, keepdims=True)

    db = mm_tn(dg[...], c16) + mm_nt(q16[...], back16[...])
    dc = mm(dg[...], b16) + mm_nt(rdy[...], into16[...])
    du[0:tok, :xo] = jnp.concatenate([db, dc], axis=1)
    edge = None
    for i in range(nb):
        rows = slice(i * TB, (i + 1) * TB)
        uu = u[rows, :]
        sg = jax.nn.sigmoid(uu)
        du[rows, :] = du[rows, :] * (sg * (1.0 + uu * (1.0 - sg)))
        if edge is None:
            edge = remote(du.at[pl.ds(0, 8)], du.at[pl.ds(tok, 8)], cx(nc - 1))
        pump(PUMP[3][i])
    edge.wait_recv()
    taps_of = jnp.concatenate([conv_bc[...], conv_x[...]], axis=1)
    conv_acc = [jnp.zeros((1, conv_w), F32) for _ in range(taps)]
    for i in range(nb):
        lo, hi = i * TB, (i + 1) * TB
        here = seg_col(lo, TB)
        x_rows = xp[16 + lo : 16 + hi, :]
        acc = jnp.zeros((TB, conv_w), F32)
        for d in range(taps):
            m = du[lo + d : hi + d, :]
            if d > 0:
                m = m * (seg_col(lo, TB, d) == here).astype(F32)
            acc = acc + m * taps_of[taps - 1 - d : taps - d, :]
            conv_acc[taps - 1 - d] = conv_acc[taps - 1 - d] + jnp.sum(m * x_rows, axis=0, keepdims=True)
        gall[lo:hi, :xo] = acc[:, :xo].astype(BF16)
        gall[lo:hi, off[1] : off[2]] = acc[:, xo:].astype(BF16)
        pump(PUMP[4][i])
    for k in range(taps):
        sm[0, 1 + k : 2 + k, :conv_w] = conv_acc[k]

    w_all = weights(0, gall_w)
    acc_norm = jnp.zeros((1, width), F32)
    for i in range(nb):
        rows = slice(i * TB, (i + 1) * TB)
        part = mm_nt(gall[rows, :], w_all)
        hb[rows, :] = part.astype(BF16)
        line_h.begin(range(i * TB // PR, (i + 1) * TB // PR))
        h = hid[rows, :].astype(F32)
        rr = lax.rsqrt(jnp.mean(h * h, axis=1, keepdims=True) + EPS)
        acc_norm = acc_norm + jnp.sum(part * (h * rr), axis=0, keepdims=True)
        pump(PUMP[5][i])
    sm[0, 0:1, :] = acc_norm
    late = line_h.actions()
    mixed_todo = []
    while todo or late:
        if todo:
            mixed_todo.append(todo.pop(0))
        if late:
            mixed_todo.append(late.pop(0))
    todo.extend(mixed_todo)

    def small_send(level, slot, sends):
        return [remote(sm.at[level], smbuf.at[slot + k], dev) for k, dev in enumerate(sends)]

    def small_sum(level, slot, copies):
        acc = sm[level]
        for k, copy in enumerate(copies):
            copy.wait_recv()
            acc = acc + smbuf[slot + k]
        return acc

    sm0 = small_send(0, 0, [cx(k) for k in range(1, nc)])

    for b in range(width // block):
        cols = slice(b * block, (b + 1) * block)
        got = mm_tn(nl[16:, cols], gall[:, : off[2]])
        store_grads(b, 0, off[2], got)
    grads0 = send_grads(0)
    pump(PUMP[6][0])
    sm[1] = small_sum(0, 0, sm0)
    sm1 = small_send(1, nc - 1, [fs(k) for k in range(1, nf)])
    onward0 = pass_grads(0, grads0)
    pump(PUMP[6][1])
    sm[2] = small_sum(1, nc - 1, sm1)
    sm2 = small_send(2, nc + nf - 2, [tx(k) for k in range(1, nt)])
    got = finish_grads(1, onward1)
    gwz[...] = got[:, :inner]
    gwo[...] = got[:, inner:]
    pump(PUMP[6][2])
    got = finish_grads(0, onward0)
    gwx[...] = got[:, off[1] :]
    gwdt[...] = got[:, xo : off[1]]
    bcs[...] = got[:, :xo].astype(BF16)
    bc_copies = [remote(bcs, bcbuf.at[k - 1], tx(k)) for k in range(1, nt)]
    pump(PUMP[6][3])
    shape8 = (8, width)
    over_tp = (iota(shape8, 0) == 0) | (
        (iota(shape8, 1) < xo) & (iota(shape8, 0) >= 1) & (iota(shape8, 0) <= taps)
    )
    acc = sm[2]
    for copy in sm2:
        copy.wait_recv()

    def tp_order(own, box, first):
        total = None
        for k in range(nt):
            part = jnp.where(t == k, own, 0.0)
            for j in range(1, nt):
                part = jnp.where(lax.rem(t + nt - j, nt) == k, box[first + j - 1].astype(F32), part)
            total = part if total is None else total + part
        return total

    small[...] = jnp.where(over_tp, tp_order(sm[2], smbuf, nc + nf - 2), acc)
    pump(PUMP[6][4])
    for copy in bc_copies:
        copy.wait_recv()
    gwbc[...] = tp_order(bcs[...].astype(F32), bcbuf, 0)
    pump(len(todo))

    line_o.close()
    line_h.close()
    for copy in pending:
        copy.wait_send()


def finish_kernel(dims, hid, cot, gain, hsum, osum, gx, gz, gbc, gdt, go, small,
                  out, gh, o_norm, o_x, o_z, o_bc, o_dt, o_cx, o_cbc, o_bias, o_rate, o_skip, o_gain, o_out):
    hl, xo = dims
    width = hid.shape[1]
    rows_w, inner = gx.shape
    h = hid[...].astype(F32)
    out[...] = (h + osum[...].astype(F32)).astype(BF16)
    rr = lax.rsqrt(jnp.mean(h * h, axis=1, keepdims=True) + EPS)
    q = hsum[...].astype(F32) * gain[...].reshape(1, width)
    inner_mean = jnp.mean(q * h, axis=1, keepdims=True)
    gh[...] = cot[...].astype(F32) + rr * (q - h * (rr * rr * inner_mean))

    @pl.when(pl.program_id(0) == 0)
    def _():
        conv_w = xo + inner
        o_norm[...] = small[0:1, :].reshape(width)
        o_x[...] = gx[...]
        o_z[...] = gz[...]
        o_bc[...] = gbc[...]
        o_out[...] = go[...]
        flat = jnp.concatenate([gdt[...], jnp.zeros((128 - rows_w, 128), F32)], axis=0).T
        for k in range(hl):
            for d in range(2):
                o_dt[k, d : d + 1, :] = flat[d * hl + k : d * hl + k + 1, :rows_w]
        taps = o_cx.shape[0]
        o_cx[...] = small[1 : 1 + taps, xo:conv_w]
        o_cbc[...] = small[1 : 1 + taps, :xo]
        for row, ref in ((1, o_bias), (2, o_rate)):
            for d in range(2):
                ref[d : d + 1, :] = small[row : row + 1, conv_w + d * hl : conv_w + (d + 1) * hl]
        o_skip[...] = small[3:4, conv_w : conv_w + hl].reshape(hl)
        o_gain[...] = small[5:6, :inner].reshape(inner)


def per_device(dims, hidden, seq_lengths, norm_gain, weight_x, weight_z, weight_bc, weight_dt,
               conv_x, conv_bc, dt_bias, log_rate, skip_scale, gate_gain, weight_out, cotangent):
    nf, nc, nt = dims
    tok, width = hidden.shape
    rows_w, inner = weight_x.shape
    hl = skip_scale.shape[0]
    shards = nf * nc
    xo = weight_bc.shape[1]
    state_n = xo // 2
    taps = conv_x.shape[0]
    conv_w = xo + inner
    p2 = xo + 128 + inner
    cw = p2 + 2 * inner
    pieces = tok // PR
    n_small = nf + nc + nt - 3
    scratch = {
        "hbuf": ((16, width), BF16),
        "nl": ((tok + 16, width), BF16),
        "wbuf": ((shards, rows_w, cw), BF16),
        "xp": ((tok + 16, conv_w), F32),
        "dtr": ((tok, 128), F32),
        "u": ((tok, conv_w), F32),
        "low": ((tok, conv_w), BF16),
        "z": ((tok, inner), F32),
        "ggate": ((tok, inner), BF16),
        "ld": ((tok, 128), F32),
        "cc": ((tok, 128), F32),
        "cct": ((128, tok), F32),
        "dte": ((tok, 2 * inner), F32),
        "rea": ((tok, 2 * inner), F32),
        "tol": ((tok, 2 * inner), F32),
        "w16": ((tok, 2 * inner), BF16),
        "q16": ((tok, 2 * inner), BF16),
        "gm": ((tok, tok), F32),
        "gmt": ((tok, tok), F32),
        "pexp": ((hl, tok, tok), BF16),
        "yfr": ((tok, 2 * inner), F32),
        "s16": ((state_n, 2 * inner), BF16),
        "sbuf": ((nc - 1, state_n, inner), BF16),
        "dec": ((8, 128), F32),
        "decbuf": ((nc - 1, 8, 128), F32),
        "into16": ((state_n, 2 * inner), BF16),
        "gated": ((tok, inner), F32),
        "mixed": ((tok, inner), F32),
        "dmix": ((tok, inner), F32),
        "dy": ((tok, inner), BF16),
        "st": ((8, tok), F32),
        "stbuf": ((nt - 1, 8, tok), F32),
        "gall": ((tok, p2 + inner), BF16),
        "glow": ((tok, inner), BF16),
        "ob": ((tok, width), BF16),
        "oin": ((pieces, PR, width), BF16),
        "oex": ((pieces, PR, width), BF16),
        "hb": ((tok, width), BF16),
        "hin": ((pieces, PR, width), BF16),
        "hex": ((pieces, PR, width), BF16),
        "rdy": ((tok, 2 * inner), BF16),
        "d16": ((state_n, 2 * inner), BF16),
        "dbuf": ((nc - 1, state_n, inner), BF16),
        "back16": ((state_n, 2 * inner), BF16),
        "dg": ((tok, tok), BF16),
        "dw": ((tok, 2 * inner), F32),
        "dcc": ((tok, 128), F32),
        "ddt": ((tok, 128), F32),
        "du": ((tok + 8, conv_w), F32),
        "gw16": ((shards, rows_w, cw), BF16),
        "fbuf": ((nf - 1, nc, rows_w, cw), BF16),
        "hsend": ((nc, rows_w, cw), BF16),
        "cbuf": ((nc - 1, rows_w, cw), BF16),
        "bcs": ((rows_w, xo), BF16),
        "bcbuf": ((nt - 1, rows_w, xo), BF16),
        "sm": ((3, 8, width), F32),
        "smbuf": ((n_small, 8, width), F32),
    }
    n_sems = 2 + 4 * (nc + nf - 2 + (nc - 1) * (nf - 1)) + 3 * (nc - 1) + 2 * (nt - 1)
    n_sems += 2 * (nf - 1 + nc - 1) + n_small + 6 * pieces
    vmem = pl.BlockSpec(memory_space=pltpu.VMEM)
    smem = pl.BlockSpec(memory_space=pltpu.SMEM)
    f32 = lambda *shape: jax.ShapeDtypeStruct(shape, F32)
    bf16 = lambda *shape: jax.ShapeDtypeStruct(shape, BF16)
    osum, hsum, gx, gz, gbc, gdt, go, small = pl.pallas_call(
        partial(mixer_kernel, (nf, nc, nt, hl)),
        out_shape=(
            bf16(tok, width), bf16(tok, width), f32(rows_w, inner), f32(rows_w, inner),
            f32(rows_w, xo), f32(rows_w, 128), f32(rows_w, inner), f32(8, width),
        ),
        in_specs=[smem] + [vmem] * 9 + [smem] * 3 + [vmem] * 2,
        out_specs=[vmem] * 8,
        scratch_shapes=[pltpu.VMEM(s, d) for s, d in scratch.values()]
        + [pltpu.SemaphoreType.DMA((n_sems,)), pltpu.SemaphoreType.DMA((n_sems,))],
        compiler_params=pltpu.CompilerParams(
            collective_id=0, has_side_effects=True, vmem_limit_bytes=60 << 20
        ),
    )(
        seq_lengths, hidden, norm_gain, weight_x, weight_z, weight_bc,
        jnp.transpose(weight_dt, (2, 1, 0)), weight_out.T, conv_x, conv_bc, dt_bias, log_rate,
        skip_scale, gate_gain, cotangent,
    )
    row_block = pl.BlockSpec((TB, width), lambda i: (i, 0))

    def whole(*shape):
        return pl.BlockSpec(shape, lambda i: (0,) * len(shape))

    got = pl.pallas_call(
        partial(finish_kernel, (hl, xo)),
        grid=(tok // TB,),
        out_shape=(
            bf16(tok, width), f32(tok, width), f32(width), f32(rows_w, inner), f32(rows_w, inner),
            f32(rows_w, xo), f32(hl, 2, rows_w), f32(taps, inner), f32(taps, xo), f32(2, hl), f32(2, hl),
            f32(hl), f32(inner), f32(rows_w, inner),
        ),
        in_specs=[
            row_block, row_block, whole(width), row_block, row_block, whole(rows_w, inner),
            whole(rows_w, inner), whole(rows_w, xo), whole(rows_w, 128), whole(rows_w, inner),
            whole(8, width),
        ],
        out_specs=[
            row_block, row_block, whole(width), whole(rows_w, inner), whole(rows_w, inner),
            whole(rows_w, xo), whole(hl, 2, rows_w), whole(taps, inner), whole(taps, xo), whole(2, hl),
            whole(2, hl), whole(hl), whole(inner), whole(rows_w, inner),
        ],
        compiler_params=pltpu.CompilerParams(vmem_limit_bytes=60 << 20),
    )(hidden, cotangent, norm_gain, hsum, osum, gx, gz, gbc, gdt, go, small)
    got = list(got)
    got[6] = jnp.transpose(got[6], (2, 1, 0))
    got[13] = got[13].T
    return tuple(got)


def solution(mesh):
    dims = tuple(mesh.shape[a] for a in ("fsdp", "ctx", "tp"))
    both = ("fsdp", "ctx")
    return jax.shard_map(
        partial(per_device, dims),
        mesh=mesh,
        in_specs=(
            P(both, None), P("fsdp", None), P(), P(both, "tp"), P(both, "tp"), P(both, None),
            P(both, None, "tp"), P(None, "tp"), P(), P(None, "tp"), P(None, "tp"), P("tp"),
            P("tp"), P("tp", both), P(both, None),
        ),
        out_specs=(
            P(both, None), P(both, None), P(), P(both, "tp"), P(both, "tp"), P(both, None),
            P(both, None, "tp"), P(None, "tp"), P(), P(None, "tp"), P(None, "tp"), P("tp"),
            P("tp"), P("tp", both),
        ),
        check_vma=False,
    )
```

```python
from functools import partial

import jax
import jax.numpy as jnp
from jax import lax
from jax.experimental import pallas as pl
from jax.experimental.pallas import tpu as pltpu
from jax.sharding import PartitionSpec as P

MESH = pl.DeviceIdType.MESH
F32 = jnp.float32
BF16 = jnp.bfloat16
EPS = 1e-05
TB = 128
PR = 64
LAG = 2
PUMP = (
    (1, 0, 0, 1), (0, 0, 0, 1), (0, 1, 0, 2), (0, 0, 0, 0), (0, 0, 0, 1), (0, 0, 0, 2), (4, 0, 4, 6, 0, 4, 2)
)


def mm(left, right):
    return lax.dot_general(left, right, (((1,), (0,)), ((), ())), preferred_element_type=F32)


def mm_nt(left, right):
    return lax.dot_general(left, right, (((1,), (1,)), ((), ())), preferred_element_type=F32)


def mm_tn(left, right):
    return lax.dot_general(left, right, (((0,), (0,)), ((), ())), preferred_element_type=F32)


def split3(value):
    high = value.astype(BF16)
    rest = value - high.astype(F32)
    middle = rest.astype(BF16)
    low = (rest - middle.astype(F32)).astype(BF16)
    return high, middle, low


def exact_left(ones, value, dot=mm):
    a, b, c = split3(value)
    return dot(ones, a) + dot(ones, b) + dot(ones, c)


def exact_right(value, ones, dot=mm):
    a, b, c = split3(value)
    return dot(a, ones) + dot(b, ones) + dot(c, ones)


def iota(shape, dim):
    return lax.broadcasted_iota(jnp.int32, shape, dim)


def near_right(value, ones):
    high = value.astype(BF16)
    low = (value - high.astype(F32)).astype(BF16)
    return mm_nt(high, ones) + mm_nt(low, ones)


def mixer_kernel(dims, *refs):
    (lens, gain, wdt, conv_x, conv_bc, dtb, rate, skip, ggain, hid_h, cot_h, wx_h, wz_h, wbc_h, wot_h,
     out_h, gh_h, gwx_h, gwz_h, gwbc_h, gwdt_h, gwo_h, small_h,
     hid, cot, oag, hag, out_v, gh_v, gwx, gwz, gwbc, gwdt, gwo, small, hbuf, nl, wbuf, xp, dtr, u, low, z, zd, ggate, ld, cc, cct, dte,
     rea, tol, w16, q16, gm, gmt, pexp, yfr, s16, sbuf, dec, decbuf, into16, gated, mixed, dmix, dy,
     st, stbuf, gall, glow, ob, oin, oex, hb, hin, hex_, rdy, d16, dbuf, back16, dg, dw, dcc, ddt,
     du, gw16, fbuf, hsend, cbuf, bcs, bcbuf, sm, smbuf, tps, tpbuf, ssem, rsem, lsem) = refs
    nf, nc, nt, hl = dims
    tok, width = hid.shape
    rows_w, inner = wx_h.shape
    pdim = inner // hl
    state_n = wbc_h.shape[1] // 2
    xo = 2 * state_n
    conv_w = xo + inner
    off = (0, xo + 128, xo + 128 + inner, xo + 128 + 2 * inner, xo + 128 + 3 * inner)
    gall_w = off[3]
    nb = tok // TB
    taps = conv_x.shape[0]
    f, c, t = lax.axis_index("fsdp"), lax.axis_index("ctx"), lax.axis_index("tp")
    base = c * tok
    counter = [0]
    pending = []

    def take(count):
        counter[0] += count
        return counter[0] - count

    def describe(i, src, dst, dev):
        return pltpu.make_async_remote_copy(
            src_ref=src, dst_ref=dst, send_sem=ssem.at[i], recv_sem=rsem.at[i],
            device_id=dev, device_id_type=MESH,
        )

    def remote(src, dst, dev):
        copy = describe(take(1), src, dst, dev)
        copy.start()
        pending.append(copy)
        return copy

    def fs(k):
        return (lax.rem(f + k, nf), c, t)

    def cx(k):
        return (f, lax.rem(c + k, nc), t)

    def tx(k):
        return (f, c, lax.rem(t + k, nt))

    barrier = pltpu.get_barrier_semaphore()
    peers = [fs(k) for k in range(1, nf)] + [cx(k) for k in range(1, nc)] + [tx(k) for k in range(1, nt)]
    for dev in peers:
        pl.semaphore_signal(barrier, inc=1, device_id=dev, device_id_type=MESH)

    local_count = [0]
    local_copies = []

    def bring(src, dst):
        i = local_count[0]
        local_count[0] += 1
        copy = pltpu.make_async_copy(src, dst, lsem.at[i])
        copy.start()
        return copy

    def keep(src, dst):
        local_copies.append(bring(src, dst))

    me = f * nc + c
    get_hid = bring(hid_h, hid)
    shard_copies = []
    for p, src in ((0, wbc_h), (1, wx_h), (2, wz_h), (3, wot_h)):
        width_p = xo if p == 0 else inner
        shard_copies.append(bring(src, wbuf.at[me, :, pl.ds(off[p], width_p)]))
    get_cot = bring(cot_h, cot)
    flat = jnp.concatenate(
        [wdt[h].astype(F32) for h in range(hl)] + [jnp.zeros((16 - 2 * hl, rows_w), F32)], axis=0
    ).astype(BF16)
    lane_of = lax.rem(iota((16, 128), 0), 2) * hl + lax.div(iota((16, 128), 0), 2)
    turn = (iota((16, 128), 1) == lane_of).astype(F32).astype(BF16)
    wbuf[me, :, xo : off[1]] = mm_tn(flat, turn).astype(BF16)

    lane = iota((1, 128), 1)
    is_fwd = lane < hl
    bias_row = jnp.zeros((1, 128), F32)
    log_row = jnp.zeros((1, 128), F32)
    for d in range(2):
        for h in range(hl):
            bias_row = jnp.where(lane == d * hl + h, dtb[d, h], bias_row)
            log_row = jnp.where(lane == d * hl + h, rate[d, h], log_row)
    rate_row = -jnp.exp(log_row)
    head_of = lax.div(iota((1, inner), 1), pdim)
    skip_row = jnp.zeros((1, inner), F32)
    for h in range(hl):
        skip_row = jnp.where(head_of == h, skip[h], skip_row)
    gain_row = gain[...].reshape(1, width)
    gain_gate = ggain[...].reshape(1, inner)

    def norm_low(rows):
        h = rows.astype(F32)
        r = lax.rsqrt(jnp.mean(h * h, axis=1, keepdims=True) + EPS)
        return (h * r * gain_row).astype(BF16)

    get_hid.wait()

    @pl.loop(0, nb)
    def _(i):
        at = pl.multiple_of(i * TB, TB)
        nl[pl.ds(16 + at, TB), :] = norm_low(hid[pl.ds(at, TB), :])

    for copy in shard_copies:
        copy.wait()
    pl.semaphore_wait(barrier, len(peers))

    col_parts = [pl.ds(off[p], off[p + 1] - off[p]) for p in range(4)]
    rim = remote(hid.at[pl.ds(tok - 16, 16)], hbuf, cx(1))
    ctx_copies = []
    fwd_copies = []

    def send_weights(part):
        own = wbuf.at[me, :, col_parts[part]]
        ctx_copies.append([remote(own, own, cx(k)) for k in range(1, nc)])
        fwd_copies.append([remote(own, own, fs(k)) for k in range(1, nf)])

    for part in range(4):
        send_weights(part)

    def pass_weights(part):
        for k in range(1, nc):
            ctx_copies[part][k - 1].wait_recv()
            src = wbuf.at[f * nc + lax.rem(c + nc - k, nc), :, col_parts[part]]
            for j in range(1, nf):
                fwd_copies[part].append(remote(src, src, fs(j)))

    def get_weights(part):
        for copy in fwd_copies[part]:
            copy.wait_recv()

    def weights(lo, hi):
        if rows_w % 16 == 0:
            return wbuf[:, :, lo:hi].reshape(width, hi - lo)
        return wbuf[:, :, lo:hi].astype(F32).reshape(width, hi - lo).astype(BF16)

    ends = []
    total = lens[0, 0]
    ends.append(total)
    for k in range(1, lens.shape[1]):
        total = total + lens[0, k]
        ends.append(total)

    def seg_of(pos):
        seg = jnp.where(pos < 0, -1, 0)
        for e in ends:
            seg = seg + jnp.where(pos >= e, 1, 0)
        return seg

    one_pos = jnp.full((1, 1), 0, jnp.int32)
    seg_before = seg_of(one_pos + (base - 1))
    seg_first = seg_of(one_pos + base)
    seg_last = seg_of(one_pos + (base + tok - 1))
    seg_after = seg_of(one_pos + (base + tok))
    seg_row = seg_of(iota((1, tok), 1) + base)
    place_row = iota((1, tok), 1)

    def seg_col(start, count, shift=0):
        return seg_of(iota((count, 1), 0) + (base + start + shift))

    spread = (
        iota((128, 2 * inner), 0) == lax.div(iota((128, 2 * inner), 1), pdim)
    ).astype(F32).astype(BF16)
    tri = (iota((tok, tok), 0) >= iota((tok, tok), 1)).astype(F32).astype(BF16)
    seg_all = seg_col(0, tok)

    rim.wait_recv()
    nl[0:16, :] = norm_low(hbuf[...])
    pass_weights(0)
    get_weights(0)

    w_part = weights(off[0], off[1])
    xp[0:16, :xo] = mm(nl[0:16, :], w_part)[:, :xo]
    for i in range(tok // 256):
        got = mm(nl[16 + i * 256 : 16 + (i + 1) * 256, :], w_part)
        xp[16 + i * 256 : 16 + (i + 1) * 256, :xo] = got[:, :xo]
        dtr[i * 256 : (i + 1) * 256, :] = got[:, xo:] + bias_row

    def conv_forward(cols, taps_ref):
        for i in range(nb):
            lo = i * TB
            here = seg_col(lo, TB)
            acc = xp[16 + lo : 16 + lo + TB, cols] * taps_ref[taps - 1 : taps, :]
            for d in range(1, taps):
                match = (seg_col(lo, TB, -d) == here).astype(F32)
                acc = acc + xp[16 + lo - d : 16 + lo - d + TB, cols] * taps_ref[taps - 1 - d : taps - d, :] * match
            sg = jax.nn.sigmoid(acc)
            u[lo : lo + TB, cols] = sg * (1.0 + acc * (1.0 - sg))
            low[lo : lo + TB, cols] = (acc * sg).astype(BF16)

    bc_cols, x_cols = slice(0, xo), slice(xo, conv_w)
    conv_forward(bc_cols, conv_bc)
    raw = dtr[...]
    step = jnp.maximum(raw, 0.0) + jnp.log1p(jnp.exp(-jnp.abs(raw)))
    decay = step * rate_row
    ld[...] = decay
    sums = exact_left(tri, decay)
    tot = sums[tok - 1 : tok, :]
    cum = jnp.where(is_fwd, sums, tot - sums + decay)
    cc[...] = cum
    cct[...] = cum.T
    dec_mask = jnp.where(
        is_fwd,
        (seg_last == seg_before).astype(F32),
        (seg_first == seg_after).astype(F32),
    )
    dec[...] = jnp.exp(tot) * dec_mask
    dec_copies = [remote(dec, decbuf.at[k - 1], cx(k)) for k in range(1, nc)]
    reach = jnp.exp(cum) * jnp.where(
        is_fwd, (seg_all == seg_before).astype(F32), (seg_all == seg_after).astype(F32)
    )
    to_end = jnp.exp(tot - cum) * jnp.where(
        is_fwd, (seg_all == seg_last).astype(F32), (seg_all == seg_first).astype(F32)
    )
    dte[...] = mm(step.astype(BF16), spread).astype(BF16)
    tol[...] = mm(to_end.astype(BF16), spread).astype(BF16)
    pass_weights(1)
    rea[...] = mm(reach.astype(BF16), spread).astype(BF16)

    b16 = low[:, 0:state_n]
    c16 = low[:, state_n:xo]

    def mix_mask(i):
        same = seg_col(i * TB, TB) == seg_row
        return same & (iota((TB, 1), 0) + i * TB != place_row)

    for i in range(nb):
        lo, hi = i * TB, (i + 1) * TB
        mask = mix_mask(i)
        gm[lo:hi, :] = jnp.where(mask, mm_nt(c16[lo:hi], b16), 0.0)
        gmt[lo:hi, :] = jnp.where(mask, mm_nt(b16[lo:hi], c16), 0.0)

    get_weights(1)
    w_part = weights(off[1], off[2])
    xp[0:16, xo:] = mm(nl[0:16, :], w_part)
    for i in range(tok // 256):
        xp[16 + i * 256 : 16 + (i + 1) * 256, xo:] = mm(nl[16 + i * 256 : 16 + (i + 1) * 256, :], w_part)
    conv_forward(x_cols, conv_x)

    @pl.loop(0, nb)
    def _(i):
        rows = pl.ds(pl.multiple_of(i * TB, TB), TB)
        x = low[rows, xo:].astype(F32)
        w = (jnp.concatenate([x, x], axis=1) * dte[rows, :].astype(F32)).astype(BF16)
        w16[rows, :] = w
        q16[rows, :] = (w.astype(F32) * tol[rows, :].astype(F32)).astype(BF16)

    s16[...] = mm_tn(b16, q16[...]).astype(BF16)

    def half_of(forward):
        return pl.ds(pl.multiple_of(jnp.where(forward, 0, inner), 128), inner)

    state_copies = []
    for k in range(1, nc):
        forward = lax.rem(c + k, nc) > c
        state_copies.append(remote(s16.at[:, half_of(forward)], sbuf.at[k - 1], cx(k)))

    local = iota((TB, TB), 0)
    below = local > iota((TB, TB), 1)
    above = local < iota((TB, TB), 1)
    pair_left = iota((1, 128), 1) < pdim

    def pair_cols(pair):
        return (
            slice(pair * 128, (pair + 1) * 128),
            slice(inner + pair * 128, inner + (pair + 1) * 128),
        )

    def beside(parts):
        return jnp.concatenate(parts, axis=1) if len(parts) > 1 else parts[0]

    for i in range(nb):
        lo, hi = i * TB, (i + 1) * TB
        if i == 2:
            pass_weights(2)
        g_diag = gm[lo:hi, lo:hi]
        g_low = jnp.where(below, g_diag, 0.0)
        g_up = jnp.where(above, g_diag, 0.0)
        for pair in range(hl // 2):
            cols, cols_r = pair_cols(pair)
            ys = []
            for h in (2 * pair, 2 * pair + 1):
                fc = cc[lo:hi, h : h + 1]
                rc = cc[lo:hi, hl + h : hl + h + 1]
                fr = cct[h : h + 1, :]
                rr = cct[hl + h : hl + h + 1, :]
                p = jnp.exp(jnp.minimum(fc - fr[:, lo:hi], rc - rr[:, lo:hi]))
                pexp[h, lo:hi, lo:hi] = p.astype(BF16)
                lows = [(g_low * p).astype(BF16)]
                ups = [(g_up * p).astype(BF16)]
                if i > 0:
                    p = jnp.exp(fc - fr[:, :lo])
                    pexp[h, lo:hi, :lo] = p.astype(BF16)
                    lows.insert(0, (gm[lo:hi, :lo] * p).astype(BF16))
                if i < nb - 1:
                    p = jnp.exp(rc - rr[:, hi:])
                    pexp[h, lo:hi, hi:] = p.astype(BF16)
                    ups.append((gm[lo:hi, hi:] * p).astype(BF16))
                ys.append((mm(beside(lows), w16[:hi, cols]), mm(beside(ups), w16[lo:, cols_r])))
            yfr[lo:hi, cols] = jnp.where(pair_left, ys[0][0], ys[1][0])
            yfr[lo:hi, cols_r] = jnp.where(pair_left, ys[0][1], ys[1][1])

    get_weights(2)
    w_part = weights(off[2], off[3])
    for i in range(tok // 256):
        zz = mm(nl[16 + i * 256 : 16 + (i + 1) * 256, :], w_part)
        sg = jax.nn.sigmoid(zz)
        z[i * 256 : (i + 1) * 256, :] = zz * sg
        zd[i * 256 : (i + 1) * 256, :] = sg * (1.0 + zz * (1.0 - sg))

    dec_spread = []
    for k in range(1, nc):
        dec_copies[k - 1].wait_recv()
        dec_spread.append(exact_right(jnp.broadcast_to(decbuf[k - 1], (8, 128)), spread)[0:1, :])
    for copy in state_copies:
        copy.wait_recv()
    acc_f = jnp.zeros((state_n, inner), F32)
    acc_r = jnp.zeros((state_n, inner), F32)
    for k in range(nc - 1, 0, -1):
        new = dec_spread[k - 1][:, :inner] * acc_f + sbuf[k - 1].astype(F32)
        acc_f = jnp.where(k <= c, new, acc_f)
    for k in range(1, nc):
        new = dec_spread[k - 1][:, inner:] * acc_r + sbuf[k - 1].astype(F32)
        acc_r = jnp.where(k > c, new, acc_r)
    into16[:, :inner] = acc_f.astype(BF16)
    into16[:, inner:] = acc_r.astype(BF16)

    ones8 = jnp.ones((8, inner), BF16)
    for i in range(nb):
        rows = slice(i * TB, (i + 1) * TB)
        carried = mm(low[rows, state_n:xo], into16[...]) * rea[rows, :].astype(F32)
        y = yfr[rows, :] + carried
        yfr[rows, :] = y
        mix = y[:, :inner] + y[:, inner:] + skip_row * low[rows, xo:].astype(F32)
        mixed[rows, :] = mix
        gt = mix * z[rows, :]
        gated[rows, :] = gt
        st[0, :, rows] = mm_nt(ones8, (gt * gt).astype(BF16))[0:1]
    s_copies = [remote(st.at[0], stbuf.at[0, k - 1], tx(k)) for k in range(1, nt)]

    pass_weights(3)
    get_weights(3)
    get_cot.wait()
    wo = weights(off[3], off[4])
    for i in range(nb):
        rows = slice(i * TB, (i + 1) * TB)
        gg = mm(cot[rows, :], wo).astype(BF16)
        ggate[rows, :] = gg
        st[1, :, rows] = mm_nt(ones8, (gg.astype(F32) * gain_gate * gated[rows, :]).astype(BF16))[0:1]
    t_copies = [remote(st.at[1], stbuf.at[1, k - 1], tx(k)) for k in range(1, nt)]
    total_inner = inner * nt
    pick = (iota((8, 128), 0) == 0).astype(F32).astype(BF16)

    def row_total(which, copies):
        total = st[which]
        for k in range(1, nt):
            copies[k - 1].wait_recv()
            total = total + stbuf[which, k - 1]
        return total

    r_row = lax.rsqrt(row_total(0, s_copies) * (1.0 / total_inner) + EPS)
    r_cols = exact_right(jnp.broadcast_to(r_row, (8, tok)), pick, mm_tn)

    is_mid = (t > 0) & (t < nt - 1)
    is_end = (t == 0) | (t == nt - 1)
    inside = (f, c, 1 + lax.div(t, nt - 1))
    across = (f, c, nt - 1 - t)
    outside = (f, c, (t - 1) * (nt - 1))
    pieces = tok // PR

    def piece(ref, p):
        return ref.at[pl.ds(p * PR, PR)]

    class Line:
        def __init__(self, own, inbox, exchange, sums, done):
            self.own, self.inbox, self.exchange, self.sums = own, inbox, exchange, sums
            self.done = done
            self.ids = take(3 * pieces)

        def up(self, p):
            return describe(self.ids + p, piece(self.own, p), self.inbox.at[p], inside)

        def over(self, p):
            return describe(self.ids + pieces + p, piece(self.own, p), self.exchange.at[p], across)

        def down(self, p):
            return describe(self.ids + 2 * pieces + p, piece(self.sums, p), piece(self.sums, p), outside)

        def first(self, p):
            self.up(p).wait_recv()
            rows = slice(p * PR, (p + 1) * PR)
            both = self.own[rows, :].astype(F32) + self.inbox[p].astype(F32)
            self.own[rows, :] = both.astype(BF16)
            self.over(p).start()

        def second(self, p):
            self.over(p).wait_recv()
            rows = slice(p * PR, (p + 1) * PR)
            both = (self.own[rows, :].astype(F32) + self.exchange[p].astype(F32)).astype(BF16)
            self.sums[rows, :] = both
            self.down(p).start()
            self.done(p, rows, both)

        def last(self, p):
            self.down(p).wait_recv()
            rows = slice(p * PR, (p + 1) * PR)
            self.done(p, rows, self.sums[rows, :])

        def begin(self, p_list):
            @pl.when(is_end)
            def _():
                for p in p_list:
                    self.up(p).start()

        def close(self):
            @pl.when(is_end)
            def _():
                for p in range(pieces):
                    self.up(p).wait_send()

            @pl.when(is_mid)
            def _():
                for p in range(pieces):
                    self.over(p).wait_send()
                    self.down(p).wait_send()

    def result(i, src, dst, rows):
        return pltpu.make_async_copy(src.at[rows], dst.at[rows], lsem.at[i])

    result_ids = local_count[0]
    local_count[0] += 2 * pieces

    def out_done(p, rows, both):
        out_v[rows, :] = (hid[rows, :].astype(F32) + both.astype(F32)).astype(BF16)
        result(result_ids + p, out_v, out_h, pl.ds(p * PR, PR)).start()

    def head_done(p, rows, both):
        h = hid[rows, :].astype(F32)
        rr = lax.rsqrt(jnp.mean(h * h, axis=1, keepdims=True) + EPS)
        q = both.astype(F32) * gain_row
        inner_mean = jnp.mean(q * h, axis=1, keepdims=True)
        gh_v[rows, :] = cot[rows, :].astype(F32) + rr * (q - h * (rr * rr * inner_mean))
        result(result_ids + pieces + p, gh_v, gh_h, pl.ds(p * PR, PR)).start()

    line_o = Line(ob, oin, oex, oag, out_done)
    line_h = Line(hb, hin, hex_, hag, head_done)
    todo = []
    for p in range(2 * pieces + LAG):
        for q, stage in ((p, 0), (p - LAG, 1)):
            if 0 <= q < 2 * pieces:
                line = line_o if q < pieces else line_h
                todo.append(partial(line.first if stage == 0 else line.second, q % pieces))

    def pump(count):
        now = [todo.pop(0) for _ in range(min(count, len(todo)))]
        if now:
            @pl.when(is_mid)
            def _():
                for action in now:
                    action()

    for i in range(nb):
        rows = slice(i * TB, (i + 1) * TB)
        gl = (gated[rows, :] * r_cols[rows, 0:1] * gain_gate).astype(BF16)
        glow[rows, :] = gl
        ob[rows, :] = mm_nt(gl, wo).astype(BF16)
        line_o.begin(range(i * TB // PR, (i + 1) * TB // PR))

    block = 384
    per = block // rows_w

    def store_grads(b, lo, hi, value):
        for s in range(per):
            gw16[b * per + s, :, lo:hi] = value[s * rows_w : (s + 1) * rows_w].astype(BF16)

    for b in range(width // block):
        cols = slice(b * block, (b + 1) * block)
        store_grads(b, off[3], off[4], mm_tn(cot[:, cols], glow[...]))

    q_row = r_row * r_row * r_row * row_total(1, t_copies) * (-1.0 / total_inner)
    q_cols = exact_right(jnp.broadcast_to(q_row, (8, tok)), pick, mm_tn)
    acc_gain = jnp.zeros((1, inner), F32)
    acc_skip = jnp.zeros((1, inner), F32)
    for i in range(nb):
        rows = slice(i * TB, (i + 1) * TB)
        r = r_cols[rows, 0:1]
        gt = gated[rows, :]
        gg = ggate[rows, :].astype(F32)
        acc_gain = acc_gain + jnp.sum(gg * gt * r, axis=0, keepdims=True)
        ggated = gg * gain_gate * r + gt * q_cols[rows, 0:1]
        dm = ggated * z[rows, :]
        gall[rows, off[2] :] = (ggated * mixed[rows, :] * zd[rows, :]).astype(BF16)
        dmix[rows, :] = dm
        acc_skip = acc_skip + jnp.sum(dm * low[rows, xo:].astype(F32), axis=0, keepdims=True)
        d = dm.astype(BF16)
        dy[rows, :] = d
        rdy[rows, :] = (jnp.concatenate([d, d], axis=1).astype(F32) * rea[rows, :].astype(F32)).astype(BF16)

    d16[...] = mm_tn(low[:, state_n:xo], rdy[...]).astype(BF16)
    back_copies = []
    for k in range(1, nc):
        forward = lax.rem(c + k, nc) < c
        back_copies.append(remote(d16.at[:, half_of(forward)], dbuf.at[k - 1], cx(k)))

    col_sets = ((0, off[2]), (off[2], off[4]))

    def send_grads(part):
        lo, hi = col_sets[part]
        copies = []
        for k in range(1, nf):
            to = pl.ds(lax.rem(f + k, nf) * nc, nc)
            copies.append(
                remote(gw16.at[to, :, pl.ds(lo, hi - lo)], fbuf.at[k - 1, :, :, pl.ds(lo, hi - lo)], fs(k))
            )
        return copies

    def pass_grads(part, copies):
        lo, hi = col_sets[part]
        for copy in copies:
            copy.wait_recv()
        onward = []
        for k in list(range(1, nc)) + [0]:
            to = lax.rem(c + k, nc)
            acc = gw16[f * nc + to, :, lo:hi].astype(F32)
            for j in range(1, nf):
                acc = acc + fbuf[j - 1, to, :, lo:hi].astype(F32)
            hsend[k, :, lo:hi] = acc.astype(BF16)
            if k > 0:
                onward.append(
                    remote(hsend.at[k, :, pl.ds(lo, hi - lo)], cbuf.at[k - 1, :, pl.ds(lo, hi - lo)], cx(k))
                )
        return onward

    def finish_grads(part, onward):
        lo, hi = col_sets[part]
        for copy in onward:
            copy.wait_recv()
        acc = hsend[0, :, lo:hi].astype(F32)
        for k in range(1, nc):
            acc = acc + cbuf[k - 1, :, lo:hi].astype(F32)
        return acc

    for b in range(width // block):
        cols = slice(b * block, (b + 1) * block)
        store_grads(b, off[2], off[3], mm_tn(nl[16:, cols], gall[:, off[2] :]))
    grads1 = send_grads(1)

    for i in range(nb):
        lo, hi = i * TB, (i + 1) * TB
        g_diag = gmt[lo:hi, lo:hi]
        g_low = jnp.where(below, g_diag, 0.0)
        g_up = jnp.where(above, g_diag, 0.0)
        for pair in range(hl // 2):
            cols, cols_r = pair_cols(pair)
            ds = []
            for h in (2 * pair, 2 * pair + 1):
                fc = cc[lo:hi, h : h + 1]
                rc = cc[lo:hi, hl + h : hl + h + 1]
                fr = cct[h : h + 1, :]
                rr = cct[hl + h : hl + h + 1, :]
                p = jnp.exp(jnp.minimum(fr[:, lo:hi] - fc, rr[:, lo:hi] - rc))
                ups = [(g_up * p).astype(BF16)]
                lows = [(g_low * p).astype(BF16)]
                if i < nb - 1:
                    p = jnp.exp(fr[:, hi:] - fc)
                    ups.append((gmt[lo:hi, hi:] * p).astype(BF16))
                if i > 0:
                    p = jnp.exp(rr[:, :lo] - rc)
                    lows.insert(0, (gmt[lo:hi, :lo] * p).astype(BF16))
                ds.append((mm(beside(ups), dy[lo:, cols]), mm(beside(lows), dy[:hi, cols])))
            dw[lo:hi, cols] = jnp.where(pair_left, ds[0][0], ds[1][0])
            dw[lo:hi, cols_r] = jnp.where(pair_left, ds[0][1], ds[1][1])
        pump(PUMP[0][i])

    for i in range(nb):
        lo, hi = i * TB, (i + 1) * TB
        acc_low = jnp.zeros((TB, lo), F32) if i > 0 else None
        acc_up = jnp.zeros((TB, tok - hi), F32) if i < nb - 1 else None
        acc_diag = jnp.zeros((TB, TB), F32)
        for h in range(hl):
            cols, cols_r = pair_cols(h // 2)
            mine = pair_left if h % 2 == 0 else jnp.logical_not(pair_left)
            d = jnp.where(mine, dy[lo:hi, cols].astype(F32), 0.0).astype(BF16)
            wf = mm_nt(d, w16[:hi, cols])
            wr = mm_nt(d, w16[lo:, cols_r])
            acc_diag = acc_diag + jnp.where(below, wf[:, lo:], wr[:, :TB]) * pexp[h, lo:hi, lo:hi].astype(F32)
            if i > 0:
                acc_low = acc_low + wf[:, :lo] * pexp[h, lo:hi, :lo].astype(F32)
            if i < nb - 1:
                acc_up = acc_up + wr[:, TB:] * pexp[h, lo:hi, hi:].astype(F32)
        parts = ([acc_low] if i > 0 else []) + [acc_diag] + ([acc_up] if i < nb - 1 else [])
        dg[lo:hi, :] = jnp.where(mix_mask(i), beside(parts), 0.0).astype(BF16)
        pump(PUMP[1][i])

    for copy in back_copies:
        copy.wait_recv()
    acc_f = jnp.zeros((state_n, inner), F32)
    acc_r = jnp.zeros((state_n, inner), F32)
    for k in range(1, nc):
        new = dec_spread[k - 1][:, :inner] * acc_f + dbuf[k - 1].astype(F32)
        acc_f = jnp.where(k > c, new, acc_f)
    for k in range(nc - 1, 0, -1):
        new = dec_spread[k - 1][:, inner:] * acc_r + dbuf[k - 1].astype(F32)
        acc_r = jnp.where(k <= c, new, acc_r)
    back16[:, :inner] = acc_f.astype(BF16)
    back16[:, inner:] = acc_r.astype(BF16)
    dec_own = exact_right(jnp.broadcast_to(dec[...], (8, 128)), spread)[0:1, :]
    last_row = dec_own * jnp.sum(
        back16[...].astype(F32) * into16[...].astype(F32), axis=0, keepdims=True
    )

    db = mm_tn(dg[...], c16) + mm_nt(q16[...], back16[...])
    dc = mm(dg[...], b16) + mm_nt(rdy[...], into16[...])
    du[0:tok, :xo] = jnp.concatenate([db, dc], axis=1) * u[:, :xo]
    edge = None
    for i in range(nb):
        rows = slice(i * TB, (i + 1) * TB)
        bgt = mm(low[rows, 0:state_n], back16[...])
        w = w16[rows, :].astype(F32)
        qb = q16[rows, :].astype(F32) * bgt
        last_row = last_row + jnp.sum(qb, axis=0, keepdims=True)
        dwl = dw[rows, :]
        dwt = dwl + tol[rows, :].astype(F32) * bgt
        x = low[rows, xo:].astype(F32)
        dted = dte[rows, :].astype(F32) * dwt
        gx = dted[:, :inner] + dted[:, inner:] + skip_row * dmix[rows, :]
        du[rows, xo:] = gx.astype(BF16).astype(F32) * u[rows, xo:]
        if edge is None:
            edge = remote(du.at[pl.ds(0, 8)], du.at[pl.ds(tok, 8)], cx(nc - 1))
        d = dy[rows, :].astype(F32)
        ac = jnp.concatenate([d, d], axis=1) * yfr[rows, :] - w * dwl - qb
        xd = jnp.concatenate([x, x], axis=1) * dwt
        dcc[rows, :] = near_right(ac, spread)
        ddt[rows, :] = near_right(xd, spread)
        pump(PUMP[2][i])
    last_heads = exact_right(jnp.broadcast_to(last_row, (8, 2 * inner)), spread, mm_nt)[0:1, :]
    place = iota((tok, 1), 0)
    at_end = ((place == tok - 1) & is_fwd) | ((place == 0) & jnp.logical_not(is_fwd))
    dc_all = dcc[...] + jnp.where(at_end, last_heads, 0.0)
    dsums = exact_left(tri, dc_all)
    dld = jnp.where(is_fwd, dsums[tok - 1 : tok, :] - dsums + dc_all, dsums)
    gdt = (ddt[...] + dld * rate_row) * jax.nn.sigmoid(dtr[...])
    gall[:, xo : off[1]] = gdt.astype(BF16)
    misc = slice(conv_w, conv_w + 128)
    sm[...] = jnp.zeros(sm.shape, F32)
    sm[0, 5:6, :inner] = acc_gain
    sm[0, 3:4, misc] = exact_right(
        jnp.broadcast_to(acc_skip, (8, inner)), spread[:, :inner], mm_nt
    )[0:1, :]
    sm[0, 1:2, misc] = jnp.sum(gdt, axis=0, keepdims=True)
    sm[0, 2:3, misc] = jnp.sum(dld * ld[...], axis=0, keepdims=True)

    onward1 = pass_grads(1, grads1)

    taps_of = jnp.concatenate([conv_bc[...], conv_x[...]], axis=1)
    conv_acc = [jnp.zeros((1, conv_w), F32) for _ in range(taps)]
    for i in range(nb):
        lo, hi = i * TB, (i + 1) * TB
        if i == nb - 1:
            edge.wait_recv()
        here = seg_col(lo, TB)
        x_rows = xp[16 + lo : 16 + hi, :]
        acc = jnp.zeros((TB, conv_w), F32)
        for d in range(taps):
            m = du[lo + d : hi + d, :]
            if d > 0:
                m = m * (seg_col(lo, TB, d) == here).astype(F32)
            acc = acc + m * taps_of[taps - 1 - d : taps - d, :]
            conv_acc[taps - 1 - d] = conv_acc[taps - 1 - d] + jnp.sum(m * x_rows, axis=0, keepdims=True)
        gall[lo:hi, :xo] = acc[:, :xo].astype(BF16)
        gall[lo:hi, off[1] : off[2]] = acc[:, xo:].astype(BF16)
        pump(PUMP[4][i])
    for k in range(taps):
        sm[0, 1 + k : 2 + k, :conv_w] = conv_acc[k]

    w_all = weights(0, gall_w)
    acc_norm = jnp.zeros((1, width), F32)
    for i in range(nb):
        rows = slice(i * TB, (i + 1) * TB)
        part = mm_nt(gall[rows, :], w_all)
        hb[rows, :] = part.astype(BF16)
        line_h.begin(range(i * TB // PR, (i + 1) * TB // PR))
        h = hid[rows, :].astype(F32)
        rr = lax.rsqrt(jnp.mean(h * h, axis=1, keepdims=True) + EPS)
        acc_norm = acc_norm + jnp.sum(part * (h * rr), axis=0, keepdims=True)
        pump(PUMP[5][i])
    sm[0, 0:1, :] = acc_norm

    def small_send(level, slot, sends):
        return [remote(sm.at[level], smbuf.at[slot + k], dev) for k, dev in enumerate(sends)]

    def small_sum(level, slot, copies):
        acc = sm[level]
        for k, copy in enumerate(copies):
            copy.wait_recv()
            acc = acc + smbuf[slot + k]
        return acc

    sm0 = small_send(0, 0, [cx(k) for k in range(1, nc)])

    for b in range(width // block):
        cols = slice(b * block, (b + 1) * block)
        got = mm_tn(nl[16:, cols], gall[:, : off[2]])
        store_grads(b, 0, off[2], got)
    grads0 = send_grads(0)
    pump(PUMP[6][0])
    sm[1] = small_sum(0, 0, sm0)
    sm1 = small_send(1, nc - 1, [fs(k) for k in range(1, nf)])
    pump(PUMP[6][1])
    onward0 = pass_grads(0, grads0)
    pump(PUMP[6][2])
    sm[2] = small_sum(1, nc - 1, sm1)
    parts = [sm[2, 0:1, k * 128 : (k + 1) * 128] for k in range(width // 128)]
    parts = parts + [sm[2, 1 : 1 + taps, :xo], jnp.zeros((16 - taps - width // 128, 128), F32)]
    tps[...] = jnp.concatenate(parts, axis=0)
    tp_copies = [remote(tps, tpbuf.at[k - 1], tx(k)) for k in range(1, nt)]
    pump(PUMP[6][3])
    got = finish_grads(1, onward1)
    gwz[...] = got[:, :inner]
    gwo[...] = got[:, inner:]
    keep(gwz, gwz_h)
    keep(gwo, gwo_h)
    pump(PUMP[6][4])
    got = finish_grads(0, onward0)
    gwx[...] = got[:, off[1] :]
    gwdt[...] = got[:, xo : off[1]]
    keep(gwx, gwx_h)
    keep(gwdt, gwdt_h)
    bcs[...] = got[:, :xo].astype(BF16)
    bc_copies = [remote(bcs, bcbuf.at[k - 1], tx(k)) for k in range(1, nt)]
    pump(PUMP[6][5])
    def tp_order(own, box, first):
        total = None
        for k in range(nt):
            part = jnp.where(t == k, own, 0.0)
            for j in range(1, nt):
                part = jnp.where(lax.rem(t + nt - j, nt) == k, box[first + j - 1].astype(F32), part)
            total = part if total is None else total + part
        return total

    for copy in tp_copies:
        copy.wait_recv()
    got = tp_order(tps[...], tpbuf, 0)
    small[...] = sm[2]
    for k in range(width // 128):
        small[0:1, k * 128 : (k + 1) * 128] = got[k : k + 1, :]
    small[1 : 1 + taps, :xo] = got[width // 128 : width // 128 + taps, :]
    keep(small, small_h)
    pump(PUMP[6][6])
    for copy in bc_copies:
        copy.wait_recv()
    gwbc[...] = tp_order(bcs[...].astype(F32), bcbuf, 0)
    keep(gwbc, gwbc_h)
    pump(len(todo))

    @pl.when(is_end)
    def _():
        for line in (line_o, line_h):
            for p in range(pieces):
                line.last(p)

    line_o.close()
    line_h.close()
    for p in range(pieces):
        rows = pl.ds(p * PR, PR)
        result(result_ids + p, out_v, out_h, rows).wait()
        result(result_ids + pieces + p, gh_v, gh_h, rows).wait()
    for copy in local_copies:
        copy.wait()
    for copy in pending:
        copy.wait_send()


def finish_kernel(dims, gdt_h, small_h, gh_h, out_h, gx_h, gz_h, gbc_h, go_h,
                  gh, out, o_x, o_z, o_bc, o_out, o_norm, o_dt, o_cx, o_cbc, o_bias, o_rate, o_skip, o_gain,
                  gh_s, out_s, x_s, z_s, bc_s, go_s, norm_s, dt_s, cx_s, cbc_s, bias_s, rate_s, skip_s, gain_s,
                  gdt, small, sems):
    hl, xo = dims
    count = [0]

    def move(src, dst):
        copy = pltpu.make_async_copy(src, dst, sems.at[count[0]])
        count[0] += 1
        copy.start()
        return copy

    first = [move(small_h, small), move(gdt_h, gdt)]
    moves = []
    for src, stage, dst, cuts in (
        (gh_h, gh_s, gh, 4), (out_h, out_s, out, 2), (gx_h, x_s, o_x, 1), (gz_h, z_s, o_z, 1),
        (go_h, go_s, o_out, 1), (gbc_h, bc_s, o_bc, 1),
    ):
        step = src.shape[0] // cuts
        for k in range(cuts):
            rows = pl.ds(k * step, step)
            moves.append((move(src.at[rows], stage.at[rows]), stage.at[rows], dst.at[rows]))
    rows_w, inner = gx_h.shape
    width = small.shape[1]
    conv_w = xo + inner
    for copy in first:
        copy.wait()
    norm_s[...] = small[0:1, :].reshape(width)
    flat = jnp.concatenate([gdt[...], jnp.zeros((128 - rows_w, 128), F32)], axis=0).T
    for k in range(hl):
        for d in range(2):
            dt_s[k, d : d + 1, :] = flat[d * hl + k : d * hl + k + 1, :rows_w]
    taps = cx_s.shape[0]
    cx_s[...] = small[1 : 1 + taps, xo:conv_w]
    cbc_s[...] = small[1 : 1 + taps, :xo]
    for row, ref in ((1, bias_s), (2, rate_s)):
        for d in range(2):
            ref[d : d + 1, :] = small[row : row + 1, conv_w + d * hl : conv_w + (d + 1) * hl]
    skip_s[...] = small[3:4, conv_w : conv_w + hl].reshape(hl)
    gain_s[...] = small[5:6, :inner].reshape(inner)
    leaving = [
        move(src, dst)
        for src, dst in (
            (norm_s, o_norm), (dt_s, o_dt), (cx_s, o_cx), (cbc_s, o_cbc), (bias_s, o_bias),
            (rate_s, o_rate), (skip_s, o_skip), (gain_s, o_gain),
        )
    ]
    for into, stage, dst in moves:
        into.wait()
        leaving.append(move(stage, dst))
    for copy in leaving:
        copy.wait()


def per_device(dims, hidden, seq_lengths, norm_gain, weight_x, weight_z, weight_bc, weight_dt,
               conv_x, conv_bc, dt_bias, log_rate, skip_scale, gate_gain, weight_out, cotangent):
    nf, nc, nt = dims
    tok, width = hidden.shape
    rows_w, inner = weight_x.shape
    hl = skip_scale.shape[0]
    shards = nf * nc
    xo = weight_bc.shape[1]
    state_n = xo // 2
    taps = conv_x.shape[0]
    conv_w = xo + inner
    p2 = xo + 128 + inner
    cw = p2 + 2 * inner
    pieces = tok // PR
    n_small = nf + nc - 2
    scratch = {
        "hid": ((tok, width), BF16),
        "cot": ((tok, width), BF16),
        "oag": ((tok, width), BF16),
        "hag": ((tok, width), BF16),
        "out_v": ((tok, width), BF16),
        "gh_v": ((tok, width), F32),
        "gwx": ((rows_w, inner), F32),
        "gwz": ((rows_w, inner), F32),
        "gwbc": ((rows_w, xo), F32),
        "gwdt": ((rows_w, 128), F32),
        "gwo": ((rows_w, inner), F32),
        "small": ((8, width), F32),
        "hbuf": ((16, width), BF16),
        "nl": ((tok + 16, width), BF16),
        "wbuf": ((shards, rows_w, cw), BF16),
        "xp": ((tok + 16, conv_w), F32),
        "dtr": ((tok, 128), F32),
        "u": ((tok, conv_w), F32),
        "low": ((tok, conv_w), BF16),
        "z": ((tok, inner), F32),
        "zd": ((tok, inner), F32),
        "ggate": ((tok, inner), BF16),
        "ld": ((tok, 128), F32),
        "cc": ((tok, 128), F32),
        "cct": ((128, tok), F32),
        "dte": ((tok, 2 * inner), BF16),
        "rea": ((tok, 2 * inner), BF16),
        "tol": ((tok, 2 * inner), BF16),
        "w16": ((tok, 2 * inner), BF16),
        "q16": ((tok, 2 * inner), BF16),
        "gm": ((tok, tok), F32),
        "gmt": ((tok, tok), F32),
        "pexp": ((hl, tok, tok), BF16),
        "yfr": ((tok, 2 * inner), F32),
        "s16": ((state_n, 2 * inner), BF16),
        "sbuf": ((nc - 1, state_n, inner), BF16),
        "dec": ((1, 128), F32),
        "decbuf": ((nc - 1, 1, 128), F32),
        "into16": ((state_n, 2 * inner), BF16),
        "gated": ((tok, inner), F32),
        "mixed": ((tok, inner), F32),
        "dmix": ((tok, inner), F32),
        "dy": ((tok, inner), BF16),
        "st": ((2, 1, tok), F32),
        "stbuf": ((2, nt - 1, 1, tok), F32),
        "gall": ((tok, p2 + inner), BF16),
        "glow": ((tok, inner), BF16),
        "ob": ((tok, width), BF16),
        "oin": ((pieces, PR, width), BF16),
        "oex": ((pieces, PR, width), BF16),
        "hb": ((tok, width), BF16),
        "hin": ((pieces, PR, width), BF16),
        "hex": ((pieces, PR, width), BF16),
        "rdy": ((tok, 2 * inner), BF16),
        "d16": ((state_n, 2 * inner), BF16),
        "dbuf": ((nc - 1, state_n, inner), BF16),
        "back16": ((state_n, 2 * inner), BF16),
        "dg": ((tok, tok), BF16),
        "dw": ((tok, 2 * inner), F32),
        "dcc": ((tok, 128), F32),
        "ddt": ((tok, 128), F32),
        "du": ((tok + 8, conv_w), F32),
        "gw16": ((shards, rows_w, cw), BF16),
        "fbuf": ((nf - 1, nc, rows_w, cw), BF16),
        "hsend": ((nc, rows_w, cw), BF16),
        "cbuf": ((nc - 1, rows_w, cw), BF16),
        "bcs": ((rows_w, xo), BF16),
        "bcbuf": ((nt - 1, rows_w, xo), BF16),
        "sm": ((3, 8, width), F32),
        "smbuf": ((n_small, 8, width), F32),
        "tps": ((16, 128), F32),
        "tpbuf": ((nt - 1, 16, 128), F32),
    }
    n_sems = 2 + 4 * (nc + nf - 2 + (nc - 1) * (nf - 1)) + 3 * (nc - 1) + 3 * (nt - 1)
    n_sems += 2 * (nf - 1 + nc - 1) + n_small + 6 * pieces + nt - 1
    vmem = pl.BlockSpec(memory_space=pltpu.VMEM)
    smem = pl.BlockSpec(memory_space=pltpu.SMEM)
    f32 = lambda *shape: jax.ShapeDtypeStruct(shape, F32)
    bf16 = lambda *shape: jax.ShapeDtypeStruct(shape, BF16)
    anywhere = pl.BlockSpec(memory_space=pl.ANY)
    results = pl.pallas_call(
        partial(mixer_kernel, (nf, nc, nt, hl)),
        out_shape=(
            bf16(tok, width), f32(tok, width), f32(rows_w, inner), f32(rows_w, inner),
            f32(rows_w, xo), f32(rows_w, 128), f32(rows_w, inner), f32(8, width),
        ),
        in_specs=[smem] + [vmem] * 4 + [smem] * 3 + [vmem] + [anywhere] * 6,
        out_specs=[anywhere] * 8,
        scratch_shapes=[pltpu.VMEM(s, d) for s, d in scratch.values()]
        + [pltpu.SemaphoreType.DMA((n_sems,)), pltpu.SemaphoreType.DMA((n_sems,))]
        + [pltpu.SemaphoreType.DMA((12 + 2 * pieces,))],
        compiler_params=pltpu.CompilerParams(
            collective_id=0, has_side_effects=True, vmem_limit_bytes=62 << 20
        ),
    )(
        seq_lengths, norm_gain, jnp.transpose(weight_dt, (2, 1, 0)), conv_x, conv_bc, dt_bias, log_rate,
        skip_scale, gate_gain, hidden, cotangent, weight_x, weight_z, weight_bc, weight_out.T,
    )
    out, gh, gx, gz, gbc, gdt, go, small = results
    finals = (
        f32(tok, width), bf16(tok, width), f32(rows_w, inner), f32(rows_w, inner), f32(rows_w, xo),
        f32(rows_w, inner), f32(width), f32(hl, 2, rows_w), f32(taps, inner), f32(taps, xo),
        f32(2, hl), f32(2, hl), f32(hl), f32(inner),
    )
    gh, out, gx, gz, gbc, go, norm, gdt, cx, cbc, bias, rate, skip, gate = pl.pallas_call(
        partial(finish_kernel, (hl, xo)),
        out_shape=finals,
        in_specs=[anywhere] * 8,
        out_specs=[anywhere] * 14,
        scratch_shapes=[pltpu.VMEM(a.shape, a.dtype) for a in finals]
        + [pltpu.VMEM((rows_w, 128), F32), pltpu.VMEM((8, width), F32), pltpu.SemaphoreType.DMA((32,))],
        compiler_params=pltpu.CompilerParams(vmem_limit_bytes=62 << 20),
    )(gdt, small, gh, out, gx, gz, gbc, go)
    return (
        out, gh, norm, gx, gz, gbc, jnp.transpose(gdt, (2, 1, 0)), cx, cbc, bias, rate, skip, gate, go.T
    )


def solution(mesh):
    dims = tuple(mesh.shape[a] for a in ("fsdp", "ctx", "tp"))
    both = ("fsdp", "ctx")
    return jax.shard_map(
        partial(per_device, dims),
        mesh=mesh,
        in_specs=(
            P(both, None), P("fsdp", None), P(), P(both, "tp"), P(both, "tp"), P(both, None),
            P(both, None, "tp"), P(None, "tp"), P(), P(None, "tp"), P(None, "tp"), P("tp"),
            P("tp"), P("tp", both), P(both, None),
        ),
        out_specs=(
            P(both, None), P(both, None), P(), P(both, "tp"), P(both, "tp"), P(both, None),
            P(both, None, "tp"), P(None, "tp"), P(), P(None, "tp"), P(None, "tp"), P("tp"),
            P("tp"), P("tp", both),
        ),
        check_vma=False,
    )
```

```python
from functools import partial

import jax
import jax.numpy as jnp
from jax import lax
from jax.experimental import pallas as pl
from jax.experimental.pallas import tpu as pltpu
from jax.sharding import PartitionSpec as P

MESH = pl.DeviceIdType.MESH
F32 = jnp.float32
BF16 = jnp.bfloat16
EPS = 1e-05
TB = 128
PR = 64
LAG = 2
PUMP = (
    (0, 1, 1, 1), (1, 0, 1, 1), (1, 1, 1, 1), (0, 0, 0, 0), (1, 1, 1, 1), (1, 1, 1, 1), (2, 2, 3, 4, 0, 4, 0)
)


def mm(left, right):
    return lax.dot_general(left, right, (((1,), (0,)), ((), ())), preferred_element_type=F32)


def mm_nt(left, right):
    return lax.dot_general(left, right, (((1,), (1,)), ((), ())), preferred_element_type=F32)


def mm_tn(left, right):
    return lax.dot_general(left, right, (((0,), (0,)), ((), ())), preferred_element_type=F32)


def split3(value):
    high = value.astype(BF16)
    rest = value - high.astype(F32)
    middle = rest.astype(BF16)
    low = (rest - middle.astype(F32)).astype(BF16)
    return high, middle, low


def exact_left(ones, value, dot=mm):
    a, b, c = split3(value)
    return dot(ones, a) + dot(ones, b) + dot(ones, c)


def exact_right(value, ones, dot=mm):
    a, b, c = split3(value)
    return dot(a, ones) + dot(b, ones) + dot(c, ones)


def iota(shape, dim):
    return lax.broadcasted_iota(jnp.int32, shape, dim)


def near_right(value, ones):
    high = value.astype(BF16)
    low = (value - high.astype(F32)).astype(BF16)
    return mm_nt(high, ones) + mm_nt(low, ones)


def mixer_kernel(dims, *refs):
    (lens, gain, wdt, conv_x, conv_bc, dtb, rate, skip, ggain, hid_h, cot_h, wx_h, wz_h, wbc_h, wot_h,
     out_h, gh_h, gwx_h, gwz_h, gwbc_h, gwdt_h, gwo_h, small_h,
     hid, cot, oag, hag, out_v, gh_v, gwx, gwz, gwbc, gwdt, gwo, small, hbuf, nl, wbuf, xp, dtr, u, low, z, zd, ggate, ld, cc, cct, dte,
     rea, tol, w16, q16, gm, gmt, pexp, yfr, s16, sbuf, dec, decbuf, into16, gated, mixed, dmix, dy,
     st, stbuf, gall, glow, r_cols, ob, oin, oex, hb, hin, hex_, rdy, d16, dbuf, back16, dg, dw, dcc, ddt,
     du, gw16, fbuf, hsend, cbuf, bcs, bcbuf, sm, smbuf, tps, tpbuf, ssem, rsem, lsem) = refs
    nf, nc, nt, hl = dims
    tok, width = hid.shape
    rows_w, inner = wx_h.shape
    pdim = inner // hl
    state_n = wbc_h.shape[1] // 2
    xo = 2 * state_n
    conv_w = xo + inner
    off = (0, xo + 128, xo + 128 + inner, xo + 128 + 2 * inner, xo + 128 + 3 * inner)
    gall_w = off[3]
    nb = tok // TB
    taps = conv_x.shape[0]
    f, c, t = lax.axis_index("fsdp"), lax.axis_index("ctx"), lax.axis_index("tp")
    base = c * tok
    counter = [0]
    pending = []

    def take(count):
        counter[0] += count
        return counter[0] - count

    def describe(i, src, dst, dev):
        return pltpu.make_async_remote_copy(
            src_ref=src, dst_ref=dst, send_sem=ssem.at[i], recv_sem=rsem.at[i],
            device_id=dev, device_id_type=MESH,
        )

    def remote(src, dst, dev):
        copy = describe(take(1), src, dst, dev)
        copy.start()
        pending.append(copy)
        return copy

    def fs(k):
        return (lax.rem(f + k, nf), c, t)

    def cx(k):
        return (f, lax.rem(c + k, nc), t)

    def tx(k):
        return (f, c, lax.rem(t + k, nt))

    barrier = pltpu.get_barrier_semaphore()
    peers = [fs(k) for k in range(1, nf)] + [cx(k) for k in range(1, nc)] + [tx(k) for k in range(1, nt)]
    for dev in peers:
        pl.semaphore_signal(barrier, inc=1, device_id=dev, device_id_type=MESH)

    local_count = [0]
    local_copies = []

    def bring(src, dst):
        i = local_count[0]
        local_count[0] += 1
        copy = pltpu.make_async_copy(src, dst, lsem.at[i])
        copy.start()
        return copy

    def keep(src, dst):
        local_copies.append(bring(src, dst))

    me = f * nc + c
    get_hid = bring(hid_h, hid)
    shard_copies = []
    for p, src in ((0, wbc_h), (1, wx_h), (2, wz_h), (3, wot_h)):
        width_p = xo if p == 0 else inner
        shard_copies.append(bring(src, wbuf.at[me, :, pl.ds(off[p], width_p)]))
    get_cot = bring(cot_h, cot)
    flat = jnp.concatenate(
        [wdt[h].astype(F32) for h in range(hl)] + [jnp.zeros((16 - 2 * hl, rows_w), F32)], axis=0
    ).astype(BF16)
    lane_of = lax.rem(iota((16, 128), 0), 2) * hl + lax.div(iota((16, 128), 0), 2)
    turn = (iota((16, 128), 1) == lane_of).astype(F32).astype(BF16)
    wbuf[me, :, xo : off[1]] = mm_tn(flat, turn).astype(BF16)

    lane = iota((1, 128), 1)
    is_fwd = lane < hl
    bias_row = jnp.zeros((1, 128), F32)
    log_row = jnp.zeros((1, 128), F32)
    for d in range(2):
        for h in range(hl):
            bias_row = jnp.where(lane == d * hl + h, dtb[d, h], bias_row)
            log_row = jnp.where(lane == d * hl + h, rate[d, h], log_row)
    rate_row = -jnp.exp(log_row)
    head_of = lax.div(iota((1, inner), 1), pdim)
    skip_row = jnp.zeros((1, inner), F32)
    for h in range(hl):
        skip_row = jnp.where(head_of == h, skip[h], skip_row)
    gain_row = gain[...].reshape(1, width)
    gain_gate = ggain[...].reshape(1, inner)

    def norm_low(rows):
        h = rows.astype(F32)
        r = lax.rsqrt(jnp.mean(h * h, axis=1, keepdims=True) + EPS)
        return (h * r * gain_row).astype(BF16)

    get_hid.wait()

    @pl.loop(0, nb)
    def _(i):
        at = pl.multiple_of(i * TB, TB)
        nl[pl.ds(16 + at, TB), :] = norm_low(hid[pl.ds(at, TB), :])

    for copy in shard_copies:
        copy.wait()
    pl.semaphore_wait(barrier, len(peers))

    col_parts = [pl.ds(off[p], off[p + 1] - off[p]) for p in range(4)]
    rim = remote(hid.at[pl.ds(tok - 16, 16)], hbuf, cx(1))
    ctx_copies = []
    fwd_copies = []

    def send_weights(part):
        own = wbuf.at[me, :, col_parts[part]]
        ctx_copies.append([remote(own, own, cx(k)) for k in range(1, nc)])
        fwd_copies.append([remote(own, own, fs(k)) for k in range(1, nf)])

    for part in range(4):
        send_weights(part)

    def pass_weights(part):
        for k in range(1, nc):
            ctx_copies[part][k - 1].wait_recv()
            src = wbuf.at[f * nc + lax.rem(c + nc - k, nc), :, col_parts[part]]
            for j in range(1, nf):
                fwd_copies[part].append(remote(src, src, fs(j)))

    def get_weights(part):
        for copy in fwd_copies[part]:
            copy.wait_recv()

    def weights(lo, hi):
        if rows_w % 16 == 0:
            return wbuf[:, :, lo:hi].reshape(width, hi - lo)
        return wbuf[:, :, lo:hi].astype(F32).reshape(width, hi - lo).astype(BF16)

    ends = []
    total = lens[0, 0]
    ends.append(total)
    for k in range(1, lens.shape[1]):
        total = total + lens[0, k]
        ends.append(total)

    def seg_of(pos):
        seg = jnp.where(pos < 0, -1, 0)
        for e in ends:
            seg = seg + jnp.where(pos >= e, 1, 0)
        return seg

    one_pos = jnp.full((1, 1), 0, jnp.int32)
    seg_before = seg_of(one_pos + (base - 1))
    seg_first = seg_of(one_pos + base)
    seg_last = seg_of(one_pos + (base + tok - 1))
    seg_after = seg_of(one_pos + (base + tok))
    seg_row = seg_of(iota((1, tok), 1) + base)
    place_row = iota((1, tok), 1)

    def seg_col(start, count, shift=0):
        return seg_of(iota((count, 1), 0) + (base + start + shift))

    spread = (
        iota((128, 2 * inner), 0) == lax.div(iota((128, 2 * inner), 1), pdim)
    ).astype(F32).astype(BF16)
    tri = (iota((tok, tok), 0) >= iota((tok, tok), 1)).astype(F32).astype(BF16)
    seg_all = seg_col(0, tok)

    rim.wait_recv()
    nl[0:16, :] = norm_low(hbuf[...])
    pass_weights(0)
    get_weights(0)

    w_part = weights(off[0], off[1])
    xp[0:16, :xo] = mm(nl[0:16, :], w_part)[:, :xo]
    for i in range(tok // 256):
        got = mm(nl[16 + i * 256 : 16 + (i + 1) * 256, :], w_part)
        xp[16 + i * 256 : 16 + (i + 1) * 256, :xo] = got[:, :xo]
        dtr[i * 256 : (i + 1) * 256, :] = got[:, xo:] + bias_row

    def conv_forward(cols, taps_ref):
        for i in range(nb):
            lo = i * TB
            here = seg_col(lo, TB)
            acc = xp[16 + lo : 16 + lo + TB, cols] * taps_ref[taps - 1 : taps, :]
            for d in range(1, taps):
                match = (seg_col(lo, TB, -d) == here).astype(F32)
                acc = acc + xp[16 + lo - d : 16 + lo - d + TB, cols] * taps_ref[taps - 1 - d : taps - d, :] * match
            sg = jax.nn.sigmoid(acc)
            u[lo : lo + TB, cols] = sg * (1.0 + acc * (1.0 - sg))
            low[lo : lo + TB, cols] = (acc * sg).astype(BF16)

    bc_cols, x_cols = slice(0, xo), slice(xo, conv_w)
    conv_forward(bc_cols, conv_bc)
    raw = dtr[...]
    step = jnp.maximum(raw, 0.0) + jnp.log1p(jnp.exp(-jnp.abs(raw)))
    decay = step * rate_row
    ld[...] = decay
    sums = exact_left(tri, decay)
    tot = sums[tok - 1 : tok, :]
    cum = jnp.where(is_fwd, sums, tot - sums + decay)
    cc[...] = cum
    cct[...] = cum.T
    dec_mask = jnp.where(
        is_fwd,
        (seg_last == seg_before).astype(F32),
        (seg_first == seg_after).astype(F32),
    )
    dec[...] = jnp.exp(tot) * dec_mask
    dec_copies = [remote(dec, decbuf.at[k - 1], cx(k)) for k in range(1, nc)]
    reach = jnp.exp(cum) * jnp.where(
        is_fwd, (seg_all == seg_before).astype(F32), (seg_all == seg_after).astype(F32)
    )
    to_end = jnp.exp(tot - cum) * jnp.where(
        is_fwd, (seg_all == seg_last).astype(F32), (seg_all == seg_first).astype(F32)
    )
    dte[...] = mm(step.astype(BF16), spread).astype(BF16)
    tol[...] = mm(to_end.astype(BF16), spread).astype(BF16)
    pass_weights(1)
    rea[...] = mm(reach.astype(BF16), spread).astype(BF16)

    b16 = low[:, 0:state_n]
    c16 = low[:, state_n:xo]

    def mix_mask(i):
        same = seg_col(i * TB, TB) == seg_row
        return same & (iota((TB, 1), 0) + i * TB != place_row)

    for i in range(nb):
        lo, hi = i * TB, (i + 1) * TB
        mask = mix_mask(i)
        gm[lo:hi, :] = jnp.where(mask, mm_nt(c16[lo:hi], b16), 0.0)
        gmt[lo:hi, :] = jnp.where(mask, mm_nt(b16[lo:hi], c16), 0.0)

    get_weights(1)
    w_part = weights(off[1], off[2])
    xp[0:16, xo:] = mm(nl[0:16, :], w_part)
    for i in range(tok // 256):
        xp[16 + i * 256 : 16 + (i + 1) * 256, xo:] = mm(nl[16 + i * 256 : 16 + (i + 1) * 256, :], w_part)
    conv_forward(x_cols, conv_x)

    @pl.loop(0, nb)
    def _(i):
        rows = pl.ds(pl.multiple_of(i * TB, TB), TB)
        x = low[rows, xo:].astype(F32)
        w = (jnp.concatenate([x, x], axis=1) * dte[rows, :].astype(F32)).astype(BF16)
        w16[rows, :] = w
        q16[rows, :] = (w.astype(F32) * tol[rows, :].astype(F32)).astype(BF16)

    s16[...] = mm_tn(b16, q16[...]).astype(BF16)

    def half_of(forward):
        return pl.ds(pl.multiple_of(jnp.where(forward, 0, inner), 128), inner)

    state_copies = []
    for k in range(1, nc):
        forward = lax.rem(c + k, nc) > c
        state_copies.append(remote(s16.at[:, half_of(forward)], sbuf.at[k - 1], cx(k)))

    local = iota((TB, TB), 0)
    below = local > iota((TB, TB), 1)
    above = local < iota((TB, TB), 1)
    pair_left = iota((1, 128), 1) < pdim

    def pair_cols(pair):
        return (
            slice(pair * 128, (pair + 1) * 128),
            slice(inner + pair * 128, inner + (pair + 1) * 128),
        )

    def beside(parts):
        return jnp.concatenate(parts, axis=1) if len(parts) > 1 else parts[0]

    for i in range(nb):
        lo, hi = i * TB, (i + 1) * TB
        if i == 2:
            pass_weights(2)
        g_diag = gm[lo:hi, lo:hi]
        g_low = jnp.where(below, g_diag, 0.0)
        g_up = jnp.where(above, g_diag, 0.0)
        for pair in range(hl // 2):
            cols, cols_r = pair_cols(pair)
            ys = []
            for h in (2 * pair, 2 * pair + 1):
                fc = cc[lo:hi, h : h + 1]
                rc = cc[lo:hi, hl + h : hl + h + 1]
                fr = cct[h : h + 1, :]
                rr = cct[hl + h : hl + h + 1, :]
                p = jnp.exp(jnp.minimum(fc - fr[:, lo:hi], rc - rr[:, lo:hi]))
                pexp[h, lo:hi, lo:hi] = p.astype(BF16)
                lows = [(g_low * p).astype(BF16)]
                ups = [(g_up * p).astype(BF16)]
                if i > 0:
                    p = jnp.exp(fc - fr[:, :lo])
                    pexp[h, lo:hi, :lo] = p.astype(BF16)
                    lows.insert(0, (gm[lo:hi, :lo] * p).astype(BF16))
                if i < nb - 1:
                    p = jnp.exp(rc - rr[:, hi:])
                    pexp[h, lo:hi, hi:] = p.astype(BF16)
                    ups.append((gm[lo:hi, hi:] * p).astype(BF16))
                ys.append((mm(beside(lows), w16[:hi, cols]), mm(beside(ups), w16[lo:, cols_r])))
            yfr[lo:hi, cols] = jnp.where(pair_left, ys[0][0], ys[1][0])
            yfr[lo:hi, cols_r] = jnp.where(pair_left, ys[0][1], ys[1][1])

    get_weights(2)
    w_part = weights(off[2], off[3])
    for i in range(tok // 256):
        zz = mm(nl[16 + i * 256 : 16 + (i + 1) * 256, :], w_part)
        sg = jax.nn.sigmoid(zz)
        z[i * 256 : (i + 1) * 256, :] = zz * sg
        zd[i * 256 : (i + 1) * 256, :] = sg * (1.0 + zz * (1.0 - sg))

    pass_weights(3)
    get_weights(3)
    get_cot.wait()
    wo = weights(off[3], off[4])
    for i in range(tok // 256):
        rows = slice(i * 256, (i + 1) * 256)
        ggate[rows, :] = mm(cot[rows, :], wo).astype(BF16)

    dec_spread = []
    for k in range(1, nc):
        dec_copies[k - 1].wait_recv()
        dec_spread.append(exact_right(jnp.broadcast_to(decbuf[k - 1], (8, 128)), spread)[0:1, :])
    for copy in state_copies:
        copy.wait_recv()
    acc_f = jnp.zeros((state_n, inner), F32)
    acc_r = jnp.zeros((state_n, inner), F32)
    for k in range(nc - 1, 0, -1):
        new = dec_spread[k - 1][:, :inner] * acc_f + sbuf[k - 1].astype(F32)
        acc_f = jnp.where(k <= c, new, acc_f)
    for k in range(1, nc):
        new = dec_spread[k - 1][:, inner:] * acc_r + sbuf[k - 1].astype(F32)
        acc_r = jnp.where(k > c, new, acc_r)
    into16[:, :inner] = acc_f.astype(BF16)
    into16[:, inner:] = acc_r.astype(BF16)

    ones8 = jnp.ones((8, inner), BF16)
    for i in range(nb):
        rows = slice(i * TB, (i + 1) * TB)
        carried = mm(low[rows, state_n:xo], into16[...]) * rea[rows, :].astype(F32)
        y = yfr[rows, :] + carried
        yfr[rows, :] = y
        mix = y[:, :inner] + y[:, inner:] + skip_row * low[rows, xo:].astype(F32)
        mixed[rows, :] = mix
        gt = mix * z[rows, :]
        gated[rows, :] = gt
        st[0:1, rows] = mm_nt(ones8, (gt * gt).astype(BF16))[0:1]
        gl = gt * gain_gate
        glow[rows, :] = gl.astype(BF16)
        st[1:2, rows] = mm_nt(ones8, (ggate[rows, :].astype(F32) * gl).astype(BF16))[0:1]
    st_copies = [remote(st, stbuf.at[k - 1], tx(k)) for k in range(1, nt)]
    total_inner = inner * nt
    pick = (iota((8, 128), 0) == 0).astype(F32).astype(BF16)

    is_mid = (t > 0) & (t < nt - 1)
    is_end = (t == 0) | (t == nt - 1)
    inside = (f, c, 1 + lax.div(t, nt - 1))
    across = (f, c, nt - 1 - t)
    outside = (f, c, (t - 1) * (nt - 1))
    pieces = tok // PR

    def piece(ref, p):
        return ref.at[pl.ds(p * PR, PR)]

    class Line:
        def __init__(self, own, inbox, exchange, sums, done):
            self.own, self.inbox, self.exchange, self.sums = own, inbox, exchange, sums
            self.done = done
            self.ids = take(3 * pieces)

        def up(self, p):
            return describe(self.ids + p, piece(self.own, p), self.inbox.at[p], inside)

        def over(self, p):
            return describe(self.ids + pieces + p, piece(self.own, p), self.exchange.at[p], across)

        def down(self, p):
            return describe(self.ids + 2 * pieces + p, piece(self.sums, p), piece(self.sums, p), outside)

        def first(self, p):
            self.up(p).wait_recv()
            rows = slice(p * PR, (p + 1) * PR)
            both = self.own[rows, :].astype(F32) + self.inbox[p].astype(F32)
            self.own[rows, :] = both.astype(BF16)
            self.over(p).start()

        def second(self, p):
            self.over(p).wait_recv()
            rows = slice(p * PR, (p + 1) * PR)
            both = (self.own[rows, :].astype(F32) + self.exchange[p].astype(F32)).astype(BF16)
            self.sums[rows, :] = both
            self.down(p).start()
            self.done(p, rows, both)

        def last(self, p):
            self.down(p).wait_recv()
            rows = slice(p * PR, (p + 1) * PR)
            self.done(p, rows, self.sums[rows, :])

        def begin(self, p_list):
            @pl.when(is_end)
            def _():
                for p in p_list:
                    self.up(p).start()

        def close(self):
            @pl.when(is_end)
            def _():
                for p in range(pieces):
                    self.up(p).wait_send()

            @pl.when(is_mid)
            def _():
                for p in range(pieces):
                    self.over(p).wait_send()
                    self.down(p).wait_send()

    def result(i, src, dst, rows):
        return pltpu.make_async_copy(src.at[rows], dst.at[rows], lsem.at[i])

    result_ids = local_count[0]
    local_count[0] += 2 * pieces

    def out_done(p, rows, both):
        out_v[rows, :] = (hid[rows, :].astype(F32) + both.astype(F32) * r_cols[rows, 0:1]).astype(BF16)
        result(result_ids + p, out_v, out_h, pl.ds(p * PR, PR)).start()

    def head_done(p, rows, both):
        h = hid[rows, :].astype(F32)
        rr = lax.rsqrt(jnp.mean(h * h, axis=1, keepdims=True) + EPS)
        q = both.astype(F32) * gain_row
        inner_mean = jnp.mean(q * h, axis=1, keepdims=True)
        gh_v[rows, :] = cot[rows, :].astype(F32) + rr * (q - h * (rr * rr * inner_mean))
        result(result_ids + pieces + p, gh_v, gh_h, pl.ds(p * PR, PR)).start()

    line_o = Line(ob, oin, oex, oag, out_done)
    line_h = Line(hb, hin, hex_, hag, head_done)
    todo = []
    for p in range(2 * pieces + LAG):
        for q, stage in ((p, 0), (p - LAG, 1)):
            if 0 <= q < 2 * pieces:
                line = line_o if q < pieces else line_h
                todo.append(partial(line.first if stage == 0 else line.second, q % pieces))

    def pump(count):
        now = [todo.pop(0) for _ in range(min(count, len(todo)))]
        if now:
            @pl.when(is_mid)
            def _():
                for action in now:
                    action()

    for i in range(nb):
        rows = slice(i * TB, (i + 1) * TB)
        ob[rows, :] = mm_nt(glow[rows, :], wo).astype(BF16)
        line_o.begin(range(i * TB // PR, (i + 1) * TB // PR))

    def tp_order(own, box):
        total = None
        for k in range(nt):
            part = jnp.where(t == k, own, 0.0)
            for j in range(1, nt):
                part = jnp.where(lax.rem(t + nt - j, nt) == k, box[j - 1].astype(F32), part)
            total = part if total is None else total + part
        return total

    for copy in st_copies:
        copy.wait_recv()
    both = tp_order(st[...], stbuf)
    r_row = lax.rsqrt(both[0:1, :] * (1.0 / total_inner) + EPS)
    q_row = r_row * r_row * r_row * both[1:2, :] * (-1.0 / total_inner)
    r_cols[...] = exact_right(jnp.broadcast_to(r_row, (8, tok)), pick, mm_tn)
    q_cols = exact_right(jnp.broadcast_to(q_row, (8, tok)), pick, mm_tn)

    block = 384
    per = block // rows_w

    def store_grads(b, lo, hi, value):
        for s in range(per):
            gw16[b * per + s, :, lo:hi] = value[s * rows_w : (s + 1) * rows_w].astype(BF16)

    acc_gain = jnp.zeros((1, inner), F32)
    acc_skip = jnp.zeros((1, inner), F32)
    for i in range(nb):
        rows = slice(i * TB, (i + 1) * TB)
        r = r_cols[rows, 0:1]
        gt = gated[rows, :]
        gg = ggate[rows, :].astype(F32)
        ghat = gt * r
        glow[rows, :] = (ghat * gain_gate).astype(BF16)
        acc_gain = acc_gain + jnp.sum(gg * ghat, axis=0, keepdims=True)
        ggated = gg * gain_gate * r + gt * q_cols[rows, 0:1]
        dm = ggated * z[rows, :]
        gall[rows, off[2] :] = (ggated * mixed[rows, :] * zd[rows, :]).astype(BF16)
        dmix[rows, :] = dm
        acc_skip = acc_skip + jnp.sum(dm * low[rows, xo:].astype(F32), axis=0, keepdims=True)
        d = dm.astype(BF16)
        dy[rows, :] = d
        rdy[rows, :] = (jnp.concatenate([d, d], axis=1).astype(F32) * rea[rows, :].astype(F32)).astype(BF16)

    d16[...] = mm_tn(low[:, state_n:xo], rdy[...]).astype(BF16)
    back_copies = []
    for k in range(1, nc):
        forward = lax.rem(c + k, nc) < c
        back_copies.append(remote(d16.at[:, half_of(forward)], dbuf.at[k - 1], cx(k)))

    col_sets = ((0, off[2]), (off[2], off[4]))

    def send_grads(part):
        lo, hi = col_sets[part]
        copies = []
        for k in range(1, nf):
            to = pl.ds(lax.rem(f + k, nf) * nc, nc)
            copies.append(
                remote(gw16.at[to, :, pl.ds(lo, hi - lo)], fbuf.at[k - 1, :, :, pl.ds(lo, hi - lo)], fs(k))
            )
        return copies

    def pass_grads(part, copies):
        lo, hi = col_sets[part]
        for copy in copies:
            copy.wait_recv()
        onward = []
        for k in list(range(1, nc)) + [0]:
            to = lax.rem(c + k, nc)
            acc = gw16[f * nc + to, :, lo:hi].astype(F32)
            for j in range(1, nf):
                acc = acc + fbuf[j - 1, to, :, lo:hi].astype(F32)
            hsend[k, :, lo:hi] = acc.astype(BF16)
            if k > 0:
                onward.append(
                    remote(hsend.at[k, :, pl.ds(lo, hi - lo)], cbuf.at[k - 1, :, pl.ds(lo, hi - lo)], cx(k))
                )
        return onward

    def finish_grads(part, onward):
        lo, hi = col_sets[part]
        for copy in onward:
            copy.wait_recv()
        acc = hsend[0, :, lo:hi].astype(F32)
        for k in range(1, nc):
            acc = acc + cbuf[k - 1, :, lo:hi].astype(F32)
        return acc

    for b in range(width // block):
        cols = slice(b * block, (b + 1) * block)
        store_grads(b, off[2], off[3], mm_tn(nl[16:, cols], gall[:, off[2] :]))
        store_grads(b, off[3], off[4], mm_tn(cot[:, cols], glow[...]))
    grads1 = send_grads(1)

    for i in range(nb):
        lo, hi = i * TB, (i + 1) * TB
        g_diag = gmt[lo:hi, lo:hi]
        g_low = jnp.where(below, g_diag, 0.0)
        g_up = jnp.where(above, g_diag, 0.0)
        for pair in range(hl // 2):
            cols, cols_r = pair_cols(pair)
            ds = []
            for h in (2 * pair, 2 * pair + 1):
                fc = cc[lo:hi, h : h + 1]
                rc = cc[lo:hi, hl + h : hl + h + 1]
                fr = cct[h : h + 1, :]
                rr = cct[hl + h : hl + h + 1, :]
                p = jnp.exp(jnp.minimum(fr[:, lo:hi] - fc, rr[:, lo:hi] - rc))
                ups = [(g_up * p).astype(BF16)]
                lows = [(g_low * p).astype(BF16)]
                if i < nb - 1:
                    p = jnp.exp(fr[:, hi:] - fc)
                    ups.append((gmt[lo:hi, hi:] * p).astype(BF16))
                if i > 0:
                    p = jnp.exp(rr[:, :lo] - rc)
                    lows.insert(0, (gmt[lo:hi, :lo] * p).astype(BF16))
                ds.append((mm(beside(ups), dy[lo:, cols]), mm(beside(lows), dy[:hi, cols])))
            dw[lo:hi, cols] = jnp.where(pair_left, ds[0][0], ds[1][0])
            dw[lo:hi, cols_r] = jnp.where(pair_left, ds[0][1], ds[1][1])
        pump(PUMP[0][i])

    for i in range(nb):
        lo, hi = i * TB, (i + 1) * TB
        acc_low = jnp.zeros((TB, lo), F32) if i > 0 else None
        acc_up = jnp.zeros((TB, tok - hi), F32) if i < nb - 1 else None
        acc_diag = jnp.zeros((TB, TB), F32)
        for h in range(hl):
            cols, cols_r = pair_cols(h // 2)
            mine = pair_left if h % 2 == 0 else jnp.logical_not(pair_left)
            d = jnp.where(mine, dy[lo:hi, cols].astype(F32), 0.0).astype(BF16)
            wf = mm_nt(d, w16[:hi, cols])
            wr = mm_nt(d, w16[lo:, cols_r])
            acc_diag = acc_diag + jnp.where(below, wf[:, lo:], wr[:, :TB]) * pexp[h, lo:hi, lo:hi].astype(F32)
            if i > 0:
                acc_low = acc_low + wf[:, :lo] * pexp[h, lo:hi, :lo].astype(F32)
            if i < nb - 1:
                acc_up = acc_up + wr[:, TB:] * pexp[h, lo:hi, hi:].astype(F32)
        parts = ([acc_low] if i > 0 else []) + [acc_diag] + ([acc_up] if i < nb - 1 else [])
        dg[lo:hi, :] = jnp.where(mix_mask(i), beside(parts), 0.0).astype(BF16)
        pump(PUMP[1][i])

    for copy in back_copies:
        copy.wait_recv()
    acc_f = jnp.zeros((state_n, inner), F32)
    acc_r = jnp.zeros((state_n, inner), F32)
    for k in range(1, nc):
        new = dec_spread[k - 1][:, :inner] * acc_f + dbuf[k - 1].astype(F32)
        acc_f = jnp.where(k > c, new, acc_f)
    for k in range(nc - 1, 0, -1):
        new = dec_spread[k - 1][:, inner:] * acc_r + dbuf[k - 1].astype(F32)
        acc_r = jnp.where(k <= c, new, acc_r)
    back16[:, :inner] = acc_f.astype(BF16)
    back16[:, inner:] = acc_r.astype(BF16)
    dec_own = exact_right(jnp.broadcast_to(dec[...], (8, 128)), spread)[0:1, :]
    last_row = dec_own * jnp.sum(
        back16[...].astype(F32) * into16[...].astype(F32), axis=0, keepdims=True
    )

    db = mm_tn(dg[...], c16) + mm_nt(q16[...], back16[...])
    dc = mm(dg[...], b16) + mm_nt(rdy[...], into16[...])
    du[0:tok, :xo] = jnp.concatenate([db, dc], axis=1) * u[:, :xo]
    edge = None
    for i in range(nb):
        rows = slice(i * TB, (i + 1) * TB)
        bgt = mm(low[rows, 0:state_n], back16[...])
        w = w16[rows, :].astype(F32)
        qb = q16[rows, :].astype(F32) * bgt
        last_row = last_row + jnp.sum(qb, axis=0, keepdims=True)
        dwl = dw[rows, :]
        dwt = dwl + tol[rows, :].astype(F32) * bgt
        x = low[rows, xo:].astype(F32)
        dted = dte[rows, :].astype(F32) * dwt
        gx = dted[:, :inner] + dted[:, inner:] + skip_row * dmix[rows, :]
        du[rows, xo:] = gx.astype(BF16).astype(F32) * u[rows, xo:]
        if edge is None:
            edge = remote(du.at[pl.ds(0, 8)], du.at[pl.ds(tok, 8)], cx(nc - 1))
        d = dy[rows, :].astype(F32)
        ac = jnp.concatenate([d, d], axis=1) * yfr[rows, :] - w * dwl - qb
        xd = jnp.concatenate([x, x], axis=1) * dwt
        dcc[rows, :] = near_right(ac, spread)
        ddt[rows, :] = near_right(xd, spread)
        pump(PUMP[2][i])
    last_heads = exact_right(jnp.broadcast_to(last_row, (8, 2 * inner)), spread, mm_nt)[0:1, :]
    place = iota((tok, 1), 0)
    at_end = ((place == tok - 1) & is_fwd) | ((place == 0) & jnp.logical_not(is_fwd))
    dc_all = dcc[...] + jnp.where(at_end, last_heads, 0.0)
    dsums = exact_left(tri, dc_all)
    dld = jnp.where(is_fwd, dsums[tok - 1 : tok, :] - dsums + dc_all, dsums)
    gdt = (ddt[...] + dld * rate_row) * jax.nn.sigmoid(dtr[...])
    gall[:, xo : off[1]] = gdt.astype(BF16)
    misc = slice(conv_w, conv_w + 128)
    sm[...] = jnp.zeros(sm.shape, F32)
    sm[0, 5:6, :inner] = acc_gain
    sm[0, 3:4, misc] = exact_right(
        jnp.broadcast_to(acc_skip, (8, inner)), spread[:, :inner], mm_nt
    )[0:1, :]
    sm[0, 1:2, misc] = jnp.sum(gdt, axis=0, keepdims=True)
    sm[0, 2:3, misc] = jnp.sum(dld * ld[...], axis=0, keepdims=True)

    onward1 = pass_grads(1, grads1)

    taps_of = jnp.concatenate([conv_bc[...], conv_x[...]], axis=1)
    conv_acc = [jnp.zeros((1, conv_w), F32) for _ in range(taps)]
    for i in range(nb):
        lo, hi = i * TB, (i + 1) * TB
        if i == nb - 1:
            edge.wait_recv()
        here = seg_col(lo, TB)
        x_rows = xp[16 + lo : 16 + hi, :]
        acc = jnp.zeros((TB, conv_w), F32)
        for d in range(taps):
            m = du[lo + d : hi + d, :]
            if d > 0:
                m = m * (seg_col(lo, TB, d) == here).astype(F32)
            acc = acc + m * taps_of[taps - 1 - d : taps - d, :]
            conv_acc[taps - 1 - d] = conv_acc[taps - 1 - d] + jnp.sum(m * x_rows, axis=0, keepdims=True)
        gall[lo:hi, :xo] = acc[:, :xo].astype(BF16)
        gall[lo:hi, off[1] : off[2]] = acc[:, xo:].astype(BF16)
        pump(PUMP[4][i])
    for k in range(taps):
        sm[0, 1 + k : 2 + k, :conv_w] = conv_acc[k]

    w_all = weights(0, gall_w)
    acc_norm = jnp.zeros((1, width), F32)
    for i in range(nb):
        rows = slice(i * TB, (i + 1) * TB)
        part = mm_nt(gall[rows, :], w_all)
        hb[rows, :] = part.astype(BF16)
        line_h.begin(range(i * TB // PR, (i + 1) * TB // PR))
        h = hid[rows, :].astype(F32)
        rr = lax.rsqrt(jnp.mean(h * h, axis=1, keepdims=True) + EPS)
        acc_norm = acc_norm + jnp.sum(part * (h * rr), axis=0, keepdims=True)
        pump(PUMP[5][i])
    sm[0, 0:1, :] = acc_norm

    def small_send(level, slot, sends):
        return [remote(sm.at[level], smbuf.at[slot + k], dev) for k, dev in enumerate(sends)]

    def small_sum(level, slot, copies):
        acc = sm[level]
        for k, copy in enumerate(copies):
            copy.wait_recv()
            acc = acc + smbuf[slot + k]
        return acc

    sm0 = small_send(0, 0, [cx(k) for k in range(1, nc)])

    for b in range(width // block):
        cols = slice(b * block, (b + 1) * block)
        got = mm_tn(nl[16:, cols], gall[:, : off[2]])
        store_grads(b, 0, off[2], got)
    grads0 = send_grads(0)
    pump(PUMP[6][0])
    sm[1] = small_sum(0, 0, sm0)
    sm1 = small_send(1, nc - 1, [fs(k) for k in range(1, nf)])
    pump(PUMP[6][1])
    onward0 = pass_grads(0, grads0)
    pump(PUMP[6][2])
    sm[2] = small_sum(1, nc - 1, sm1)
    parts = [sm[2, 0:1, k * 128 : (k + 1) * 128] for k in range(width // 128)]
    parts = parts + [sm[2, 1 : 1 + taps, :xo], jnp.zeros((16 - taps - width // 128, 128), F32)]
    tps[...] = jnp.concatenate(parts, axis=0)
    tp_copies = [remote(tps, tpbuf.at[k - 1], tx(k)) for k in range(1, nt)]
    pump(PUMP[6][3])
    got = finish_grads(1, onward1)
    gwz[...] = got[:, :inner]
    gwo[...] = got[:, inner:]
    keep(gwz, gwz_h)
    keep(gwo, gwo_h)
    pump(PUMP[6][4])
    got = finish_grads(0, onward0)
    gwx[...] = got[:, off[1] :]
    gwdt[...] = got[:, xo : off[1]]
    keep(gwx, gwx_h)
    keep(gwdt, gwdt_h)
    bcs[...] = got[:, :xo].astype(BF16)
    bc_copies = [remote(bcs, bcbuf.at[k - 1], tx(k)) for k in range(1, nt)]
    pump(PUMP[6][5])
    for copy in tp_copies:
        copy.wait_recv()
    got = tp_order(tps[...], tpbuf)
    small[...] = sm[2]
    for k in range(width // 128):
        small[0:1, k * 128 : (k + 1) * 128] = got[k : k + 1, :]
    small[1 : 1 + taps, :xo] = got[width // 128 : width // 128 + taps, :]
    keep(small, small_h)
    pump(PUMP[6][6])
    for copy in bc_copies:
        copy.wait_recv()
    gwbc[...] = tp_order(bcs[...].astype(F32), bcbuf)
    keep(gwbc, gwbc_h)
    pump(len(todo))

    @pl.when(is_end)
    def _():
        for line in (line_o, line_h):
            for p in range(pieces):
                line.last(p)

    line_o.close()
    line_h.close()
    for p in range(pieces):
        rows = pl.ds(p * PR, PR)
        result(result_ids + p, out_v, out_h, rows).wait()
        result(result_ids + pieces + p, gh_v, gh_h, rows).wait()
    for copy in local_copies:
        copy.wait()
    for copy in pending:
        copy.wait_send()


def finish_kernel(dims, gdt_h, small_h, gh_h, out_h, gx_h, gz_h, gbc_h, go_h,
                  gh, out, o_x, o_z, o_bc, o_out, o_norm, o_dt, o_cx, o_cbc, o_bias, o_rate, o_skip, o_gain,
                  gh_s, out_s, x_s, z_s, bc_s, go_s, norm_s, dt_s, cx_s, cbc_s, bias_s, rate_s, skip_s, gain_s,
                  gdt, small, sems):
    hl, xo = dims
    count = [0]

    def move(src, dst):
        copy = pltpu.make_async_copy(src, dst, sems.at[count[0]])
        count[0] += 1
        copy.start()
        return copy

    first = [move(small_h, small), move(gdt_h, gdt)]
    moves = []
    for src, stage, dst, cuts in (
        (gh_h, gh_s, gh, 4), (out_h, out_s, out, 2), (gx_h, x_s, o_x, 1), (gz_h, z_s, o_z, 1),
        (go_h, go_s, o_out, 1), (gbc_h, bc_s, o_bc, 1),
    ):
        step = src.shape[0] // cuts
        for k in range(cuts):
            rows = pl.ds(k * step, step)
            moves.append((move(src.at[rows], stage.at[rows]), stage.at[rows], dst.at[rows]))
    rows_w, inner = gx_h.shape
    width = small.shape[1]
    conv_w = xo + inner
    for copy in first:
        copy.wait()
    norm_s[...] = small[0:1, :].reshape(width)
    flat = jnp.concatenate([gdt[...], jnp.zeros((128 - rows_w, 128), F32)], axis=0).T
    for k in range(hl):
        for d in range(2):
            dt_s[k, d : d + 1, :] = flat[d * hl + k : d * hl + k + 1, :rows_w]
    taps = cx_s.shape[0]
    cx_s[...] = small[1 : 1 + taps, xo:conv_w]
    cbc_s[...] = small[1 : 1 + taps, :xo]
    for row, ref in ((1, bias_s), (2, rate_s)):
        for d in range(2):
            ref[d : d + 1, :] = small[row : row + 1, conv_w + d * hl : conv_w + (d + 1) * hl]
    skip_s[...] = small[3:4, conv_w : conv_w + hl].reshape(hl)
    gain_s[...] = small[5:6, :inner].reshape(inner)
    leaving = [
        move(src, dst)
        for src, dst in (
            (norm_s, o_norm), (dt_s, o_dt), (cx_s, o_cx), (cbc_s, o_cbc), (bias_s, o_bias),
            (rate_s, o_rate), (skip_s, o_skip), (gain_s, o_gain),
        )
    ]
    for into, stage, dst in moves:
        into.wait()
        leaving.append(move(stage, dst))
    for copy in leaving:
        copy.wait()


def per_device(dims, hidden, seq_lengths, norm_gain, weight_x, weight_z, weight_bc, weight_dt,
               conv_x, conv_bc, dt_bias, log_rate, skip_scale, gate_gain, weight_out, cotangent):
    nf, nc, nt = dims
    tok, width = hidden.shape
    rows_w, inner = weight_x.shape
    hl = skip_scale.shape[0]
    shards = nf * nc
    xo = weight_bc.shape[1]
    state_n = xo // 2
    taps = conv_x.shape[0]
    conv_w = xo + inner
    p2 = xo + 128 + inner
    cw = p2 + 2 * inner
    pieces = tok // PR
    n_small = nf + nc - 2
    scratch = {
        "hid": ((tok, width), BF16),
        "cot": ((tok, width), BF16),
        "oag": ((tok, width), BF16),
        "hag": ((tok, width), BF16),
        "out_v": ((tok, width), BF16),
        "gh_v": ((tok, width), F32),
        "gwx": ((rows_w, inner), F32),
        "gwz": ((rows_w, inner), F32),
        "gwbc": ((rows_w, xo), F32),
        "gwdt": ((rows_w, 128), F32),
        "gwo": ((rows_w, inner), F32),
        "small": ((8, width), F32),
        "hbuf": ((16, width), BF16),
        "nl": ((tok + 16, width), BF16),
        "wbuf": ((shards, rows_w, cw), BF16),
        "xp": ((tok + 16, conv_w), F32),
        "dtr": ((tok, 128), F32),
        "u": ((tok, conv_w), F32),
        "low": ((tok, conv_w), BF16),
        "z": ((tok, inner), F32),
        "zd": ((tok, inner), F32),
        "ggate": ((tok, inner), BF16),
        "ld": ((tok, 128), F32),
        "cc": ((tok, 128), F32),
        "cct": ((128, tok), F32),
        "dte": ((tok, 2 * inner), BF16),
        "rea": ((tok, 2 * inner), BF16),
        "tol": ((tok, 2 * inner), BF16),
        "w16": ((tok, 2 * inner), BF16),
        "q16": ((tok, 2 * inner), BF16),
        "gm": ((tok, tok), F32),
        "gmt": ((tok, tok), F32),
        "pexp": ((hl, tok, tok), BF16),
        "yfr": ((tok, 2 * inner), F32),
        "s16": ((state_n, 2 * inner), BF16),
        "sbuf": ((nc - 1, state_n, inner), BF16),
        "dec": ((1, 128), F32),
        "decbuf": ((nc - 1, 1, 128), F32),
        "into16": ((state_n, 2 * inner), BF16),
        "gated": ((tok, inner), F32),
        "mixed": ((tok, inner), F32),
        "dmix": ((tok, inner), F32),
        "dy": ((tok, inner), BF16),
        "st": ((2, tok), F32),
        "stbuf": ((nt - 1, 2, tok), F32),
        "gall": ((tok, p2 + inner), BF16),
        "glow": ((tok, inner), BF16),
        "r_cols": ((tok, 128), F32),
        "ob": ((tok, width), BF16),
        "oin": ((pieces, PR, width), BF16),
        "oex": ((pieces, PR, width), BF16),
        "hb": ((tok, width), BF16),
        "hin": ((pieces, PR, width), BF16),
        "hex": ((pieces, PR, width), BF16),
        "rdy": ((tok, 2 * inner), BF16),
        "d16": ((state_n, 2 * inner), BF16),
        "dbuf": ((nc - 1, state_n, inner), BF16),
        "back16": ((state_n, 2 * inner), BF16),
        "dg": ((tok, tok), BF16),
        "dw": ((tok, 2 * inner), F32),
        "dcc": ((tok, 128), F32),
        "ddt": ((tok, 128), F32),
        "du": ((tok + 8, conv_w), F32),
        "gw16": ((shards, rows_w, cw), BF16),
        "fbuf": ((nf - 1, nc, rows_w, cw), BF16),
        "hsend": ((nc, rows_w, cw), BF16),
        "cbuf": ((nc - 1, rows_w, cw), BF16),
        "bcs": ((rows_w, xo), BF16),
        "bcbuf": ((nt - 1, rows_w, xo), BF16),
        "sm": ((3, 8, width), F32),
        "smbuf": ((n_small, 8, width), F32),
        "tps": ((16, 128), F32),
        "tpbuf": ((nt - 1, 16, 128), F32),
    }
    n_sems = 2 + 4 * (nc + nf - 2 + (nc - 1) * (nf - 1)) + 3 * (nc - 1) + 3 * (nt - 1)
    n_sems += 2 * (nf - 1 + nc - 1) + n_small + 6 * pieces + nt - 1
    vmem = pl.BlockSpec(memory_space=pltpu.VMEM)
    smem = pl.BlockSpec(memory_space=pltpu.SMEM)
    f32 = lambda *shape: jax.ShapeDtypeStruct(shape, F32)
    bf16 = lambda *shape: jax.ShapeDtypeStruct(shape, BF16)
    anywhere = pl.BlockSpec(memory_space=pl.ANY)
    results = pl.pallas_call(
        partial(mixer_kernel, (nf, nc, nt, hl)),
        out_shape=(
            bf16(tok, width), f32(tok, width), f32(rows_w, inner), f32(rows_w, inner),
            f32(rows_w, xo), f32(rows_w, 128), f32(rows_w, inner), f32(8, width),
        ),
        in_specs=[smem] + [vmem] * 4 + [smem] * 3 + [vmem] + [anywhere] * 6,
        out_specs=[anywhere] * 8,
        scratch_shapes=[pltpu.VMEM(s, d) for s, d in scratch.values()]
        + [pltpu.SemaphoreType.DMA((n_sems,)), pltpu.SemaphoreType.DMA((n_sems,))]
        + [pltpu.SemaphoreType.DMA((12 + 2 * pieces,))],
        compiler_params=pltpu.CompilerParams(
            collective_id=0, has_side_effects=True, vmem_limit_bytes=62 << 20
        ),
    )(
        seq_lengths, norm_gain, jnp.transpose(weight_dt, (2, 1, 0)), conv_x, conv_bc, dt_bias, log_rate,
        skip_scale, gate_gain, hidden, cotangent, weight_x, weight_z, weight_bc, weight_out.T,
    )
    out, gh, gx, gz, gbc, gdt, go, small = results
    finals = (
        f32(tok, width), bf16(tok, width), f32(rows_w, inner), f32(rows_w, inner), f32(rows_w, xo),
        f32(rows_w, inner), f32(width), f32(hl, 2, rows_w), f32(taps, inner), f32(taps, xo),
        f32(2, hl), f32(2, hl), f32(hl), f32(inner),
    )
    gh, out, gx, gz, gbc, go, norm, gdt, cx, cbc, bias, rate, skip, gate = pl.pallas_call(
        partial(finish_kernel, (hl, xo)),
        out_shape=finals,
        in_specs=[anywhere] * 8,
        out_specs=[anywhere] * 14,
        scratch_shapes=[pltpu.VMEM(a.shape, a.dtype) for a in finals]
        + [pltpu.VMEM((rows_w, 128), F32), pltpu.VMEM((8, width), F32), pltpu.SemaphoreType.DMA((32,))],
        compiler_params=pltpu.CompilerParams(vmem_limit_bytes=62 << 20),
    )(gdt, small, gh, out, gx, gz, gbc, go)
    return (
        out, gh, norm, gx, gz, gbc, jnp.transpose(gdt, (2, 1, 0)), cx, cbc, bias, rate, skip, gate, go.T
    )


def solution(mesh):
    dims = tuple(mesh.shape[a] for a in ("fsdp", "ctx", "tp"))
    both = ("fsdp", "ctx")
    return jax.shard_map(
        partial(per_device, dims),
        mesh=mesh,
        in_specs=(
            P(both, None), P("fsdp", None), P(), P(both, "tp"), P(both, "tp"), P(both, None),
            P(both, None, "tp"), P(None, "tp"), P(), P(None, "tp"), P(None, "tp"), P("tp"),
            P("tp"), P("tp", both), P(both, None),
        ),
        out_specs=(
            P(both, None), P(both, None), P(), P(both, "tp"), P(both, "tp"), P(both, None),
            P(both, None, "tp"), P(None, "tp"), P(), P(None, "tp"), P(None, "tp"), P("tp"),
            P("tp"), P("tp", both),
        ),
        check_vma=False,
    )
```

```python
from functools import partial

import jax
import jax.numpy as jnp
from jax import lax
from jax.experimental import pallas as pl
from jax.experimental.pallas import tpu as pltpu
from jax.sharding import PartitionSpec as P

MESH = pl.DeviceIdType.MESH
F32 = jnp.float32
BF16 = jnp.bfloat16
EPS = 1e-05
TB = 128
PR = 64
LAG = 2
PUMP = (
    (0, 1, 1, 1), (1, 0, 1, 1), (1, 1, 1, 1), (0, 0, 0, 0), (1, 1, 1, 1), (1, 1, 1, 1), (2, 2, 3, 4, 0, 4, 0)
)


def mm(left, right):
    return lax.dot_general(left, right, (((1,), (0,)), ((), ())), preferred_element_type=F32)


def mm_nt(left, right):
    return lax.dot_general(left, right, (((1,), (1,)), ((), ())), preferred_element_type=F32)


def mm_tn(left, right):
    return lax.dot_general(left, right, (((0,), (0,)), ((), ())), preferred_element_type=F32)


def split3(value):
    high = value.astype(BF16)
    rest = value - high.astype(F32)
    middle = rest.astype(BF16)
    low = (rest - middle.astype(F32)).astype(BF16)
    return high, middle, low


def exact_left(ones, value, dot=mm):
    a, b, c = split3(value)
    return dot(ones, a) + dot(ones, b) + dot(ones, c)


def exact_right(value, ones, dot=mm):
    a, b, c = split3(value)
    return dot(a, ones) + dot(b, ones) + dot(c, ones)


def iota(shape, dim):
    return lax.broadcasted_iota(jnp.int32, shape, dim)


def near_right(value, ones):
    high = value.astype(BF16)
    low = (value - high.astype(F32)).astype(BF16)
    return mm_nt(high, ones) + mm_nt(low, ones)


def mixer_kernel(dims, *refs):
    (lens, gain, wdt, conv_x, conv_bc, dtb, rate, skip, ggain, hid_h, cot_h, wx_h, wz_h, wbc_h, wot_h,
     out_h, gh_h, gwx_h, gwz_h, gwbc_h, gwdt_h, gwo_h, small_h,
     hid, cot, oag, hag, out_v, gh_v, gwx, gwz, gwbc, gwdt, gwo, small, hbuf, nl, wbuf, xp, dtr, u, low, z, zd, ggate, ld, cc, cct, dte,
     rea, tol, w16, q16, gm, gmt, pexp, yfr, s16, sbuf, dec, decbuf, into16, gated, mixed, dmix, dy,
     st, stbuf, gall, glow, r_cols, ob, oin, oex, hb, hin, hex_, rdy, d16, dbuf, back16, dg, dw, dcc, ddt,
     du, gw16, fbuf, hsend, cbuf, bcs, bcbuf, sm, smbuf, tps, tpbuf, ssem, rsem, lsem) = refs
    nf, nc, nt, hl = dims
    tok, width = hid.shape
    rows_w, inner = wx_h.shape
    pdim = inner // hl
    state_n = wbc_h.shape[1] // 2
    xo = 2 * state_n
    conv_w = xo + inner
    off = (0, xo + 128, xo + 128 + inner, xo + 128 + 2 * inner, xo + 128 + 3 * inner)
    gall_w = off[3]
    nb = tok // TB
    taps = conv_x.shape[0]
    f, c, t = lax.axis_index("fsdp"), lax.axis_index("ctx"), lax.axis_index("tp")
    base = c * tok
    counter = [0]
    pending = []

    def take(count):
        counter[0] += count
        return counter[0] - count

    def describe(i, src, dst, dev):
        return pltpu.make_async_remote_copy(
            src_ref=src, dst_ref=dst, send_sem=ssem.at[i], recv_sem=rsem.at[i],
            device_id=dev, device_id_type=MESH,
        )

    def remote(src, dst, dev):
        copy = describe(take(1), src, dst, dev)
        copy.start()
        pending.append(copy)
        return copy

    def fs(k):
        return (lax.rem(f + k, nf), c, t)

    def cx(k):
        return (f, lax.rem(c + k, nc), t)

    def tx(k):
        return (f, c, lax.rem(t + k, nt))

    barrier = pltpu.get_barrier_semaphore()
    peers = [fs(k) for k in range(1, nf)] + [cx(k) for k in range(1, nc)] + [tx(k) for k in range(1, nt)]
    for dev in peers:
        pl.semaphore_signal(barrier, inc=1, device_id=dev, device_id_type=MESH)

    local_count = [0]
    local_copies = []

    def bring(src, dst):
        i = local_count[0]
        local_count[0] += 1
        copy = pltpu.make_async_copy(src, dst, lsem.at[i])
        copy.start()
        return copy

    def keep(src, dst):
        local_copies.append(bring(src, dst))

    me = f * nc + c
    get_hid = bring(hid_h, hid)
    shard_copies = []
    for p, src in ((0, wbc_h), (1, wx_h), (2, wz_h), (3, wot_h)):
        width_p = xo if p == 0 else inner
        shard_copies.append(bring(src, wbuf.at[me, :, pl.ds(off[p], width_p)]))
    get_cot = bring(cot_h, cot)
    flat = jnp.concatenate(
        [wdt[h].astype(F32) for h in range(hl)] + [jnp.zeros((16 - 2 * hl, rows_w), F32)], axis=0
    ).astype(BF16)
    lane_of = lax.rem(iota((16, 128), 0), 2) * hl + lax.div(iota((16, 128), 0), 2)
    turn = (iota((16, 128), 1) == lane_of).astype(F32).astype(BF16)
    wbuf[me, :, xo : off[1]] = mm_tn(flat, turn).astype(BF16)

    lane = iota((1, 128), 1)
    is_fwd = lane < hl
    bias_row = jnp.zeros((1, 128), F32)
    log_row = jnp.zeros((1, 128), F32)
    for d in range(2):
        for h in range(hl):
            bias_row = jnp.where(lane == d * hl + h, dtb[d, h], bias_row)
            log_row = jnp.where(lane == d * hl + h, rate[d, h], log_row)
    rate_row = -jnp.exp(log_row)
    head_of = lax.div(iota((1, inner), 1), pdim)
    skip_row = jnp.zeros((1, inner), F32)
    for h in range(hl):
        skip_row = jnp.where(head_of == h, skip[h], skip_row)
    gain_row = gain[...].reshape(1, width)
    gain_gate = ggain[...].reshape(1, inner)

    def norm_low(rows):
        h = rows.astype(F32)
        r = lax.rsqrt(jnp.mean(h * h, axis=1, keepdims=True) + EPS)
        return (h * r * gain_row).astype(BF16)

    get_hid.wait()

    @pl.loop(0, nb)
    def _(i):
        at = pl.multiple_of(i * TB, TB)
        nl[pl.ds(16 + at, TB), :] = norm_low(hid[pl.ds(at, TB), :])

    for copy in shard_copies:
        copy.wait()
    pl.semaphore_wait(barrier, len(peers))

    col_parts = [pl.ds(off[p], off[p + 1] - off[p]) for p in range(4)]
    rim = remote(hid.at[pl.ds(tok - 16, 16)], hbuf, cx(1))
    ctx_copies = []
    fwd_copies = []

    def send_weights(part):
        own = wbuf.at[me, :, col_parts[part]]
        ctx_copies.append([remote(own, own, cx(k)) for k in range(1, nc)])
        fwd_copies.append([remote(own, own, fs(k)) for k in range(1, nf)])

    for part in range(4):
        send_weights(part)

    def pass_weights(part):
        for k in range(1, nc):
            ctx_copies[part][k - 1].wait_recv()
            src = wbuf.at[f * nc + lax.rem(c + nc - k, nc), :, col_parts[part]]
            for j in range(1, nf):
                fwd_copies[part].append(remote(src, src, fs(j)))

    def get_weights(part):
        for copy in fwd_copies[part]:
            copy.wait_recv()

    def weights(lo, hi):
        if rows_w % 16 == 0:
            return wbuf[:, :, lo:hi].reshape(width, hi - lo)
        return wbuf[:, :, lo:hi].astype(F32).reshape(width, hi - lo).astype(BF16)

    ends = []
    total = lens[0, 0]
    ends.append(total)
    for k in range(1, lens.shape[1]):
        total = total + lens[0, k]
        ends.append(total)

    def seg_of(pos):
        seg = jnp.where(pos < 0, -1, 0)
        for e in ends:
            seg = seg + jnp.where(pos >= e, 1, 0)
        return seg

    one_pos = jnp.full((1, 1), 0, jnp.int32)
    seg_before = seg_of(one_pos + (base - 1))
    seg_first = seg_of(one_pos + base)
    seg_last = seg_of(one_pos + (base + tok - 1))
    seg_after = seg_of(one_pos + (base + tok))
    seg_row = seg_of(iota((1, tok), 1) + base)
    place_row = iota((1, tok), 1)

    def seg_col(start, count, shift=0):
        return seg_of(iota((count, 1), 0) + (base + start + shift))

    spread = (
        iota((128, 2 * inner), 0) == lax.div(iota((128, 2 * inner), 1), pdim)
    ).astype(F32).astype(BF16)
    tri = (iota((tok, tok), 0) >= iota((tok, tok), 1)).astype(F32).astype(BF16)
    seg_all = seg_col(0, tok)

    rim.wait_recv()
    nl[0:16, :] = norm_low(hbuf[...])
    pass_weights(0)
    get_weights(0)

    w_part = weights(off[0], off[1])
    xp[0:16, :xo] = mm(nl[0:16, :], w_part)[:, :xo]
    for i in range(tok // 256):
        got = mm(nl[16 + i * 256 : 16 + (i + 1) * 256, :], w_part)
        xp[16 + i * 256 : 16 + (i + 1) * 256, :xo] = got[:, :xo]
        dtr[i * 256 : (i + 1) * 256, :] = got[:, xo:] + bias_row

    def conv_forward(cols, taps_ref):
        for i in range(nb):
            lo = i * TB
            here = seg_col(lo, TB)
            acc = xp[16 + lo : 16 + lo + TB, cols] * taps_ref[taps - 1 : taps, :]
            for d in range(1, taps):
                match = (seg_col(lo, TB, -d) == here).astype(F32)
                acc = acc + xp[16 + lo - d : 16 + lo - d + TB, cols] * taps_ref[taps - 1 - d : taps - d, :] * match
            sg = jax.nn.sigmoid(acc)
            u[lo : lo + TB, cols] = sg * (1.0 + acc * (1.0 - sg))
            low[lo : lo + TB, cols] = (acc * sg).astype(BF16)

    bc_cols, x_cols = slice(0, xo), slice(xo, conv_w)
    conv_forward(bc_cols, conv_bc)
    raw = dtr[...]
    step = jnp.maximum(raw, 0.0) + jnp.log1p(jnp.exp(-jnp.abs(raw)))
    decay = step * rate_row
    ld[...] = decay
    sums = exact_left(tri, decay)
    tot = sums[tok - 1 : tok, :]
    cum = jnp.where(is_fwd, sums, tot - sums + decay)
    cc[...] = cum
    cct[...] = cum.T
    dec_mask = jnp.where(
        is_fwd,
        (seg_last == seg_before).astype(F32),
        (seg_first == seg_after).astype(F32),
    )
    dec[...] = jnp.exp(tot) * dec_mask
    dec_copies = [remote(dec, decbuf.at[k - 1], cx(k)) for k in range(1, nc)]
    reach = jnp.exp(cum) * jnp.where(
        is_fwd, (seg_all == seg_before).astype(F32), (seg_all == seg_after).astype(F32)
    )
    to_end = jnp.exp(tot - cum) * jnp.where(
        is_fwd, (seg_all == seg_last).astype(F32), (seg_all == seg_first).astype(F32)
    )
    dte[...] = mm(step.astype(BF16), spread).astype(BF16)
    tol[...] = mm(to_end.astype(BF16), spread).astype(BF16)
    pass_weights(1)

    b16 = low[:, 0:state_n]
    c16 = low[:, state_n:xo]

    get_weights(1)
    w_part = weights(off[1], off[2])
    xp[0:16, xo:] = mm(nl[0:16, :], w_part)
    for i in range(tok // 256):
        xp[16 + i * 256 : 16 + (i + 1) * 256, xo:] = mm(nl[16 + i * 256 : 16 + (i + 1) * 256, :], w_part)
    conv_forward(x_cols, conv_x)

    @pl.loop(0, nb)
    def _(i):
        rows = pl.ds(pl.multiple_of(i * TB, TB), TB)
        x = low[rows, xo:].astype(F32)
        w = (jnp.concatenate([x, x], axis=1) * dte[rows, :].astype(F32)).astype(BF16)
        w16[rows, :] = w
        q16[rows, :] = (w.astype(F32) * tol[rows, :].astype(F32)).astype(BF16)

    s16[...] = mm_tn(b16, q16[...]).astype(BF16)

    def half_of(forward):
        return pl.ds(pl.multiple_of(jnp.where(forward, 0, inner), 128), inner)

    state_copies = []
    for k in range(1, nc):
        forward = lax.rem(c + k, nc) > c
        state_copies.append(remote(s16.at[:, half_of(forward)], sbuf.at[k - 1], cx(k)))

    rea[...] = mm(reach.astype(BF16), spread).astype(BF16)

    def mix_mask(i):
        same = seg_col(i * TB, TB) == seg_row
        return same & (iota((TB, 1), 0) + i * TB != place_row)

    for i in range(nb):
        lo, hi = i * TB, (i + 1) * TB
        mask = mix_mask(i)
        gm[lo:hi, :] = jnp.where(mask, mm_nt(c16[lo:hi], b16), 0.0)
        gmt[lo:hi, :] = jnp.where(mask, mm_nt(b16[lo:hi], c16), 0.0)

    pass_weights(2)

    local = iota((TB, TB), 0)
    below = local > iota((TB, TB), 1)
    above = local < iota((TB, TB), 1)
    pair_left = iota((1, 128), 1) < pdim

    def pair_cols(pair):
        return (
            slice(pair * 128, (pair + 1) * 128),
            slice(inner + pair * 128, inner + (pair + 1) * 128),
        )

    def beside(parts):
        return jnp.concatenate(parts, axis=1) if len(parts) > 1 else parts[0]

    for i in range(nb):
        lo, hi = i * TB, (i + 1) * TB
        g_diag = gm[lo:hi, lo:hi]
        g_low = jnp.where(below, g_diag, 0.0)
        g_up = jnp.where(above, g_diag, 0.0)
        for pair in range(hl // 2):
            cols, cols_r = pair_cols(pair)
            ys = []
            for h in (2 * pair, 2 * pair + 1):
                fc = cc[lo:hi, h : h + 1]
                rc = cc[lo:hi, hl + h : hl + h + 1]
                fr = cct[h : h + 1, :]
                rr = cct[hl + h : hl + h + 1, :]
                p = jnp.exp(jnp.minimum(fc - fr[:, lo:hi], rc - rr[:, lo:hi]))
                pexp[h, lo:hi, lo:hi] = p.astype(BF16)
                lows = [(g_low * p).astype(BF16)]
                ups = [(g_up * p).astype(BF16)]
                if i > 0:
                    p = jnp.exp(fc - fr[:, :lo])
                    pexp[h, lo:hi, :lo] = p.astype(BF16)
                    lows.insert(0, (gm[lo:hi, :lo] * p).astype(BF16))
                if i < nb - 1:
                    p = jnp.exp(rc - rr[:, hi:])
                    pexp[h, lo:hi, hi:] = p.astype(BF16)
                    ups.append((gm[lo:hi, hi:] * p).astype(BF16))
                ys.append((mm(beside(lows), w16[:hi, cols]), mm(beside(ups), w16[lo:, cols_r])))
            yfr[lo:hi, cols] = jnp.where(pair_left, ys[0][0], ys[1][0])
            yfr[lo:hi, cols_r] = jnp.where(pair_left, ys[0][1], ys[1][1])

    get_weights(2)
    w_part = weights(off[2], off[3])
    for i in range(tok // 256):
        zz = mm(nl[16 + i * 256 : 16 + (i + 1) * 256, :], w_part)
        sg = jax.nn.sigmoid(zz)
        z[i * 256 : (i + 1) * 256, :] = zz * sg
        zd[i * 256 : (i + 1) * 256, :] = sg * (1.0 + zz * (1.0 - sg))

    pass_weights(3)
    get_weights(3)
    get_cot.wait()
    wo = weights(off[3], off[4])
    for i in range(tok // 256):
        rows = slice(i * 256, (i + 1) * 256)
        ggate[rows, :] = mm(cot[rows, :], wo).astype(BF16)

    dec_spread = []
    for k in range(1, nc):
        dec_copies[k - 1].wait_recv()
        dec_spread.append(exact_right(jnp.broadcast_to(decbuf[k - 1], (8, 128)), spread)[0:1, :])
    for copy in state_copies:
        copy.wait_recv()
    acc_f = jnp.zeros((state_n, inner), F32)
    acc_r = jnp.zeros((state_n, inner), F32)
    for k in range(nc - 1, 0, -1):
        new = dec_spread[k - 1][:, :inner] * acc_f + sbuf[k - 1].astype(F32)
        acc_f = jnp.where(k <= c, new, acc_f)
    for k in range(1, nc):
        new = dec_spread[k - 1][:, inner:] * acc_r + sbuf[k - 1].astype(F32)
        acc_r = jnp.where(k > c, new, acc_r)
    into16[:, :inner] = acc_f.astype(BF16)
    into16[:, inner:] = acc_r.astype(BF16)

    ones8 = jnp.ones((8, inner), BF16)
    for i in range(nb):
        rows = slice(i * TB, (i + 1) * TB)
        carried = mm(low[rows, state_n:xo], into16[...]) * rea[rows, :].astype(F32)
        y = yfr[rows, :] + carried
        yfr[rows, :] = y
        mix = y[:, :inner] + y[:, inner:] + skip_row * low[rows, xo:].astype(F32)
        mixed[rows, :] = mix
        gt = mix * z[rows, :]
        gated[rows, :] = gt
        st[0:1, rows] = mm_nt(ones8, (gt * gt).astype(BF16))[0:1]
        gl = gt * gain_gate
        glow[rows, :] = gl.astype(BF16)
        st[1:2, rows] = mm_nt(ones8, (ggate[rows, :].astype(F32) * gl).astype(BF16))[0:1]
    st_copies = [remote(st, stbuf.at[k - 1], tx(k)) for k in range(1, nt)]
    total_inner = inner * nt
    pick = (iota((8, 128), 0) == 0).astype(F32).astype(BF16)

    is_mid = (t > 0) & (t < nt - 1)
    is_end = (t == 0) | (t == nt - 1)
    inside = (f, c, 1 + lax.div(t, nt - 1))
    across = (f, c, nt - 1 - t)
    outside = (f, c, (t - 1) * (nt - 1))
    pieces = tok // PR

    def piece(ref, p):
        return ref.at[pl.ds(p * PR, PR)]

    class Line:
        def __init__(self, own, inbox, exchange, sums, done):
            self.own, self.inbox, self.exchange, self.sums = own, inbox, exchange, sums
            self.done = done
            self.ids = take(3 * pieces)

        def up(self, p):
            return describe(self.ids + p, piece(self.own, p), self.inbox.at[p], inside)

        def over(self, p):
            return describe(self.ids + pieces + p, piece(self.own, p), self.exchange.at[p], across)

        def down(self, p):
            return describe(self.ids + 2 * pieces + p, piece(self.sums, p), piece(self.sums, p), outside)

        def first(self, p):
            self.up(p).wait_recv()
            rows = slice(p * PR, (p + 1) * PR)
            both = self.own[rows, :].astype(F32) + self.inbox[p].astype(F32)
            self.own[rows, :] = both.astype(BF16)
            self.over(p).start()

        def second(self, p):
            self.over(p).wait_recv()
            rows = slice(p * PR, (p + 1) * PR)
            both = (self.own[rows, :].astype(F32) + self.exchange[p].astype(F32)).astype(BF16)
            self.sums[rows, :] = both
            self.down(p).start()
            self.done(p, rows, both)

        def last(self, p):
            self.down(p).wait_recv()
            rows = slice(p * PR, (p + 1) * PR)
            self.done(p, rows, self.sums[rows, :])

        def begin(self, p_list):
            @pl.when(is_end)
            def _():
                for p in p_list:
                    self.up(p).start()

        def close(self):
            @pl.when(is_end)
            def _():
                for p in range(pieces):
                    self.up(p).wait_send()

            @pl.when(is_mid)
            def _():
                for p in range(pieces):
                    self.over(p).wait_send()
                    self.down(p).wait_send()

    def result(i, src, dst, rows):
        return pltpu.make_async_copy(src.at[rows], dst.at[rows], lsem.at[i])

    result_ids = local_count[0]
    local_count[0] += 2 * pieces

    def out_done(p, rows, both):
        out_v[rows, :] = (hid[rows, :].astype(F32) + both.astype(F32) * r_cols[rows, 0:1]).astype(BF16)
        result(result_ids + p, out_v, out_h, pl.ds(p * PR, PR)).start()

    def head_done(p, rows, both):
        h = hid[rows, :].astype(F32)
        rr = lax.rsqrt(jnp.mean(h * h, axis=1, keepdims=True) + EPS)
        q = both.astype(F32) * gain_row
        inner_mean = jnp.mean(q * h, axis=1, keepdims=True)
        gh_v[rows, :] = cot[rows, :].astype(F32) + rr * (q - h * (rr * rr * inner_mean))
        result(result_ids + pieces + p, gh_v, gh_h, pl.ds(p * PR, PR)).start()

    line_o = Line(ob, oin, oex, oag, out_done)
    line_h = Line(hb, hin, hex_, hag, head_done)
    todo = []
    for p in range(2 * pieces + LAG):
        for q, stage in ((p, 0), (p - LAG, 1)):
            if 0 <= q < 2 * pieces:
                line = line_o if q < pieces else line_h
                todo.append(partial(line.first if stage == 0 else line.second, q % pieces))

    def pump(count):
        now = [todo.pop(0) for _ in range(min(count, len(todo)))]
        if now:
            @pl.when(is_mid)
            def _():
                for action in now:
                    action()

    for i in range(nb):
        rows = slice(i * TB, (i + 1) * TB)
        ob[rows, :] = mm_nt(glow[rows, :], wo).astype(BF16)
        line_o.begin(range(i * TB // PR, (i + 1) * TB // PR))

    def tp_order(own, box):
        total = None
        for k in range(nt):
            part = jnp.where(t == k, own, 0.0)
            for j in range(1, nt):
                part = jnp.where(lax.rem(t + nt - j, nt) == k, box[j - 1].astype(F32), part)
            total = part if total is None else total + part
        return total

    for copy in st_copies:
        copy.wait_recv()
    both = tp_order(st[...], stbuf)
    r_row = lax.rsqrt(both[0:1, :] * (1.0 / total_inner) + EPS)
    q_row = r_row * r_row * r_row * both[1:2, :] * (-1.0 / total_inner)
    r_cols[...] = exact_right(jnp.broadcast_to(r_row, (8, tok)), pick, mm_tn)
    q_cols = exact_right(jnp.broadcast_to(q_row, (8, tok)), pick, mm_tn)

    block = 384
    per = block // rows_w

    def store_grads(b, lo, hi, value):
        for s in range(per):
            gw16[b * per + s, :, lo:hi] = value[s * rows_w : (s + 1) * rows_w].astype(BF16)

    acc_gain = jnp.zeros((1, inner), F32)
    acc_skip = jnp.zeros((1, inner), F32)
    for i in range(nb):
        rows = slice(i * TB, (i + 1) * TB)
        r = r_cols[rows, 0:1]
        gt = gated[rows, :]
        gg = ggate[rows, :].astype(F32)
        ghat = gt * r
        glow[rows, :] = (ghat * gain_gate).astype(BF16)
        acc_gain = acc_gain + jnp.sum(gg * ghat, axis=0, keepdims=True)
        ggated = gg * gain_gate * r + gt * q_cols[rows, 0:1]
        dm = ggated * z[rows, :]
        gall[rows, off[2] :] = (ggated * mixed[rows, :] * zd[rows, :]).astype(BF16)
        dmix[rows, :] = dm
        acc_skip = acc_skip + jnp.sum(dm * low[rows, xo:].astype(F32), axis=0, keepdims=True)
        d = dm.astype(BF16)
        dy[rows, :] = d
        rdy[rows, :] = (jnp.concatenate([d, d], axis=1).astype(F32) * rea[rows, :].astype(F32)).astype(BF16)

    d16[...] = mm_tn(low[:, state_n:xo], rdy[...]).astype(BF16)
    back_copies = []
    for k in range(1, nc):
        forward = lax.rem(c + k, nc) < c
        back_copies.append(remote(d16.at[:, half_of(forward)], dbuf.at[k - 1], cx(k)))

    col_sets = ((0, off[2]), (off[2], off[4]))

    def send_grads(part):
        lo, hi = col_sets[part]
        copies = []
        for k in range(1, nf):
            to = pl.ds(lax.rem(f + k, nf) * nc, nc)
            copies.append(
                remote(gw16.at[to, :, pl.ds(lo, hi - lo)], fbuf.at[k - 1, :, :, pl.ds(lo, hi - lo)], fs(k))
            )
        return copies

    def pass_grads(part, copies):
        lo, hi = col_sets[part]
        for copy in copies:
            copy.wait_recv()
        onward = []
        for k in list(range(1, nc)) + [0]:
            to = lax.rem(c + k, nc)
            acc = gw16[f * nc + to, :, lo:hi].astype(F32)
            for j in range(1, nf):
                acc = acc + fbuf[j - 1, to, :, lo:hi].astype(F32)
            hsend[k, :, lo:hi] = acc.astype(BF16)
            if k > 0:
                onward.append(
                    remote(hsend.at[k, :, pl.ds(lo, hi - lo)], cbuf.at[k - 1, :, pl.ds(lo, hi - lo)], cx(k))
                )
        return onward

    def finish_grads(part, onward):
        lo, hi = col_sets[part]
        for copy in onward:
            copy.wait_recv()
        acc = hsend[0, :, lo:hi].astype(F32)
        for k in range(1, nc):
            acc = acc + cbuf[k - 1, :, lo:hi].astype(F32)
        return acc

    for b in range(width // block):
        cols = slice(b * block, (b + 1) * block)
        store_grads(b, off[2], off[3], mm_tn(nl[16:, cols], gall[:, off[2] :]))
        store_grads(b, off[3], off[4], mm_tn(cot[:, cols], glow[...]))
    grads1 = send_grads(1)

    for i in range(nb):
        lo, hi = i * TB, (i + 1) * TB
        g_diag = gmt[lo:hi, lo:hi]
        g_low = jnp.where(below, g_diag, 0.0)
        g_up = jnp.where(above, g_diag, 0.0)
        for pair in range(hl // 2):
            cols, cols_r = pair_cols(pair)
            ds = []
            for h in (2 * pair, 2 * pair + 1):
                fc = cc[lo:hi, h : h + 1]
                rc = cc[lo:hi, hl + h : hl + h + 1]
                fr = cct[h : h + 1, :]
                rr = cct[hl + h : hl + h + 1, :]
                p = jnp.exp(jnp.minimum(fr[:, lo:hi] - fc, rr[:, lo:hi] - rc))
                ups = [(g_up * p).astype(BF16)]
                lows = [(g_low * p).astype(BF16)]
                if i < nb - 1:
                    p = jnp.exp(fr[:, hi:] - fc)
                    ups.append((gmt[lo:hi, hi:] * p).astype(BF16))
                if i > 0:
                    p = jnp.exp(rr[:, :lo] - rc)
                    lows.insert(0, (gmt[lo:hi, :lo] * p).astype(BF16))
                ds.append((mm(beside(ups), dy[lo:, cols]), mm(beside(lows), dy[:hi, cols])))
            dw[lo:hi, cols] = jnp.where(pair_left, ds[0][0], ds[1][0])
            dw[lo:hi, cols_r] = jnp.where(pair_left, ds[0][1], ds[1][1])
        pump(PUMP[0][i])

    for i in range(nb):
        lo, hi = i * TB, (i + 1) * TB
        acc_low = jnp.zeros((TB, lo), F32) if i > 0 else None
        acc_up = jnp.zeros((TB, tok - hi), F32) if i < nb - 1 else None
        acc_diag = jnp.zeros((TB, TB), F32)
        for h in range(hl):
            cols, cols_r = pair_cols(h // 2)
            mine = pair_left if h % 2 == 0 else jnp.logical_not(pair_left)
            d = jnp.where(mine, dy[lo:hi, cols].astype(F32), 0.0).astype(BF16)
            wf = mm_nt(d, w16[:hi, cols])
            wr = mm_nt(d, w16[lo:, cols_r])
            acc_diag = acc_diag + jnp.where(below, wf[:, lo:], wr[:, :TB]) * pexp[h, lo:hi, lo:hi].astype(F32)
            if i > 0:
                acc_low = acc_low + wf[:, :lo] * pexp[h, lo:hi, :lo].astype(F32)
            if i < nb - 1:
                acc_up = acc_up + wr[:, TB:] * pexp[h, lo:hi, hi:].astype(F32)
        parts = ([acc_low] if i > 0 else []) + [acc_diag] + ([acc_up] if i < nb - 1 else [])
        dg[lo:hi, :] = jnp.where(mix_mask(i), beside(parts), 0.0).astype(BF16)
        pump(PUMP[1][i])

    for copy in back_copies:
        copy.wait_recv()
    acc_f = jnp.zeros((state_n, inner), F32)
    acc_r = jnp.zeros((state_n, inner), F32)
    for k in range(1, nc):
        new = dec_spread[k - 1][:, :inner] * acc_f + dbuf[k - 1].astype(F32)
        acc_f = jnp.where(k > c, new, acc_f)
    for k in range(nc - 1, 0, -1):
        new = dec_spread[k - 1][:, inner:] * acc_r + dbuf[k - 1].astype(F32)
        acc_r = jnp.where(k <= c, new, acc_r)
    back16[:, :inner] = acc_f.astype(BF16)
    back16[:, inner:] = acc_r.astype(BF16)
    dec_own = exact_right(jnp.broadcast_to(dec[...], (8, 128)), spread)[0:1, :]
    last_row = dec_own * jnp.sum(
        back16[...].astype(F32) * into16[...].astype(F32), axis=0, keepdims=True
    )

    db = mm_tn(dg[...], c16) + mm_nt(q16[...], back16[...])
    dc = mm(dg[...], b16) + mm_nt(rdy[...], into16[...])
    du[0:tok, :xo] = jnp.concatenate([db, dc], axis=1) * u[:, :xo]
    edge = None
    for i in range(nb):
        rows = slice(i * TB, (i + 1) * TB)
        bgt = mm(low[rows, 0:state_n], back16[...])
        w = w16[rows, :].astype(F32)
        qb = q16[rows, :].astype(F32) * bgt
        last_row = last_row + jnp.sum(qb, axis=0, keepdims=True)
        dwl = dw[rows, :]
        dwt = dwl + tol[rows, :].astype(F32) * bgt
        x = low[rows, xo:].astype(F32)
        dted = dte[rows, :].astype(F32) * dwt
        gx = dted[:, :inner] + dted[:, inner:] + skip_row * dmix[rows, :]
        du[rows, xo:] = gx.astype(BF16).astype(F32) * u[rows, xo:]
        if edge is None:
            edge = remote(du.at[pl.ds(0, 8)], du.at[pl.ds(tok, 8)], cx(nc - 1))
        d = dy[rows, :].astype(F32)
        ac = jnp.concatenate([d, d], axis=1) * yfr[rows, :] - w * dwl - qb
        xd = jnp.concatenate([x, x], axis=1) * dwt
        dcc[rows, :] = near_right(ac, spread)
        ddt[rows, :] = near_right(xd, spread)
        pump(PUMP[2][i])
    last_heads = exact_right(jnp.broadcast_to(last_row, (8, 2 * inner)), spread, mm_nt)[0:1, :]
    place = iota((tok, 1), 0)
    at_end = ((place == tok - 1) & is_fwd) | ((place == 0) & jnp.logical_not(is_fwd))
    dc_all = dcc[...] + jnp.where(at_end, last_heads, 0.0)
    dsums = exact_left(tri, dc_all)
    dld = jnp.where(is_fwd, dsums[tok - 1 : tok, :] - dsums + dc_all, dsums)
    gdt = (ddt[...] + dld * rate_row) * jax.nn.sigmoid(dtr[...])
    gall[:, xo : off[1]] = gdt.astype(BF16)
    misc = slice(conv_w, conv_w + 128)
    sm[...] = jnp.zeros(sm.shape, F32)
    sm[0, 5:6, :inner] = acc_gain
    sm[0, 3:4, misc] = exact_right(
        jnp.broadcast_to(acc_skip, (8, inner)), spread[:, :inner], mm_nt
    )[0:1, :]
    sm[0, 1:2, misc] = jnp.sum(gdt, axis=0, keepdims=True)
    sm[0, 2:3, misc] = jnp.sum(dld * ld[...], axis=0, keepdims=True)

    onward1 = pass_grads(1, grads1)

    taps_of = jnp.concatenate([conv_bc[...], conv_x[...]], axis=1)
    conv_acc = [jnp.zeros((1, conv_w), F32) for _ in range(taps)]
    for i in range(nb):
        lo, hi = i * TB, (i + 1) * TB
        if i == nb - 1:
            edge.wait_recv()
        here = seg_col(lo, TB)
        x_rows = xp[16 + lo : 16 + hi, :]
        acc = jnp.zeros((TB, conv_w), F32)
        for d in range(taps):
            m = du[lo + d : hi + d, :]
            if d > 0:
                m = m * (seg_col(lo, TB, d) == here).astype(F32)
            acc = acc + m * taps_of[taps - 1 - d : taps - d, :]
            conv_acc[taps - 1 - d] = conv_acc[taps - 1 - d] + jnp.sum(m * x_rows, axis=0, keepdims=True)
        gall[lo:hi, :xo] = acc[:, :xo].astype(BF16)
        gall[lo:hi, off[1] : off[2]] = acc[:, xo:].astype(BF16)
        pump(PUMP[4][i])
    for k in range(taps):
        sm[0, 1 + k : 2 + k, :conv_w] = conv_acc[k]

    w_all = weights(0, gall_w)
    acc_norm = jnp.zeros((1, width), F32)
    for i in range(nb):
        rows = slice(i * TB, (i + 1) * TB)
        part = mm_nt(gall[rows, :], w_all)
        hb[rows, :] = part.astype(BF16)
        line_h.begin(range(i * TB // PR, (i + 1) * TB // PR))
        h = hid[rows, :].astype(F32)
        rr = lax.rsqrt(jnp.mean(h * h, axis=1, keepdims=True) + EPS)
        acc_norm = acc_norm + jnp.sum(part * (h * rr), axis=0, keepdims=True)
        pump(PUMP[5][i])
    sm[0, 0:1, :] = acc_norm

    def small_send(level, slot, sends):
        return [remote(sm.at[level], smbuf.at[slot + k], dev) for k, dev in enumerate(sends)]

    def small_sum(level, slot, copies):
        acc = sm[level]
        for k, copy in enumerate(copies):
            copy.wait_recv()
            acc = acc + smbuf[slot + k]
        return acc

    sm0 = small_send(0, 0, [cx(k) for k in range(1, nc)])

    for b in range(width // block):
        cols = slice(b * block, (b + 1) * block)
        got = mm_tn(nl[16:, cols], gall[:, : off[2]])
        store_grads(b, 0, off[2], got)
    grads0 = send_grads(0)
    pump(PUMP[6][0])
    sm[1] = small_sum(0, 0, sm0)
    sm1 = small_send(1, nc - 1, [fs(k) for k in range(1, nf)])
    pump(PUMP[6][1])
    onward0 = pass_grads(0, grads0)
    pump(PUMP[6][2])
    sm[2] = small_sum(1, nc - 1, sm1)
    parts = [sm[2, 0:1, k * 128 : (k + 1) * 128] for k in range(width // 128)]
    parts = parts + [sm[2, 1 : 1 + taps, :xo], jnp.zeros((16 - taps - width // 128, 128), F32)]
    tps[...] = jnp.concatenate(parts, axis=0)
    tp_copies = [remote(tps, tpbuf.at[k - 1], tx(k)) for k in range(1, nt)]
    pump(PUMP[6][3])
    got = finish_grads(1, onward1)
    gwz[...] = got[:, :inner]
    gwo[...] = got[:, inner:]
    keep(gwz, gwz_h)
    keep(gwo, gwo_h)
    pump(PUMP[6][4])
    got = finish_grads(0, onward0)
    gwx[...] = got[:, off[1] :]
    gwdt[...] = got[:, xo : off[1]]
    keep(gwx, gwx_h)
    keep(gwdt, gwdt_h)
    bcs[...] = got[:, :xo].astype(BF16)
    bc_copies = [remote(bcs, bcbuf.at[k - 1], tx(k)) for k in range(1, nt)]
    pump(PUMP[6][5])
    for copy in tp_copies:
        copy.wait_recv()
    got = tp_order(tps[...], tpbuf)
    small[...] = sm[2]
    for k in range(width // 128):
        small[0:1, k * 128 : (k + 1) * 128] = got[k : k + 1, :]
    small[1 : 1 + taps, :xo] = got[width // 128 : width // 128 + taps, :]
    keep(small, small_h)
    pump(PUMP[6][6])
    for copy in bc_copies:
        copy.wait_recv()
    gwbc[...] = tp_order(bcs[...].astype(F32), bcbuf)
    keep(gwbc, gwbc_h)
    pump(len(todo))

    @pl.when(is_end)
    def _():
        for line in (line_o, line_h):
            for p in range(pieces):
                line.last(p)

    line_o.close()
    line_h.close()
    for p in range(pieces):
        rows = pl.ds(p * PR, PR)
        result(result_ids + p, out_v, out_h, rows).wait()
        result(result_ids + pieces + p, gh_v, gh_h, rows).wait()
    for copy in local_copies:
        copy.wait()
    for copy in pending:
        copy.wait_send()


def finish_kernel(dims, gdt_h, small_h, gh_h, out_h, gx_h, gz_h, gbc_h, go_h,
                  gh, out, o_x, o_z, o_bc, o_out, o_norm, o_dt, o_cx, o_cbc, o_bias, o_rate, o_skip, o_gain,
                  gh_s, out_s, x_s, z_s, bc_s, go_s, norm_s, dt_s, cx_s, cbc_s, bias_s, rate_s, skip_s, gain_s,
                  gdt, small, sems):
    hl, xo = dims
    count = [0]

    def move(src, dst):
        copy = pltpu.make_async_copy(src, dst, sems.at[count[0]])
        count[0] += 1
        copy.start()
        return copy

    first = [move(small_h, small), move(gdt_h, gdt)]
    moves = []
    for src, stage, dst, cuts in (
        (gh_h, gh_s, gh, 4), (out_h, out_s, out, 2), (gx_h, x_s, o_x, 1), (gz_h, z_s, o_z, 1),
        (go_h, go_s, o_out, 1), (gbc_h, bc_s, o_bc, 1),
    ):
        step = src.shape[0] // cuts
        for k in range(cuts):
            rows = pl.ds(k * step, step)
            moves.append((move(src.at[rows], stage.at[rows]), stage.at[rows], dst.at[rows]))
    rows_w, inner = gx_h.shape
    width = small.shape[1]
    conv_w = xo + inner
    for copy in first:
        copy.wait()
    norm_s[...] = small[0:1, :].reshape(width)
    flat = jnp.concatenate([gdt[...], jnp.zeros((128 - rows_w, 128), F32)], axis=0).T
    for k in range(hl):
        for d in range(2):
            dt_s[k, d : d + 1, :] = flat[d * hl + k : d * hl + k + 1, :rows_w]
    taps = cx_s.shape[0]
    cx_s[...] = small[1 : 1 + taps, xo:conv_w]
    cbc_s[...] = small[1 : 1 + taps, :xo]
    for row, ref in ((1, bias_s), (2, rate_s)):
        for d in range(2):
            ref[d : d + 1, :] = small[row : row + 1, conv_w + d * hl : conv_w + (d + 1) * hl]
    skip_s[...] = small[3:4, conv_w : conv_w + hl].reshape(hl)
    gain_s[...] = small[5:6, :inner].reshape(inner)
    leaving = [
        move(src, dst)
        for src, dst in (
            (norm_s, o_norm), (dt_s, o_dt), (cx_s, o_cx), (cbc_s, o_cbc), (bias_s, o_bias),
            (rate_s, o_rate), (skip_s, o_skip), (gain_s, o_gain),
        )
    ]
    for into, stage, dst in moves:
        into.wait()
        leaving.append(move(stage, dst))
    for copy in leaving:
        copy.wait()


def per_device(dims, hidden, seq_lengths, norm_gain, weight_x, weight_z, weight_bc, weight_dt,
               conv_x, conv_bc, dt_bias, log_rate, skip_scale, gate_gain, weight_out, cotangent):
    nf, nc, nt = dims
    tok, width = hidden.shape
    rows_w, inner = weight_x.shape
    hl = skip_scale.shape[0]
    shards = nf * nc
    xo = weight_bc.shape[1]
    state_n = xo // 2
    taps = conv_x.shape[0]
    conv_w = xo + inner
    p2 = xo + 128 + inner
    cw = p2 + 2 * inner
    pieces = tok // PR
    n_small = nf + nc - 2
    scratch = {
        "hid": ((tok, width), BF16),
        "cot": ((tok, width), BF16),
        "oag": ((tok, width), BF16),
        "hag": ((tok, width), BF16),
        "out_v": ((tok, width), BF16),
        "gh_v": ((tok, width), F32),
        "gwx": ((rows_w, inner), F32),
        "gwz": ((rows_w, inner), F32),
        "gwbc": ((rows_w, xo), F32),
        "gwdt": ((rows_w, 128), F32),
        "gwo": ((rows_w, inner), F32),
        "small": ((8, width), F32),
        "hbuf": ((16, width), BF16),
        "nl": ((tok + 16, width), BF16),
        "wbuf": ((shards, rows_w, cw), BF16),
        "xp": ((tok + 16, conv_w), F32),
        "dtr": ((tok, 128), F32),
        "u": ((tok, conv_w), F32),
        "low": ((tok, conv_w), BF16),
        "z": ((tok, inner), F32),
        "zd": ((tok, inner), F32),
        "ggate": ((tok, inner), BF16),
        "ld": ((tok, 128), F32),
        "cc": ((tok, 128), F32),
        "cct": ((128, tok), F32),
        "dte": ((tok, 2 * inner), BF16),
        "rea": ((tok, 2 * inner), BF16),
        "tol": ((tok, 2 * inner), BF16),
        "w16": ((tok, 2 * inner), BF16),
        "q16": ((tok, 2 * inner), BF16),
        "gm": ((tok, tok), F32),
        "gmt": ((tok, tok), F32),
        "pexp": ((hl, tok, tok), BF16),
        "yfr": ((tok, 2 * inner), F32),
        "s16": ((state_n, 2 * inner), BF16),
        "sbuf": ((nc - 1, state_n, inner), BF16),
        "dec": ((1, 128), F32),
        "decbuf": ((nc - 1, 1, 128), F32),
        "into16": ((state_n, 2 * inner), BF16),
        "gated": ((tok, inner), F32),
        "mixed": ((tok, inner), F32),
        "dmix": ((tok, inner), F32),
        "dy": ((tok, inner), BF16),
        "st": ((2, tok), F32),
        "stbuf": ((nt - 1, 2, tok), F32),
        "gall": ((tok, p2 + inner), BF16),
        "glow": ((tok, inner), BF16),
        "r_cols": ((tok, 128), F32),
        "ob": ((tok, width), BF16),
        "oin": ((pieces, PR, width), BF16),
        "oex": ((pieces, PR, width), BF16),
        "hb": ((tok, width), BF16),
        "hin": ((pieces, PR, width), BF16),
        "hex": ((pieces, PR, width), BF16),
        "rdy": ((tok, 2 * inner), BF16),
        "d16": ((state_n, 2 * inner), BF16),
        "dbuf": ((nc - 1, state_n, inner), BF16),
        "back16": ((state_n, 2 * inner), BF16),
        "dg": ((tok, tok), BF16),
        "dw": ((tok, 2 * inner), F32),
        "dcc": ((tok, 128), F32),
        "ddt": ((tok, 128), F32),
        "du": ((tok + 8, conv_w), F32),
        "gw16": ((shards, rows_w, cw), BF16),
        "fbuf": ((nf - 1, nc, rows_w, cw), BF16),
        "hsend": ((nc, rows_w, cw), BF16),
        "cbuf": ((nc - 1, rows_w, cw), BF16),
        "bcs": ((rows_w, xo), BF16),
        "bcbuf": ((nt - 1, rows_w, xo), BF16),
        "sm": ((3, 8, width), F32),
        "smbuf": ((n_small, 8, width), F32),
        "tps": ((16, 128), F32),
        "tpbuf": ((nt - 1, 16, 128), F32),
    }
    n_sems = 2 + 4 * (nc + nf - 2 + (nc - 1) * (nf - 1)) + 3 * (nc - 1) + 3 * (nt - 1)
    n_sems += 2 * (nf - 1 + nc - 1) + n_small + 6 * pieces + nt - 1
    vmem = pl.BlockSpec(memory_space=pltpu.VMEM)
    smem = pl.BlockSpec(memory_space=pltpu.SMEM)
    f32 = lambda *shape: jax.ShapeDtypeStruct(shape, F32)
    bf16 = lambda *shape: jax.ShapeDtypeStruct(shape, BF16)
    anywhere = pl.BlockSpec(memory_space=pl.ANY)
    results = pl.pallas_call(
        partial(mixer_kernel, (nf, nc, nt, hl)),
        out_shape=(
            bf16(tok, width), f32(tok, width), f32(rows_w, inner), f32(rows_w, inner),
            f32(rows_w, xo), f32(rows_w, 128), f32(rows_w, inner), f32(8, width),
        ),
        in_specs=[smem] + [vmem] * 4 + [smem] * 3 + [vmem] + [anywhere] * 6,
        out_specs=[anywhere] * 8,
        scratch_shapes=[pltpu.VMEM(s, d) for s, d in scratch.values()]
        + [pltpu.SemaphoreType.DMA((n_sems,)), pltpu.SemaphoreType.DMA((n_sems,))]
        + [pltpu.SemaphoreType.DMA((12 + 2 * pieces,))],
        compiler_params=pltpu.CompilerParams(
            collective_id=0, has_side_effects=True, vmem_limit_bytes=62 << 20
        ),
    )(
        seq_lengths, norm_gain, jnp.transpose(weight_dt, (2, 1, 0)), conv_x, conv_bc, dt_bias, log_rate,
        skip_scale, gate_gain, hidden, cotangent, weight_x, weight_z, weight_bc, weight_out.T,
    )
    out, gh, gx, gz, gbc, gdt, go, small = results
    finals = (
        f32(tok, width), bf16(tok, width), f32(rows_w, inner), f32(rows_w, inner), f32(rows_w, xo),
        f32(rows_w, inner), f32(width), f32(hl, 2, rows_w), f32(taps, inner), f32(taps, xo),
        f32(2, hl), f32(2, hl), f32(hl), f32(inner),
    )
    gh, out, gx, gz, gbc, go, norm, gdt, cx, cbc, bias, rate, skip, gate = pl.pallas_call(
        partial(finish_kernel, (hl, xo)),
        out_shape=finals,
        in_specs=[anywhere] * 8,
        out_specs=[anywhere] * 14,
        scratch_shapes=[pltpu.VMEM(a.shape, a.dtype) for a in finals]
        + [pltpu.VMEM((rows_w, 128), F32), pltpu.VMEM((8, width), F32), pltpu.SemaphoreType.DMA((32,))],
        compiler_params=pltpu.CompilerParams(vmem_limit_bytes=62 << 20),
    )(gdt, small, gh, out, gx, gz, gbc, go)
    return (
        out, gh, norm, gx, gz, gbc, jnp.transpose(gdt, (2, 1, 0)), cx, cbc, bias, rate, skip, gate, go.T
    )


def solution(mesh):
    dims = tuple(mesh.shape[a] for a in ("fsdp", "ctx", "tp"))
    both = ("fsdp", "ctx")
    return jax.shard_map(
        partial(per_device, dims),
        mesh=mesh,
        in_specs=(
            P(both, None), P("fsdp", None), P(), P(both, "tp"), P(both, "tp"), P(both, None),
            P(both, None, "tp"), P(None, "tp"), P(), P(None, "tp"), P(None, "tp"), P("tp"),
            P("tp"), P("tp", both), P(both, None),
        ),
        out_specs=(
            P(both, None), P(both, None), P(), P(both, "tp"), P(both, "tp"), P(both, None),
            P(both, None, "tp"), P(None, "tp"), P(), P(None, "tp"), P(None, "tp"), P("tp"),
            P("tp"), P("tp", both),
        ),
        check_vma=False,
    )
```
